128 devices in a mesh: gx: 8 (over x_lo, y), gy: 16 (over z, x_hi, core).
Axes of the slice: x: 4 (x_hi: 2, x_lo: 2; x = x_hi * 2 + x_lo), y: 4, z: 4, core: 2. Of those that a mesh axis runs over, the one named last changes fastest.
Arguments:
- features: bfloat16 [256, 512, 128], P(('gx', 'gy')), may hold values from -11 to 11
- brick_pos: int32 [256], P(('gx', 'gy')), may hold values from 0 to 4, as said below
- cotangent: bfloat16 [256, 512, 128], P(('gx', 'gy')), may hold values from -40 to 40
- first_kernel: bfloat16 [27, 128, 128], replicated, may hold values from -0.109375 to 0.109375
- second_kernel: bfloat16 [27, 128, 128], replicated, may hold values from -0.109375 to 0.109375
- norm_gain: float32 [128], replicated, may hold values from 0.1 to 1.9
Outputs:
- block_out: bfloat16 [256, 512, 128], P(('gx', 'gy'))
- feature_grad: bfloat16 [256, 512, 128], P(('gx', 'gy'))
- kernel_update: float32 [2, 27, 128, 128], replicated
- gain_update: float32 [128], replicated
The draws below stay inside these ranges and needn't reach their ends.
Inputs may be any that keep to these rules, and one draw needn't show every extreme that they name: `brick_pos`: on each device block the first k slots (k between max(1, 0) and 2, and k = 2 on at least one block) hold distinct positions below 4; the remaining slots hold 4.
All inputs are finite; a program needn't handle non-finite values.
Results may differ from the reference program's by a relative error of at most 0.0029.
Values may be sent and summed in bfloat16 or wider, within the bound.
A program may use at most 128 MiB of HBM per device.

```python
import math
import jax
import jax.numpy as jnp
from jax import lax

CHANNEL_COUNT = 128
TAPS = 27
BX = 2
BY = 2
BZ = 1
BRICK_VOXELS = 512
POS = 4
BLOCK_SLOTS = 2
TOTAL_SLOTS = 256
N_GX = 8
N_GY = 16


def draw_brick_pos(key, part):
    device_blocks = TOTAL_SLOTS // BLOCK_SLOTS
    key_orders = jax.random.fold_in(key, 11)
    key_counts = jax.random.fold_in(key, 12)
    key_chosen = jax.random.fold_in(key, 13)
    order_keys = jax.random.split(key_orders, device_blocks)
    orders = jax.vmap(lambda single: jax.random.permutation(single, POS))(order_keys)[:, :BLOCK_SLOTS]
    fewest = max(1, BLOCK_SLOTS // 4)
    counts = jax.random.randint(key_counts, (device_blocks,), fewest, BLOCK_SLOTS + 1)
    chosen = jax.random.randint(key_chosen, (), 0, device_blocks)
    counts = jnp.where(jnp.arange(device_blocks) == chosen, BLOCK_SLOTS, counts)
    slot_index = jnp.arange(BLOCK_SLOTS)[None, :]
    placed = jnp.where(slot_index < counts[:, None], orders, POS)
    return placed.reshape(-1).astype(jnp.int32)


def draw_features(key, part):
    key_channel = jax.random.fold_in(key, 21)
    noise_key = jax.random.fold_in(key, 22)
    channel = jnp.exp(jax.random.uniform(key_channel, (CHANNEL_COUNT,), minval=math.log(0.3), maxval=math.log(3.0)))
    random_noise = jnp.clip(jax.random.normal(noise_key, (TOTAL_SLOTS, BRICK_VOXELS, CHANNEL_COUNT)), -3.5, 3.5)
    return (random_noise * channel).astype(jnp.bfloat16)


def draw_cotangent(key, part):
    device_blocks = TOTAL_SLOTS // BLOCK_SLOTS
    key_channel = jax.random.fold_in(key, 31)
    noise_key = jax.random.fold_in(key, 32)
    key_block = jax.random.fold_in(key, 33)
    channel = jnp.exp(jax.random.uniform(key_channel, (CHANNEL_COUNT,), minval=math.log(0.3), maxval=math.log(3.0)))
    ramp = jnp.arange(device_blocks, dtype=jnp.float32) / max(device_blocks - 1, 1) - 0.5
    jitter = jax.random.uniform(key_block, (device_blocks,), minval=0.8, maxval=1.25)
    factor = jnp.exp(ramp * math.log(3.0)) * jitter
    random_noise = jnp.clip(jax.random.normal(noise_key, (TOTAL_SLOTS, BRICK_VOXELS, CHANNEL_COUNT)), -3.5, 3.5)
    rows = jnp.repeat(factor, BLOCK_SLOTS)
    return (random_noise * channel[None, None, :] * rows[:, None, None]).astype(jnp.bfloat16)


def centred(key, shape, deviation, limit, kind=jnp.bfloat16):
    return jnp.clip(deviation * jax.random.normal(key, shape, jnp.float32), -limit, limit).astype(kind)


def setup_inputs(seed: int = 0) -> dict:
    splits = jax.random.split(jax.random.key(seed), 7)
    features = draw_features(jax.random.fold_in(splits[6], 71), 0)
    brick_pos = draw_brick_pos(jax.random.fold_in(splits[6], 71), 0)
    cotangent = draw_cotangent(jax.random.fold_in(splits[6], 71), 0)
    first_kernel = centred(splits[3], (TAPS, CHANNEL_COUNT, CHANNEL_COUNT), (TAPS * CHANNEL_COUNT) ** -0.5, 0.109375)
    second_kernel = centred(splits[4], (TAPS, CHANNEL_COUNT, CHANNEL_COUNT), (TAPS * CHANNEL_COUNT) ** -0.5, 0.109375)
    norm_gain = jnp.clip(1.0 + 0.18 * jax.random.normal(splits[5], (CHANNEL_COUNT,), jnp.float32), 0.1, 1.9)
    return {"features": features, "brick_pos": brick_pos, "cotangent": cotangent, "first_kernel": first_kernel, "second_kernel": second_kernel, "norm_gain": norm_gain}


clip_level = 0.5

def brick_coords(position):
    brick_x = position // (BY * BZ)
    brick_y = position // BZ % BY
    brick_z = position % BZ
    return (brick_x, brick_y, brick_z)

def activate(pre, norm_gain):
    average = lax.optimization_barrier(jnp.mean(pre, axis=-1, keepdims=True))
    center = pre - average
    spread = lax.optimization_barrier(jnp.mean(center * center, axis=-1, keepdims=True))
    normed = center * lax.rsqrt(spread + 1e-05) * norm_gain
    return normed * jax.nn.sigmoid(normed)

def apply_taps(tile_set, kernel, flipped):
    slot_count, channels = (tile_set.shape[0], tile_set.shape[-1])
    summed = jnp.zeros((slot_count * 512, channels), jnp.float32)
    for step_x in range(3):
        for step_y in range(3):
            for step_z in range(3):
                tap_index = (step_x * 3 + step_y) * 3 + step_z
                if flipped:
                    start_x, start_y, start_z = (2 - step_x, 2 - step_y, 2 - step_z)
                else:
                    start_x, start_y, start_z = (step_x, step_y, step_z)
                window = tile_set[:, start_x:start_x + 8, start_y:start_y + 8, start_z:start_z + 8, :]
                window = window.reshape(slot_count * 512, channels)
                if flipped:
                    summed = summed + lax.dot_general(window, kernel[tap_index], (((1,), (1,)), ((), ())), preferred_element_type=jnp.float32)
                else:
                    summed = summed + jnp.dot(window, kernel[tap_index], preferred_element_type=jnp.float32)
    return summed.reshape(slot_count, 512, channels)

def tap_grads(tile_set, upstream):
    slot_count, channels = (tile_set.shape[0], tile_set.shape[-1])
    flat_rows = upstream.reshape(slot_count * 512, channels)
    result = []
    for step_x in range(3):
        for step_y in range(3):
            for step_z in range(3):
                window = tile_set[:, step_x:step_x + 8, step_y:step_y + 8, step_z:step_z + 8, :]
                window = window.reshape(slot_count * 512, channels)
                result.append(lax.dot_general(window, flat_rows, (((0,), (0,)), ((), ())), preferred_element_type=jnp.float32))
    return jnp.stack(result)

def to_grid(values, put_x, put_y, put_z, bricks_x, bricks_y):
    slot_count, channels = (values.shape[0], values.shape[-1])
    bricks = jnp.zeros((bricks_x, bricks_y, BZ, 8, 8, 8, channels), values.dtype)
    bricks = bricks.at[put_x, put_y, put_z].set(values.reshape(slot_count, 8, 8, 8, channels), mode='drop')
    return bricks.transpose(0, 3, 1, 4, 2, 5, 6).reshape(bricks_x * 8, bricks_y * 8, BZ * 8, channels)

def cut_tiles(padded, brick_x, brick_y, brick_z):
    channels = padded.shape[-1]

    def take_tile(start_x, start_y, start_z):
        return lax.dynamic_slice(padded, (start_x * 8, start_y * 8, start_z * 8, start_x * 0), (10, 10, 10, channels))
    return jax.vmap(take_tile)(brick_x, brick_y, brick_z)

def reference(features, brick_pos, cotangent, first_kernel, second_kernel, norm_gain):
    bricks_x = BX * N_GX
    bricks_y = BY * N_GY
    slot_index = jnp.arange(TOTAL_SLOTS, dtype=jnp.int32)
    device = slot_index // BLOCK_SLOTS
    is_live = brick_pos < POS
    brick_x, brick_y, brick_z = brick_coords(jnp.minimum(brick_pos, POS - 1).astype(jnp.int32))
    whole_x = (device // N_GY * BX + brick_x).astype(jnp.int32)
    whole_y = (device % N_GY * BY + brick_y).astype(jnp.int32)
    brick_z = brick_z.astype(jnp.int32)
    put_x = jnp.where(is_live, whole_x, bricks_x).astype(jnp.int32)
    live_mask = is_live[:, None, None]
    given_rows = jnp.where(live_mask, features, jnp.zeros_like(features))
    upstream = jnp.where(live_mask, cotangent, jnp.zeros_like(cotangent))

    def tiles_for(values):
        dense_grid = to_grid(values, put_x, whole_y, brick_z, bricks_x, bricks_y)
        padded = jnp.pad(dense_grid, ((1, 1), (1, 1), (1, 1), (0, 0)))
        return cut_tiles(padded, whole_x, whole_y, brick_z)
    given_tiles = tiles_for(given_rows)
    first_pre = jnp.where(live_mask, apply_taps(given_tiles, first_kernel, False), 0.0)
    hidden_full, pullback = jax.vjp(activate, first_pre, norm_gain)
    hidden = jnp.where(live_mask, hidden_full, 0.0).astype(jnp.bfloat16)
    hidden_tiles = tiles_for(hidden)
    second_pre = jnp.where(live_mask, apply_taps(hidden_tiles, second_kernel, False), 0.0)
    block_out = (given_rows.astype(jnp.float32) + second_pre).astype(jnp.bfloat16)
    second_grad = tap_grads(hidden_tiles, upstream)
    hidden_grad = jnp.where(live_mask, apply_taps(tiles_for(upstream), second_kernel, True), 0.0)
    pre_full, gain_grad = pullback(hidden_grad)
    pre_grad = jnp.where(live_mask, pre_full, 0.0).astype(jnp.bfloat16)
    first_grad = tap_grads(given_tiles, pre_grad)
    back_conv = apply_taps(tiles_for(pre_grad), first_kernel, True)
    feature_grad = jnp.where(live_mask, upstream.astype(jnp.float32) + back_conv, 0.0).astype(jnp.bfloat16)
    stacked = jnp.stack([first_grad, second_grad])
    squares = jnp.sum(stacked * stacked) + jnp.sum(gain_grad * gain_grad)
    entries = 54.0 * CHANNEL_COUNT * CHANNEL_COUNT + CHANNEL_COUNT
    shrink = jnp.minimum(1.0, clip_level / jnp.sqrt(squares / entries + 1e-06))
    return (block_out, feature_grad, shrink * stacked, shrink * gain_grad)
```

```python
import jax
import jax.numpy as jnp
from jax import lax
from jax.experimental import pallas as pl
from jax.experimental.pallas import tpu as pltpu
from jax.sharding import PartitionSpec as P

MESH = pl.DeviceIdType.MESH
F32 = jnp.float32
BF16 = jnp.bfloat16
CLIP = 0.5
C = 128
POS = 4
DIRS = [(dx, dy) for dx in (-1, 0, 1) for dy in (-1, 0, 1) if (dx, dy) != (0, 0)]
ORDERS = [(0, 1, 2), (1, 2, 0), (2, 0, 1)]
NT = (((1,), (1,)), ((), ()))


def span(d, size, halo):
    if d == 0:
        return pl.ds(1, 16)
    if d < 0:
        return pl.ds(0 if halo else 1, 1)
    return pl.ds(17 if halo else 16, 1)


def step_kernel(
    pos_ref, gain_ref, feat_hbm, cot_hbm, k1_hbm, k2_hbm,
    out_hbm, fgrad_hbm, full_ref, stats_ref,
    feat, cot, w1, w2, r1, r2, grid1, grid2, ag, au, ah, ap,
    hid, pgr, outv, part, rcore, sa, ra, sb, rb, rc, gains,
    in_sem, out_sem, hs, hr, cs, cr, as_, ar, bs, br, zs, zr, ebs, ebr, eas, ear, ecs, ecr, gs, gr,
):
    gx = lax.axis_index("gx")
    gy = lax.axis_index("gy")
    core = gy % 2
    coord = ((gy // 2) % 2 * 2 + gx // 4, gx % 4, gy // 4)

    def peer(axis, value):
        x, y, z = (value if i == axis else coord[i] for i in range(3))
        return (x % 2 * 4 + y, z * 4 + x // 2 * 2 + core)

    sibling = (gx, gy + 1 - 2 * core)

    def there(d):
        x, y = gx + d[0], gy + d[1]
        return (x >= 0) & (x < 8) & (y >= 0) & (y < 16)

    def load(i, src, dst):
        return pltpu.make_async_copy(src, dst, in_sem.at[i])

    loads = [load(0, feat_hbm, feat), load(1, cot_hbm, cot), load(2, k1_hbm, w1), load(3, k2_hbm, w2)]
    for c in loads:
        c.start()

    for g in (grid1, grid2):
        for f in range(2):
            for e in (0, 17):
                g[f, e] = jnp.zeros((18, 8, C), BF16)
                for x in range(1, 17):
                    g[f, x, e] = jnp.zeros((8, C), BF16)

    barrier = pltpu.get_barrier_semaphore()
    for d in DIRS:
        @pl.when(there(d))
        def _():
            pl.semaphore_signal(barrier, inc=1, device_id=(gx + d[0], gy + d[1]), device_id_type=MESH)
    for axis in range(3):
        for k in (1, 2, 3):
            pl.semaphore_signal(barrier, inc=1, device_id=peer(axis, (coord[axis] + k) % 4), device_id_type=MESH)
    pl.semaphore_signal(barrier, inc=1, device_id=sibling, device_id_type=MESH)

    p0, p1 = pos_ref[0], pos_ref[1]
    where = [jnp.minimum(p0, POS - 1), jnp.minimum(p1, POS - 1)]
    bx = [w // 2 for w in where]
    by = [w % 2 for w in where]
    live = [(p0 < POS).astype(F32), (p1 < POS).astype(F32)]

    def place(grid, f, source):
        for p in range(POS):
            m0, m1 = (p0 == p).astype(F32), (p1 == p).astype(F32)
            for x in range(8):
                rows = pl.ds(x * 64, 64)
                v = source[0, rows].astype(F32) * m0 + source[1, rows].astype(F32) * m1
                grid[f, 1 + p // 2 * 8 + x, pl.ds(1 + p % 2 * 8, 8)] = v.reshape(8, 8, C).astype(BF16)

    def halo(phase, grid):
        def copies(d):
            i = DIRS.index(d)
            return pltpu.make_async_remote_copy(
                src_ref=grid.at[:, span(d[0], 16, False), span(d[1], 16, False)],
                dst_ref=grid.at[:, span(-d[0], 16, True), span(-d[1], 16, True)],
                send_sem=hs.at[phase, i], recv_sem=hr.at[phase, i],
                device_id=(gx + d[0], gy + d[1]), device_id_type=MESH,
            )

        def start():
            for d in DIRS:
                @pl.when(there(d))
                def _():
                    copies(d).start()

        def arrive():
            for d in DIRS:
                @pl.when(there((-d[0], -d[1])))
                def _():
                    copies(d).wait_recv()

        def done():
            for d in DIRS:
                @pl.when(there(d))
                def _():
                    copies(d).wait_send()

        return start, arrive, done

    start1, arrive1, done1 = halo(0, grid1)
    start2, arrive2, done2 = halo(1, grid2)

    loads[0].wait()
    loads[1].wait()
    place(grid1, 0, feat)
    place(grid1, 1, cot)

    expected = 10
    for d in DIRS:
        expected = expected + there(d).astype(jnp.int32)
    pl.semaphore_wait(barrier, expected)
    start1()

    loads[2].wait()
    loads[3].wait()
    for w, r in ((w2, r2), (w1, r1)):
        for t in range(27):
            r[t // 9, :, pl.ds(t % 9 * C, C)] = w[26 - t]

    z = lax.broadcasted_iota(jnp.int32, (10, 8, C), 1)
    first, last = z == 0, z == 7

    def gather(a, s, grid, f):
        def layer(x, carry):
            t = grid[f, bx[s] * 8 + x, pl.ds(by[s] * 8, 10)].astype(F32)
            down = jnp.where(first, 0.0, pltpu.roll(t, 1, 1))
            up = jnp.where(last, 0.0, pltpu.roll(t, 7, 1))
            for oz, v in enumerate((down, t, up)):
                for oy in range(3):
                    a[s, pl.ds(pl.multiple_of(x * 64, 64), 64), pl.ds((oy * 3 + oz) * C, C)] = (
                        v[oy : oy + 8].reshape(64, C).astype(BF16)
                    )
            return carry

        lax.fori_loop(0, 10, layer, 0)

    def conv(a, s, w):
        total = None
        for ox in range(3):
            v = jnp.dot(a[s, pl.ds(ox * 64, 512)], w[pl.ds(ox * 9, 9)].reshape(9 * C, C), preferred_element_type=F32)
            total = v if total is None else total + v
        return total

    def conv_t(a, s, r):
        total = None
        for ox in range(3):
            v = lax.dot_general(a[s, pl.ds(ox * 64, 512)], r[ox], NT, preferred_element_type=F32)
            total = v if total is None else total + v
        return total

    arrive1()
    gain = gain_ref[0:1, :]
    ggrad = jnp.zeros((1, C), F32)
    hid_t, pgr_t = [], []
    for s in range(2):
        gather(ag, s, grid1, 0)
        gather(au, s, grid1, 1)
        pre = conv(ag, s, w1)
        hgrad = conv_t(au, s, r2) * live[s]
        center = pre - jnp.mean(pre, axis=-1, keepdims=True)
        inv = lax.rsqrt(jnp.mean(center * center, axis=-1, keepdims=True) + 1e-05)
        unit = center * inv
        normed = unit * gain
        sig = jax.nn.sigmoid(normed)
        hidden = normed * sig * live[s]
        dn = hgrad * (sig * (1.0 + normed * (1.0 - sig)))
        ggrad = ggrad + jnp.sum(dn * unit, axis=0, keepdims=True)
        du = dn * gain
        dc = inv * (du - unit * jnp.mean(du * unit, axis=-1, keepdims=True))
        pg = (dc - jnp.mean(dc, axis=-1, keepdims=True)) * live[s]
        hid[s] = hidden.astype(BF16)
        pgr[s] = pg.astype(BF16)
        hid_t.append(hidden.T.astype(BF16))
        pgr_t.append(pg.T.astype(BF16))

    place(grid2, 0, hid)
    place(grid2, 1, pgr)
    start2()

    def gain_copy(stage, k):
        if stage == 0:
            return pltpu.make_async_remote_copy(
                src_ref=gains.at[0, 0], dst_ref=gains.at[0, 1], send_sem=gs.at[0], recv_sem=gr.at[0],
                device_id=sibling, device_id_type=MESH)
        axis = stage - 1
        i = 1 + axis * 3 + k - 1
        return pltpu.make_async_remote_copy(
            src_ref=gains.at[stage, coord[axis]], dst_ref=gains.at[stage, coord[axis]],
            send_sem=gs.at[i], recv_sem=gr.at[i],
            device_id=peer(axis, (coord[axis] + k) % 4), device_id_type=MESH)

    gains[0, 0] = jnp.broadcast_to(ggrad, (8, C))
    gain_copy(0, 0).start()

    half = pl.multiple_of(core * 64, 64)
    other = pl.multiple_of((1 - core) * 64, 64)

    def core_copy(g):
        return pltpu.make_async_remote_copy(
            src_ref=part.at[pl.ds(g * 9, 9), pl.ds(other, 64)], dst_ref=rcore.at[pl.ds(g * 9, 9)],
            send_sem=cs.at[g], recv_sem=cr.at[g], device_id=sibling, device_id_type=MESH)

    def group(g):
        if g < 3:
            a, lhs, ox = au, hid_t, 2 - g
        else:
            a, lhs, ox = ag, pgr_t, g - 3
        v = (jnp.dot(lhs[0], a[0, pl.ds(ox * 64, 512)], preferred_element_type=F32)
             + jnp.dot(lhs[1], a[1, pl.ds(ox * 64, 512)], preferred_element_type=F32))
        for k in range(9):
            if g < 3:
                part[g * 9 + 8 - k] = v[:, k * C : (k + 1) * C]
            else:
                part[g * 9 + k] = v[:, k * C : (k + 1) * C].T
        core_copy(g).start()

    def axes(i):
        return ORDERS[i]

    def piece(i):
        a, b, _ = axes(i)
        return coord[a], coord[b] // 2, coord[b] % 2

    def send_a(i, k):
        a = axes(i)[0]
        to = (coord[a] + k) % 4
        return pltpu.make_async_remote_copy(
            src_ref=sa.at[pl.ds(i * 18, 18), to], dst_ref=ra.at[i, k - 1],
            send_sem=as_.at[i * 3 + k - 1], recv_sem=ar.at[i * 3 + k - 1],
            device_id=peer(a, to), device_id_type=MESH)

    def send_b(i, k):
        b = axes(i)[1]
        to = (coord[b] + k) % 4
        return pltpu.make_async_remote_copy(
            src_ref=sb.at[i, pl.ds(to // 2 * 9, 9), to % 2], dst_ref=rb.at[i, k - 1],
            send_sem=bs.at[i * 3 + k - 1], recv_sem=br.at[i * 3 + k - 1],
            device_id=peer(b, to), device_id_type=MESH)

    def send_c(i, k):
        c = axes(i)[2]
        to = (coord[c] + k) % 4
        return pltpu.make_async_remote_copy(
            src_ref=rc.at[i, coord[c]], dst_ref=rc.at[i, coord[c]],
            send_sem=zs.at[i * 3 + k - 1], recv_sem=zr.at[i * 3 + k - 1],
            device_id=peer(c, to), device_id_type=MESH)

    def share_b(i, k):
        b = axes(i)[1]
        pa, hi, lo = piece(i)
        place_ = full_ref.at[pl.ds(i * 18 + hi * 9, 9), core * 8 + pa * 2 + lo]
        return pltpu.make_async_remote_copy(
            src_ref=place_, dst_ref=place_, send_sem=ebs.at[i * 3 + k - 1], recv_sem=ebr.at[i * 3 + k - 1],
            device_id=peer(b, (coord[b] + k) % 4), device_id_type=MESH)

    def share_a(i, k):
        a = axes(i)[0]
        place_ = full_ref.at[pl.ds(i * 18, 18), pl.ds(core * 8 + coord[a] * 2, 2)]
        return pltpu.make_async_remote_copy(
            src_ref=place_, dst_ref=place_, send_sem=eas.at[i * 3 + k - 1], recv_sem=ear.at[i * 3 + k - 1],
            device_id=peer(a, (coord[a] + k) % 4), device_id_type=MESH)

    def share_core(i):
        place_ = full_ref.at[pl.ds(i * 18, 18), pl.ds(core * 8, 8)]
        return pltpu.make_async_remote_copy(
            src_ref=place_, dst_ref=place_, send_sem=ecs.at[i], recv_sem=ecr.at[i],
            device_id=sibling, device_id_type=MESH)

    def reduce_core(i):
        for g in (2 * i, 2 * i + 1):
            core_copy(g).wait_recv()

        def tap(t, carry):
            v = part[t, pl.ds(half, 64)] + rcore[t]
            rcore[t] = v
            sa[t] = v.reshape(4, 16, C).astype(BF16)
            return carry

        lax.fori_loop(i * 18, i * 18 + 18, tap, 0)
        for k in (1, 2, 3):
            send_a(i, k).start()

    def reduce_a(i):
        for k in (1, 2, 3):
            send_a(i, k).wait_recv()
        mine = pl.multiple_of(coord[axes(i)[0]] * 16, 16)
        v = rcore[pl.ds(i * 18, 18), pl.ds(mine, 16)]
        for k in range(3):
            v = v + ra[i, k].astype(F32)
        sb[i] = v.reshape(18, 2, 8, C)
        for k in (1, 2, 3):
            send_b(i, k).start()

    def reduce_b(i):
        for k in (1, 2, 3):
            send_b(i, k).wait_recv()
        _, hi, lo = piece(i)
        v = sb[i, pl.ds(hi * 9, 9), lo]
        for k in range(3):
            v = v + rb[i, k]
        rc[i, coord[axes(i)[2]]] = v
        for k in (1, 2, 3):
            send_c(i, k).start()

    def reduce_c(i):
        for k in (1, 2, 3):
            send_c(i, k).wait_recv()
        pa, hi, lo = piece(i)
        v = ((rc[i, 0] + rc[i, 1]) + rc[i, 2]) + rc[i, 3]
        full_ref[pl.ds(i * 18 + hi * 9, 9), core * 8 + pa * 2 + lo] = v.astype(BF16)
        for k in (1, 2, 3):
            share_b(i, k).start()

    def spread_a(i):
        for k in (1, 2, 3):
            share_b(i, k).wait_recv()
        for k in (1, 2, 3):
            share_a(i, k).start()

    def spread_core(i):
        for k in (1, 2, 3):
            share_a(i, k).wait_recv()
        share_core(i).start()

    def gain_step(stage):
        if stage == 0:
            gain_copy(0, 0).wait_recv()
            gains[1, coord[0]] = gains[0, 0] + gains[0, 1]
        else:
            for k in (1, 2, 3):
                gain_copy(stage, k).wait_recv()
            v = ((gains[stage, 0] + gains[stage, 1]) + gains[stage, 2]) + gains[stage, 3]
            if stage == 3:
                return v
            gains[stage + 1, coord[stage]] = v
        for k in (1, 2, 3):
            gain_copy(stage + 1, k).start()

    def second_half(s, f):
        if f == 0:
            gather(ah, s, grid2, 0)
            v = conv(ah, s, w2) * live[s] + feat[s].astype(F32) * live[s]
        else:
            gather(ap, s, grid2, 1)
            v = (conv_t(ap, s, r1) + cot[s].astype(F32)) * live[s]
        outv[f, s] = v.astype(BF16)

    group(0)
    group(1)
    gain_step(0)
    group(2)
    group(3)
    reduce_core(0)
    group(4)
    group(5)
    reduce_core(1)
    gain_step(1)
    arrive2()
    reduce_core(2)
    second_half(0, 0)
    reduce_a(0)
    reduce_a(1)
    gain_step(2)
    second_half(1, 0)
    reduce_b(0)
    reduce_a(2)
    reduce_b(1)
    second_half(0, 1)
    reduce_c(0)
    reduce_b(2)
    reduce_c(1)
    second_half(1, 1)
    out_copies = [pltpu.make_async_copy(outv.at[0], out_hbm, out_sem.at[0]),
                  pltpu.make_async_copy(outv.at[1], fgrad_hbm, out_sem.at[1])]
    for c in out_copies:
        c.start()
    spread_a(0)
    reduce_c(2)
    spread_a(1)
    gain_sum = gain_step(3)
    spread_core(0)
    spread_a(2)
    spread_core(1)

    def squares(i, acc):
        share_core(i).wait_recv()

        def tap(t, acc):
            v = full_ref[t].astype(F32)
            return acc + jnp.sum(v * v, axis=0)

        return lax.fori_loop(i * 18, i * 18 + 18, tap, acc)

    acc = jnp.zeros((8, C), F32)
    acc = squares(0, acc)
    spread_core(2)
    acc = squares(1, acc)
    acc = squares(2, acc)
    total = jnp.sum(acc) + jnp.sum(gain_sum[0:1] * gain_sum[0:1])
    entries = 54.0 * C * C + C
    mean = jnp.full((8, C), total / entries + 1e-06, F32)
    shrink = jnp.minimum(1.0, CLIP / jnp.sqrt(mean))
    stats_ref[0] = shrink
    stats_ref[1] = shrink * gain_sum

    done1()
    done2()
    for c in out_copies:
        c.wait()
    for g in range(6):
        core_copy(g).wait_send()
    gain_copy(0, 0).wait_send()
    for k in (1, 2, 3):
        for stage in (1, 2, 3):
            gain_copy(stage, k).wait_send()
        for i in range(3):
            for send in (send_a, send_b, send_c, share_b, share_a):
                send(i, k).wait_send()
    for i in range(3):
        share_core(i).wait_send()


def finish_kernel(full_ref, stats_ref, out_ref):
    v = full_ref[...].astype(F32).reshape(9, 128, C)
    out_ref[...] = v * stats_ref[0, 0:1, :]


def per_device(features, brick_pos, cotangent, first_kernel, second_kernel, norm_gain):
    hbm = pl.BlockSpec(memory_space=pl.ANY)
    vmem = pl.BlockSpec(memory_space=pltpu.VMEM)
    dma = pltpu.SemaphoreType.DMA
    V = pltpu.VMEM
    tile = (2, 640, 9 * C)
    out, fgrad, full, stats = pl.pallas_call(
        step_kernel,
        out_shape=(
            jax.ShapeDtypeStruct((2, 512, C), BF16),
            jax.ShapeDtypeStruct((2, 512, C), BF16),
            jax.ShapeDtypeStruct((54, 16, 8, C), BF16),
            jax.ShapeDtypeStruct((2, 8, C), F32),
        ),
        in_specs=[pl.BlockSpec(memory_space=pltpu.SMEM), vmem, hbm, hbm, hbm, hbm],
        out_specs=(hbm, hbm, vmem, vmem),
        scratch_shapes=[
            V((2, 512, C), BF16), V((2, 512, C), BF16),
            V((27, C, C), BF16), V((27, C, C), BF16),
            V((3, C, 9 * C), BF16), V((3, C, 9 * C), BF16),
            V((2, 18, 18, 8, C), BF16), V((2, 18, 18, 8, C), BF16),
            V(tile, BF16), V(tile, BF16), V(tile, BF16), V(tile, BF16),
            V((2, 512, C), BF16), V((2, 512, C), BF16), V((2, 2, 512, C), BF16),
            V((54, C, C), F32), V((54, 64, C), F32),
            V((54, 4, 16, C), BF16), V((3, 3, 18, 16, C), BF16),
            V((3, 18, 2, 8, C), F32), V((3, 3, 9, 8, C), F32), V((3, 4, 9, 8, C), F32),
            V((4, 4, 8, C), F32),
            dma((4,)), dma((2,)), dma((2, 8)), dma((2, 8)), dma((6,)), dma((6,)),
            dma((9,)), dma((9,)), dma((9,)), dma((9,)), dma((9,)), dma((9,)),
            dma((9,)), dma((9,)), dma((9,)), dma((9,)), dma((3,)), dma((3,)), dma((10,)), dma((10,)),
        ],
        compiler_params=pltpu.CompilerParams(
            collective_id=0, has_side_effects=True, vmem_limit_bytes=56 * 2**20
        ),
        name="step",
    )(brick_pos, norm_gain.reshape(1, C), features, cotangent, first_kernel, second_kernel)
    update = pl.pallas_call(
        finish_kernel,
        grid=(6,),
        out_shape=jax.ShapeDtypeStruct((54, C, C), F32),
        in_specs=[
            pl.BlockSpec((9, 16, 8, C), lambda i: ((i + 3) % 6, 0, 0, 0)),
            pl.BlockSpec((2, 8, C), lambda i: (0, 0, 0)),
        ],
        out_specs=pl.BlockSpec((9, C, C), lambda i: (i, 0, 0)),
        compiler_params=pltpu.CompilerParams(vmem_limit_bytes=8 * 2**20),
        name="finish",
    )(full, stats)
    return out, fgrad, update.reshape(2, 27, C, C), stats[1, 0]


def solution(mesh):
    rows = P(("gx", "gy"), None, None)
    return jax.shard_map(
        per_device, mesh=mesh, in_specs=(rows, P(("gx", "gy")), rows, P(), P(), P()),
        out_specs=(rows, rows, P(), P()), check_vma=False,
    )
```

```python
import jax
import jax.numpy as jnp
from jax import lax
from jax.experimental import pallas as pl
from jax.experimental.pallas import tpu as pltpu
from jax.sharding import PartitionSpec as P

MESH = pl.DeviceIdType.MESH
F32 = jnp.float32
BF16 = jnp.bfloat16
CLIP = 0.5
C = 128
POS = 4
DIRS = [(dx, dy) for dx in (-1, 0, 1) for dy in (-1, 0, 1) if (dx, dy) != (0, 0)]
ORDERS = [(0, 1, 2), (1, 2, 0), (2, 0, 1)]
NT = (((1,), (1,)), ((), ()))


def span(d, size, halo):
    if d == 0:
        return pl.ds(1, 16)
    if d < 0:
        return pl.ds(0 if halo else 1, 1)
    return pl.ds(17 if halo else 16, 1)


def step_kernel(
    pos_ref, gain_ref, feat_hbm, cot_hbm, k1_hbm, k2_hbm,
    outv, full_ref, stats_ref,
    feat, cot, w1, w2, r1, r2, r2y, grid1, land, grid2, ag, au, ah, ap, pre_ref, hg_ref,
    hid, pgr, part, rcore, sa, ra, sb, rb, rc, gains, units, invs,
    in_sem, hs, hr, cs, cr, a_s, a_r, b_s, b_r, c_s, c_r, eb_s, eb_r, ea_s, ea_r, sib_s, sib_r, gs, gr,
):
    gx = lax.axis_index("gx")
    gy = lax.axis_index("gy")
    core = gy % 2
    coord = ((gy // 2) % 2 * 2 + gx // 4, gx % 4, gy // 4)

    def device(x, y, z):
        return (x % 2 * 4 + y, z * 4 + x // 2 * 2 + core)

    def peer(axis, value):
        return device(*(value if i == axis else coord[i] for i in range(3)))

    sibling = (gx, gy + 1 - 2 * core)

    def there(d):
        x, y = gx + d[0], gy + d[1]
        return (x >= 0) & (x < 8) & (y >= 0) & (y < 16)

    def load(i, src, dst):
        return pltpu.make_async_copy(src, dst, in_sem.at[i])

    loads = [load(0, feat_hbm, feat), load(1, cot_hbm, cot), load(2, k1_hbm, w1), load(3, k2_hbm, w2)]
    for c in loads:
        c.start()

    for g in (grid1, land, grid2):
        for f in range(2):
            for e in (0, 17):
                g[f, e] = jnp.zeros((18, 8, C), BF16)
                for x in range(1, 17):
                    g[f, x, e] = jnp.zeros((8, C), BF16)

    barrier = pltpu.get_barrier_semaphore()
    for d in DIRS:
        @pl.when(there(d))
        def _():
            pl.semaphore_signal(barrier, inc=1, device_id=(gx + d[0], gy + d[1]), device_id_type=MESH)
    for axis in range(3):
        for k in (1, 2, 3):
            pl.semaphore_signal(barrier, inc=1, device_id=peer(axis, (coord[axis] + k) % 4), device_id_type=MESH)
    pl.semaphore_signal(barrier, inc=1, device_id=sibling, device_id_type=MESH)

    p0, p1 = pos_ref[0], pos_ref[1]
    where = [jnp.minimum(p0, POS - 1), jnp.minimum(p1, POS - 1)]
    bx = [w // 2 for w in where]
    by = [w % 2 for w in where]
    live = [(p0 < POS).astype(F32), (p1 < POS).astype(F32)]

    def place(grid, f, source):
        for p in range(POS):
            m0, m1 = (p0 == p).astype(F32), (p1 == p).astype(F32)
            for x in range(8):
                rows = pl.ds(x * 64, 64)
                v = source[0, rows].astype(F32) * m0 + source[1, rows].astype(F32) * m1
                grid[f, 1 + p // 2 * 8 + x, pl.ds(1 + p % 2 * 8, 8)] = v.reshape(8, 8, C).astype(BF16)

    def halo(phase, grid, landing):
        def copies(d):
            i = DIRS.index(d)
            return pltpu.make_async_remote_copy(
                src_ref=grid.at[:, span(d[0], 16, False), span(d[1], 16, False)],
                dst_ref=landing.at[:, span(-d[0], 16, True), span(-d[1], 16, True)],
                send_sem=hs.at[phase, i], recv_sem=hr.at[phase, i],
                device_id=(gx + d[0], gy + d[1]), device_id_type=MESH,
            )

        def start():
            for d in DIRS:
                @pl.when(there(d))
                def _():
                    copies(d).start()

        def arrive():
            for d in DIRS:
                @pl.when(there((-d[0], -d[1])))
                def _():
                    copies(d).wait_recv()

        def done():
            for d in DIRS:
                @pl.when(there(d))
                def _():
                    copies(d).wait_send()

        return start, arrive, done

    start1, arrive1, done1 = halo(0, grid1, land)
    start2, arrive2, done2 = halo(1, grid2, grid2)

    loads[0].wait()
    loads[1].wait()
    place(grid1, 0, feat)
    place(grid1, 1, cot)

    expected = 10
    for d in DIRS:
        expected = expected + there(d).astype(jnp.int32)
    pl.semaphore_wait(barrier, expected)
    start1()

    loads[2].wait()
    loads[3].wait()
    for w, r in ((w2, r2), (w1, r1)):
        for t in range(27):
            r[t // 9, :, pl.ds(t % 9 * C, C)] = w[26 - t]
    for t in range(27):
        r2y[t // 9, t % 9 // 3, :, pl.ds(t % 3 * C, C)] = w2[26 - t]

    z = lax.broadcasted_iota(jnp.int32, (10, 8, C), 1)
    first, last = z == 0, z == 7

    def gather(a, s, grid, f):
        def layer(x, carry):
            t = grid[f, bx[s] * 8 + x, pl.ds(by[s] * 8, 10)].astype(F32)
            down = jnp.where(first, 0.0, pltpu.roll(t, 1, 1))
            up = jnp.where(last, 0.0, pltpu.roll(t, 7, 1))
            for oz, v in enumerate((down, t, up)):
                for oy in range(3):
                    a[s, x, :, pl.ds((oy * 3 + oz) * C, C)] = (
                        v[oy : oy + 8].reshape(64, C).astype(BF16)
                    )
            return carry

        lax.fori_loop(0, 10, layer, 0)

    def conv(a, s, w):
        total = None
        for ox in range(3):
            v = jnp.dot(a[s, pl.ds(ox, 8)].reshape(512, 9 * C), w[pl.ds(ox * 9, 9)].reshape(9 * C, C), preferred_element_type=F32)
            total = v if total is None else total + v
        return total

    def conv_t(a, s, r):
        total = None
        for ox in range(3):
            v = lax.dot_general(a[s, pl.ds(ox, 8)].reshape(512, 9 * C), r[ox], NT, preferred_element_type=F32)
            total = v if total is None else total + v
        return total

    def fix(a, s, f, total, weights, block):
        cx = weights(a[s, bx[s] * 9], bx[s] * 2)
        for i in (0, 1):
            edge = (bx[s] == i).astype(F32)
            total[s, i * 7] = total[s, i * 7] + (cx * edge).reshape(8, 8, C)
        t = grid1[f, pl.ds(bx[s] * 8, 10), by[s] * 17].astype(F32)
        layer = lax.broadcasted_iota(jnp.int32, (10, 8, C), 0)
        low, high = (bx[s] == 1).astype(F32), (bx[s] == 0).astype(F32)
        t = t * jnp.where(layer == 0, low, jnp.where(layer == 9, high, 1.0))
        down = jnp.where(first, 0.0, pltpu.roll(t, 1, 1))
        up = jnp.where(last, 0.0, pltpu.roll(t, 7, 1))
        cy = None
        for ox in range(3):
            rows = jnp.concatenate([v[ox : ox + 8].reshape(64, C) for v in (down, t, up)], axis=1).astype(BF16)
            v = block(rows, ox, by[s] * 2)
            cy = v if cy is None else cy + v
        for i in (0, 1):
            edge = (by[s] == i).astype(F32)
            total[s, :, i * 7] = total[s, :, i * 7] + (cy * edge).reshape(8, 8, C)

    def fix_first(s):
        fix(ag, s, 0, pre_ref,
            lambda rows, ox: jnp.dot(rows, w1[pl.ds(ox * 9, 9)].reshape(9 * C, C), preferred_element_type=F32),
            lambda rows, ox, oy: jnp.dot(
                rows, w1[pl.ds(ox * 9 + oy * 3, 3)].reshape(3 * C, C), preferred_element_type=F32))

    def fix_second(s):
        fix(au, s, 1, hg_ref,
            lambda rows, ox: lax.dot_general(rows, r2[ox], NT, preferred_element_type=F32),
            lambda rows, ox, oy: lax.dot_general(
                rows, r2y[ox, oy], NT, preferred_element_type=F32))

    for s in range(2):
        gather(ag, s, grid1, 0)
        pre_ref[s] = conv(ag, s, w1).reshape(8, 8, 8, C)
    for s in range(2):
        gather(au, s, grid1, 1)
        hg_ref[s] = conv_t(au, s, r2).reshape(8, 8, 8, C)

    arrive1()
    for f in range(2):
        for e in (0, 17):
            grid1[f, e] = land[f, e]
            for x in range(1, 17):
                grid1[f, x, e] = land[f, x, e]
    gain = gain_ref[0:1, :]

    half = pl.multiple_of(core * 64, 64)
    other = pl.multiple_of((1 - core) * 64, 64)

    def core_copy(g):
        return pltpu.make_async_remote_copy(
            src_ref=part.at[pl.ds(g * 9, 9), pl.ds(other, 64)], dst_ref=rcore.at[pl.ds(g * 9, 9)],
            send_sem=cs.at[g], recv_sem=cr.at[g], device_id=sibling, device_id_type=MESH)

    def group(g, a, lhs):
        ox = 2 - g if g < 3 else g - 3
        v = (jnp.dot(lhs[0], a[0, pl.ds(ox, 8)].reshape(512, 9 * C), preferred_element_type=F32)
             + jnp.dot(lhs[1], a[1, pl.ds(ox, 8)].reshape(512, 9 * C), preferred_element_type=F32))
        for k in range(9):
            if g < 3:
                part[g * 9 + 8 - k] = v[:, k * C : (k + 1) * C]
            else:
                part[g * 9 + k] = v[:, k * C : (k + 1) * C].T
        core_copy(g).start()

    def axes(g):
        return ORDERS[g % 3]

    def remote(src, dst, send_sem, recv_sem, to):
        return pltpu.make_async_remote_copy(
            src_ref=src, dst_ref=dst, send_sem=send_sem, recv_sem=recv_sem, device_id=to, device_id_type=MESH)

    def local(ref, send_sem, recv_sem):
        return remote(ref, ref, send_sem, recv_sem, sibling)

    def three(axis, copy):
        for k in (1, 2, 3):
            to = (coord[axis] + k) % 4
            copy(k - 1, to, peer(axis, to)).start()

    def all_a(g):
        return local(ra.at[g], a_s.at[g], a_r.at[g])

    def all_b(g):
        return local(rb.at[g], b_s.at[g], b_r.at[g])

    def all_c(g):
        return local(rc.at[g, pl.ds(0, 3)], c_s.at[g], c_r.at[g])

    def all_eb(g):
        return local(full_ref.at[g, 0, 0, pl.ds(0, 15)], eb_s.at[g], eb_r.at[g])

    def all_ea(g):
        return local(full_ref.at[g, 0, pl.ds(0, 3)], ea_s.at[g], ea_r.at[g])

    def scatter(g):
        core_copy(g).wait_recv()

        def tap(k, carry):
            v = part[g * 9 + k, pl.ds(half, 64)] + rcore[g * 9 + k]
            rcore[g * 9 + k] = v
            sa[g, k] = v.reshape(4, 16, C).astype(BF16)
            return carry

        lax.fori_loop(0, 9, tap, 0)
        three(axes(g)[0], lambda k, to, d: remote(
            sa.at[g, :, to], ra.at[g, k], a_s.at[g], a_r.at[g], d))

    def reduce_a(g):
        all_a(g).wait_recv()
        a, b, _ = axes(g)
        v = rcore[pl.ds(g * 9, 9), pl.ds(pl.multiple_of(coord[a] * 16, 16), 16)]
        for k in range(3):
            v = v + ra[g, k].astype(F32)
        sb[g, pl.ds(0, 18)] = v.reshape(18, 8, C)
        three(b, lambda k, to, d: remote(
            sb.at[g, pl.ds(to * 5, 5)], rb.at[g, k], b_s.at[g], b_r.at[g], d))

    def reduce_b(g):
        all_b(g).wait_recv()
        _, b, c = axes(g)
        v = sb[g, pl.ds(coord[b] * 5, 5)]
        for k in range(3):
            v = v + rb[g, k]
        rc[g, coord[c]] = v
        mine = rc.at[g, coord[c]]
        three(c, lambda k, to, d: remote(mine, mine, c_s.at[g], c_r.at[g], d))

    def reduce_c(g):
        all_c(g).wait_recv()
        a, b, _ = axes(g)
        v = ((rc[g, 0] + rc[g, 1]) + rc[g, 2]) + rc[g, 3]
        full_ref[g, core, coord[a], pl.ds(coord[b] * 5, 5)] = v.astype(BF16)
        mine = full_ref.at[g, core, coord[a], pl.ds(coord[b] * 5, 5)]
        three(b, lambda k, to, d: remote(mine, mine, eb_s.at[g], eb_r.at[g], d))

    def spread(g):
        all_eb(g).wait_recv()
        a = axes(g)[0]
        mine = full_ref.at[g, core, coord[a]]
        three(a, lambda k, to, d: remote(mine, mine, ea_s.at[g], ea_r.at[g], d))

    def sib_copy(chunk):
        ref = full_ref.at[pl.ds(chunk * 3, 3), core]
        return remote(ref, ref, sib_s.at[chunk], sib_r.at[chunk], sibling)

    def pass_on(chunk):
        for g in range(chunk * 3, chunk * 3 + 3):
            all_ea(g).wait_recv()
        sib_copy(chunk).start()

    def gain_copy(stage, k):
        if stage == 0:
            return pltpu.make_async_remote_copy(
                src_ref=gains.at[0, 0], dst_ref=gains.at[0, 1], send_sem=gs.at[0], recv_sem=gr.at[0],
                device_id=sibling, device_id_type=MESH)
        axis = stage - 1
        i = 1 + axis * 3 + k - 1
        return pltpu.make_async_remote_copy(
            src_ref=gains.at[stage, coord[axis]], dst_ref=gains.at[stage, coord[axis]],
            send_sem=gs.at[i], recv_sem=gr.at[i],
            device_id=peer(axis, (coord[axis] + k) % 4), device_id_type=MESH)

    def gain_step(stage):
        if stage == 0:
            gain_copy(0, 0).wait_recv()
            gains[1, coord[0]] = gains[0, 0] + gains[0, 1]
        else:
            for k in (1, 2, 3):
                gain_copy(stage, k).wait_recv()
            v = ((gains[stage, 0] + gains[stage, 1]) + gains[stage, 2]) + gains[stage, 3]
            if stage == 3:
                return v
            gains[stage + 1, coord[stage]] = v
        for k in (1, 2, 3):
            gain_copy(stage + 1, k).start()

    def second_half(s, f):
        if f == 0:
            gather(ah, s, grid2, 0)
            v = conv(ah, s, w2) * live[s] + feat[s].astype(F32) * live[s]
        else:
            gather(ap, s, grid2, 1)
            v = (conv_t(ap, s, r1) + cot[s].astype(F32)) * live[s]
        outv[f, s] = v.astype(BF16)

    def forward(s):
        gather(ag, s, grid1, 0)
        fix_first(s)
        pre = pre_ref[s].reshape(512, C)
        center = pre - jnp.mean(pre, axis=-1, keepdims=True)
        inv = lax.rsqrt(jnp.mean(center * center, axis=-1, keepdims=True) + 1e-05)
        unit = center * inv
        normed = unit * gain
        sig = jax.nn.sigmoid(normed)
        hidden = normed * sig * live[s]
        hid[s] = hidden.astype(BF16)
        units[s] = unit
        invs[s] = jnp.broadcast_to(inv, (512, C))
        return hidden.T.astype(BF16)

    def backward(s):
        fix_second(s)
        hgrad = hg_ref[s].reshape(512, C) * live[s]
        unit, inv = units[s], invs[s]
        normed = unit * gain
        sig = jax.nn.sigmoid(normed)
        dn = hgrad * (sig * (1.0 + normed * (1.0 - sig)))
        du = dn * gain
        dc = inv * (du - unit * jnp.mean(du * unit, axis=-1, keepdims=True))
        pg = (dc - jnp.mean(dc, axis=-1, keepdims=True)) * live[s]
        pgr[s] = pg.astype(BF16)
        return pg.T.astype(BF16), jnp.sum(dn * unit, axis=0, keepdims=True)

    for g in range(6):
        sb[g, pl.ds(18, 2)] = jnp.zeros((2, 8, C), F32)
    hid_t = [forward(0), forward(1)]
    gather(au, 0, grid1, 1)
    gather(au, 1, grid1, 1)
    early, late = (0, 1, 2), (3, 4, 5)
    for g in early:
        group(g, au, hid_t)
    pg0, gg0 = backward(0)
    for g in early:
        scatter(g)
    pg1, gg1 = backward(1)
    gains[0, 0] = jnp.broadcast_to(gg0 + gg1, (8, C))
    gain_copy(0, 0).start()
    for g in late:
        group(g, ag, [pg0, pg1])
    place(grid2, 0, hid)
    place(grid2, 1, pgr)
    start2()
    for g in late:
        scatter(g)
    gain_step(0)
    for g in early:
        reduce_a(g)
    arrive2()
    second_half(0, 0)
    for g in late:
        reduce_a(g)
    for g in early:
        reduce_b(g)
    gain_step(1)
    second_half(1, 0)
    for g in late:
        reduce_b(g)
    for g in early:
        reduce_c(g)
    gain_step(2)
    second_half(0, 1)
    for g in late:
        reduce_c(g)
    for g in early:
        spread(g)
    second_half(1, 1)
    gain_sum = gain_step(3)
    for g in late:
        spread(g)
    pass_on(0)

    def squares(chunk, acc):
        sib_copy(chunk).wait_recv()

        def part_of(i, acc):
            v = full_ref[chunk * 3 + i // 8, i // 4 % 2, i % 4, pl.ds(0, 18)].astype(F32)
            return acc + jnp.sum(v * v, axis=0)

        return lax.fori_loop(0, 24, part_of, acc)

    acc = squares(0, jnp.zeros((8, C), F32))
    pass_on(1)
    acc = squares(1, acc)
    total = jnp.sum(acc) + jnp.sum(gain_sum[0:1] * gain_sum[0:1])
    entries = 54.0 * C * C + C
    mean = jnp.full((8, C), total / entries + 1e-06, F32)
    shrink = jnp.minimum(1.0, CLIP / jnp.sqrt(mean))
    stats_ref[0] = shrink
    stats_ref[1] = shrink * gain_sum

    done1()
    done2()
    for g in range(6):
        core_copy(g).wait_send()
        for sent in (all_a, all_b, all_c, all_eb, all_ea):
            sent(g).wait_send()
    for chunk in (0, 1):
        sib_copy(chunk).wait_send()
    gain_copy(0, 0).wait_send()
    for k in (1, 2, 3):
        for stage in (1, 2, 3):
            gain_copy(stage, k).wait_send()


def finish_kernel(outv, full_ref, stats_ref, out_hbm, fgrad_hbm, update_hbm, gain_ref, scaled, sem):
    copies = [pltpu.make_async_copy(outv.at[0], out_hbm, sem.at[18]),
              pltpu.make_async_copy(outv.at[1], fgrad_hbm, sem.at[19])]
    for c in copies:
        c.start()
    shrink = stats_ref[0, 0:1, :]
    for g in range(6):
        for k in range(9):
            for h in range(2):
                v = full_ref[g, h, :, pl.ds(k * 2, 2)].astype(F32).reshape(64, C)
                scaled[g, k, pl.ds(h * 64, 64)] = v * shrink
            if k % 3 == 2:
                c = pltpu.make_async_copy(
                    scaled.at[g, pl.ds(k - 2, 3)], update_hbm.at[1 - g // 3, pl.ds(g % 3 * 9 + k - 2, 3)],
                    sem.at[g * 3 + k // 3])
                c.start()
                copies.append(c)
    gain_ref[...] = stats_ref[1, 0:1, :]
    for c in copies:
        c.wait()


def per_device(features, brick_pos, cotangent, first_kernel, second_kernel, norm_gain):
    hbm = pl.BlockSpec(memory_space=pltpu.HBM)
    vmem = pl.BlockSpec(memory_space=pltpu.VMEM)
    dma = pltpu.SemaphoreType.DMA
    V = pltpu.VMEM
    tile = (2, 10, 64, 9 * C)
    outv, full, stats = pl.pallas_call(
        step_kernel,
        out_shape=(V((2, 2, 512, C), BF16), V((6, 2, 4, 20, 8, C), BF16), V((2, 8, C), F32)),
        in_specs=[pl.BlockSpec(memory_space=pltpu.SMEM), vmem, hbm, hbm, hbm, hbm],
        out_specs=(vmem, vmem, vmem),
        scratch_shapes=[
            V((2, 512, C), BF16), V((2, 512, C), BF16),
            V((27, C, C), BF16), V((27, C, C), BF16),
            V((3, C, 9 * C), BF16), V((3, C, 9 * C), BF16), V((3, 3, C, 3 * C), BF16),
            V((2, 18, 18, 8, C), BF16), V((2, 18, 18, 8, C), BF16), V((2, 18, 18, 8, C), BF16),
            V(tile, BF16), V(tile, BF16), V(tile, BF16), V(tile, BF16),
            V((2, 8, 8, 8, C), F32), V((2, 8, 8, 8, C), F32),
            V((2, 512, C), BF16), V((2, 512, C), BF16),
            V((54, C, C), F32), V((54, 64, C), F32),
            V((6, 9, 4, 16, C), BF16), V((6, 3, 9, 16, C), BF16),
            V((6, 20, 8, C), F32), V((6, 3, 5, 8, C), F32), V((6, 4, 5, 8, C), F32),
            V((4, 4, 8, C), F32),
            V((2, 512, C), F32), V((2, 512, C), F32),
            dma((4,)), dma((2, 8)), dma((2, 8)), dma((6,)), dma((6,)),
            dma((6,)), dma((6,)), dma((6,)), dma((6,)), dma((6,)), dma((6,)),
            dma((6,)), dma((6,)), dma((6,)), dma((6,)),
            dma((2,)), dma((2,)), dma((10,)), dma((10,)),
        ],
        compiler_params=pltpu.CompilerParams(
            collective_id=0, has_side_effects=True, vmem_limit_bytes=56 * 2**20
        ),
        name="step",
    )(brick_pos, norm_gain.reshape(1, C), features, cotangent, first_kernel, second_kernel)
    out, fgrad, update, gain = pl.pallas_call(
        finish_kernel,
        out_shape=(
            jax.ShapeDtypeStruct((2, 512, C), BF16),
            jax.ShapeDtypeStruct((2, 512, C), BF16),
            jax.ShapeDtypeStruct((2, 27, C, C), F32),
            jax.ShapeDtypeStruct((1, C), F32),
        ),
        in_specs=[vmem, vmem, vmem],
        out_specs=(hbm, hbm, hbm, vmem),
        scratch_shapes=[V((6, 9, C, C), F32), dma((20,))],
        compiler_params=pltpu.CompilerParams(vmem_limit_bytes=10 * 2**20),
        name="finish",
    )(outv, full, stats)
    return out, fgrad, update, gain.reshape(C)


def solution(mesh):
    rows = P(("gx", "gy"), None, None)
    return jax.shard_map(
        per_device, mesh=mesh, in_specs=(rows, P(("gx", "gy")), rows, P(), P(), P()),
        out_specs=(rows, rows, P(), P()), check_vma=False,
    )
```

```python
import jax
import jax.numpy as jnp
from jax import lax
from jax.experimental import pallas as pl
from jax.experimental.pallas import tpu as pltpu
from jax.sharding import PartitionSpec as P

MESH = pl.DeviceIdType.MESH
F32 = jnp.float32
BF16 = jnp.bfloat16
CLIP = 0.5
C = 128
POS = 4
DIRS = [(dx, dy) for dx in (-1, 0, 1) for dy in (-1, 0, 1) if (dx, dy) != (0, 0)]
ORDERS = [(0, 1, 2), (1, 2, 0), (2, 0, 1)]
NT = (((1,), (1,)), ((), ()))


def span(d, size, halo):
    if d == 0:
        return pl.ds(1, 16)
    if d < 0:
        return pl.ds(0 if halo else 1, 1)
    return pl.ds(17 if halo else 16, 1)


def step_kernel(
    pos_ref, gain_ref, feat_hbm, cot_hbm, k1_hbm, k2_hbm,
    outv, full_ref, stats_ref,
    feat, cot, w1, w2, r1, r2, r2y, grid1, land, grid2, ag, au, ah, ap, pre_ref, hg_ref,
    hid, pgr, part, rcore, sa, ra, sb, rb, rc, gains, units, invs,
    in_sem, hs, hr, cs, cr, a_s, a_r, b_s, b_r, c_s, c_r, eb_s, eb_r, ea_s, ea_r, sib_s, sib_r, gs, gr,
):
    gx = lax.axis_index("gx")
    gy = lax.axis_index("gy")
    core = gy % 2
    coord = ((gy // 2) % 2 * 2 + gx // 4, gx % 4, gy // 4)

    def device(x, y, z):
        return (x % 2 * 4 + y, z * 4 + x // 2 * 2 + core)

    def peer(axis, value):
        return device(*(value if i == axis else coord[i] for i in range(3)))

    sibling = (gx, gy + 1 - 2 * core)

    def there(d):
        x, y = gx + d[0], gy + d[1]
        return (x >= 0) & (x < 8) & (y >= 0) & (y < 16)

    def load(i, src, dst):
        return pltpu.make_async_copy(src, dst, in_sem.at[i])

    loads = [load(0, feat_hbm, feat), load(1, cot_hbm, cot), load(2, k1_hbm, w1), load(3, k2_hbm, w2)]
    for c in loads:
        c.start()

    for g in (grid1, land, grid2):
        for f in range(2):
            for e in (0, 17):
                g[f, e] = jnp.zeros((18, 8, C), BF16)
                for x in range(1, 17):
                    g[f, x, e] = jnp.zeros((8, C), BF16)

    barrier = pltpu.get_barrier_semaphore()
    for d in DIRS:
        @pl.when(there(d))
        def _():
            pl.semaphore_signal(barrier, inc=1, device_id=(gx + d[0], gy + d[1]), device_id_type=MESH)
    for axis in range(3):
        for k in (1, 2, 3):
            pl.semaphore_signal(barrier, inc=1, device_id=peer(axis, (coord[axis] + k) % 4), device_id_type=MESH)
    pl.semaphore_signal(barrier, inc=1, device_id=sibling, device_id_type=MESH)

    p0, p1 = pos_ref[0], pos_ref[1]
    where = [jnp.minimum(p0, POS - 1), jnp.minimum(p1, POS - 1)]
    bx = [w // 2 for w in where]
    by = [w % 2 for w in where]
    live = [(p0 < POS).astype(F32), (p1 < POS).astype(F32)]

    def place(grid, f, source):
        for p in range(POS):
            m0, m1 = (p0 == p).astype(F32), (p1 == p).astype(F32)
            for x in range(8):
                rows = pl.ds(x * 64, 64)
                v = source[0, rows].astype(F32) * m0 + source[1, rows].astype(F32) * m1
                grid[f, 1 + p // 2 * 8 + x, pl.ds(1 + p % 2 * 8, 8)] = v.reshape(8, 8, C).astype(BF16)

    def halo(phase, grid, landing):
        def copies(d):
            i = DIRS.index(d)
            return pltpu.make_async_remote_copy(
                src_ref=grid.at[:, span(d[0], 16, False), span(d[1], 16, False)],
                dst_ref=landing.at[:, span(-d[0], 16, True), span(-d[1], 16, True)],
                send_sem=hs.at[phase, i], recv_sem=hr.at[phase, i],
                device_id=(gx + d[0], gy + d[1]), device_id_type=MESH,
            )

        def start():
            for d in DIRS:
                @pl.when(there(d))
                def _():
                    copies(d).start()

        def arrive():
            for d in DIRS:
                @pl.when(there((-d[0], -d[1])))
                def _():
                    copies(d).wait_recv()

        def done():
            for d in DIRS:
                @pl.when(there(d))
                def _():
                    copies(d).wait_send()

        return start, arrive, done

    start1, arrive1, done1 = halo(0, grid1, land)
    start2, arrive2, done2 = halo(1, grid2, grid2)

    loads[0].wait()
    loads[1].wait()
    place(grid1, 0, feat)
    place(grid1, 1, cot)

    expected = 10
    for d in DIRS:
        expected = expected + there(d).astype(jnp.int32)
    pl.semaphore_wait(barrier, expected)
    start1()

    loads[2].wait()
    loads[3].wait()
    for t in range(27):
        r2[t // 9, :, pl.ds(t % 9 * C, C)] = w2[26 - t]
        r2y[t // 9, t % 9 // 3, :, pl.ds(t % 3 * C, C)] = w2[26 - t]

    z = lax.broadcasted_iota(jnp.int32, (10, 8, C), 1)
    first, last = z == 0, z == 7

    def sides(t):
        n = t.shape[0]
        return (jnp.where(first[:n], 0.0, pltpu.roll(t, 1, 1)), t, jnp.where(last[:n], 0.0, pltpu.roll(t, 7, 1)))

    def gather(a, s, grid, f, layers=None):
        def layer(x, carry):
            t = grid[f, bx[s] * 8 + x, pl.ds(by[s] * 8, 10)].astype(F32)
            for oz, v in enumerate(sides(t)):
                for oy in range(3):
                    a[s, x, :, pl.ds((oy * 3 + oz) * C, C)] = v[oy : oy + 8].reshape(64, C).astype(BF16)
            return carry

        if layers is None:
            lax.fori_loop(0, 10, layer, 0)
        else:
            for x in layers:
                layer(x, 0)

    def patch(a, s, grid, f):
        gather(a, s, grid, f, (0, 9))

        def layer(x, carry):
            for oy in (0, 2):
                t = grid[f, bx[s] * 8 + x, pl.ds(by[s] * 8 + oy * 4, 2)].astype(F32)
                for oz, v in enumerate(sides(t)):
                    a[s, x, pl.ds(oy * 24, 16), pl.ds((oy * 3 + oz) * C, C)] = v.reshape(16, C).astype(BF16)
            return carry

        lax.fori_loop(1, 9, layer, 0)

    def conv(a, s, w):
        total = None
        for ox in range(3):
            v = jnp.dot(a[s, pl.ds(ox, 8)].reshape(512, 9 * C), w[pl.ds(ox * 9, 9)].reshape(9 * C, C), preferred_element_type=F32)
            total = v if total is None else total + v
        return total

    def conv_t(a, s, r):
        total = None
        for ox in range(3):
            v = lax.dot_general(a[s, pl.ds(ox, 8)].reshape(512, 9 * C), r[ox], NT, preferred_element_type=F32)
            total = v if total is None else total + v
        return total

    def fix(a, s, f, total, weights, block):
        cx = weights(a[s, bx[s] * 9], bx[s] * 2)
        for i in (0, 1):
            edge = (bx[s] == i).astype(F32)
            total[i * 7] = total[i * 7] + (cx * edge).reshape(8, 8, C)
        t = grid1[f, pl.ds(bx[s] * 8, 10), by[s] * 17].astype(F32)
        layer = lax.broadcasted_iota(jnp.int32, (10, 8, C), 0)
        low, high = (bx[s] == 1).astype(F32), (bx[s] == 0).astype(F32)
        t = t * jnp.where(layer == 0, low, jnp.where(layer == 9, high, 1.0))
        shifted = sides(t)
        cy = None
        for ox in range(3):
            rows = jnp.concatenate([v[ox : ox + 8].reshape(64, C) for v in shifted], axis=1).astype(BF16)
            v = block(rows, ox, by[s] * 2)
            cy = v if cy is None else cy + v
        for i in (0, 1):
            edge = (by[s] == i).astype(F32)
            total[:, i * 7] = total[:, i * 7] + (cy * edge).reshape(8, 8, C)

    def fix_first(s):
        fix(ag, s, 0, pre_ref.at[s],
            lambda rows, ox: jnp.dot(rows, w1[pl.ds(ox * 9, 9)].reshape(9 * C, C), preferred_element_type=F32),
            lambda rows, ox, oy: jnp.dot(
                rows, w1[pl.ds(ox * 9 + oy * 3, 3)].reshape(3 * C, C), preferred_element_type=F32))

    def fix_second():
        fix(au, 0, 1, hg_ref,
            lambda rows, ox: lax.dot_general(rows, r2[ox], NT, preferred_element_type=F32),
            lambda rows, ox, oy: lax.dot_general(
                rows, r2y[ox, oy], NT, preferred_element_type=F32))

    for s in range(2):
        gather(ag, s, grid1, 0)
        pre_ref[s] = conv(ag, s, w1).reshape(8, 8, 8, C)
    gather(au, 0, grid1, 1)
    hg_ref[...] = conv_t(au, 0, r2).reshape(8, 8, 8, C)

    arrive1()
    for f in range(2):
        for e in (0, 17):
            grid1[f, e] = land[f, e]
            for x in range(1, 17):
                grid1[f, x, e] = land[f, x, e]
    gain = gain_ref[0:1, :]

    half = pl.multiple_of(core * 64, 64)
    other = pl.multiple_of((1 - core) * 64, 64)

    def core_copy(g):
        return pltpu.make_async_remote_copy(
            src_ref=part.at[pl.ds(g * 9, 9), pl.ds(other, 64)], dst_ref=rcore.at[pl.ds(g * 9, 9)],
            send_sem=cs.at[g], recv_sem=cr.at[g], device_id=sibling, device_id_type=MESH)

    def group(g, a, lhs):
        ox = 2 - g if g < 3 else g - 3
        v = (jnp.dot(lhs[0], a[0, pl.ds(ox, 8)].reshape(512, 9 * C), preferred_element_type=F32)
             + jnp.dot(lhs[1], a[1, pl.ds(ox, 8)].reshape(512, 9 * C), preferred_element_type=F32))
        for k in range(9):
            if g < 3:
                part[g * 9 + 8 - k] = v[:, k * C : (k + 1) * C]
            else:
                part[g * 9 + k] = v[:, k * C : (k + 1) * C].T
        core_copy(g).start()

    def axes(g):
        return ORDERS[g % 3]

    def remote(src, dst, send_sem, recv_sem, to):
        return pltpu.make_async_remote_copy(
            src_ref=src, dst_ref=dst, send_sem=send_sem, recv_sem=recv_sem, device_id=to, device_id_type=MESH)

    def local(ref, send_sem, recv_sem):
        return remote(ref, ref, send_sem, recv_sem, sibling)

    def three(axis, copy):
        for k in (1, 2, 3):
            to = (coord[axis] + k) % 4
            copy(k - 1, to, peer(axis, to)).start()

    def all_a(g):
        return local(ra.at[g], a_s.at[g], a_r.at[g])

    def all_b(g):
        return local(rb.at[g], b_s.at[g], b_r.at[g])

    def all_c(g):
        return local(rc.at[g, pl.ds(0, 3)], c_s.at[g], c_r.at[g])

    def all_eb(g):
        return local(full_ref.at[g, 0, 0, pl.ds(0, 15)], eb_s.at[g], eb_r.at[g])

    def all_ea(g):
        return local(full_ref.at[g, 0, pl.ds(0, 3)], ea_s.at[g], ea_r.at[g])

    def scatter(g):
        core_copy(g).wait_recv()

        def tap(k, carry):
            v = part[g * 9 + k, pl.ds(half, 64)] + rcore[g * 9 + k]
            rcore[g * 9 + k] = v
            sa[g, k] = v.reshape(4, 16, C).astype(BF16)
            return carry

        lax.fori_loop(0, 9, tap, 0)
        three(axes(g)[0], lambda k, to, d: remote(
            sa.at[g, :, to], ra.at[g, k], a_s.at[g], a_r.at[g], d))

    def reduce_a(g):
        all_a(g).wait_recv()
        a, b, _ = axes(g)
        v = rcore[pl.ds(g * 9, 9), pl.ds(pl.multiple_of(coord[a] * 16, 16), 16)]
        for k in range(3):
            v = v + ra[g, k].astype(F32)
        sb[g, pl.ds(0, 18)] = v.reshape(18, 8, C)
        three(b, lambda k, to, d: remote(
            sb.at[g, pl.ds(to * 5, 5)], rb.at[g, k], b_s.at[g], b_r.at[g], d))

    def reduce_b(g):
        all_b(g).wait_recv()
        _, b, c = axes(g)
        v = sb[g, pl.ds(coord[b] * 5, 5)]
        for k in range(3):
            v = v + rb[g, k]
        rc[g, coord[c]] = v
        mine = rc.at[g, coord[c]]
        three(c, lambda k, to, d: remote(mine, mine, c_s.at[g], c_r.at[g], d))

    def reduce_c(g):
        all_c(g).wait_recv()
        a, b, _ = axes(g)
        v = ((rc[g, 0] + rc[g, 1]) + rc[g, 2]) + rc[g, 3]
        full_ref[g, core, coord[a], pl.ds(coord[b] * 5, 5)] = v.astype(BF16)
        mine = full_ref.at[g, core, coord[a], pl.ds(coord[b] * 5, 5)]
        three(b, lambda k, to, d: remote(mine, mine, eb_s.at[g], eb_r.at[g], d))

    def spread(g):
        all_eb(g).wait_recv()
        a = axes(g)[0]
        mine = full_ref.at[g, core, coord[a]]
        three(a, lambda k, to, d: remote(mine, mine, ea_s.at[g], ea_r.at[g], d))

    def sib_copy(g):
        ref = full_ref.at[g, core]
        return remote(ref, ref, sib_s.at[g], sib_r.at[g], sibling)

    def squares(g, h):
        acc = None
        for a in range(4):
            v = full_ref[g, h, a, pl.ds(0, 18)].astype(F32)
            v = jnp.sum(v * v, axis=0)
            acc = v if acc is None else acc + v
        return acc

    def pass_on(g):
        all_ea(g).wait_recv()
        sib_copy(g).start()

    def close(groups):
        for g in groups:
            pass_on(g)
        own = [squares(g, core) for g in groups]
        acc = jnp.zeros((8, C), F32)
        for g, mine in zip(groups, own):
            sib_copy(g).wait_recv()
            acc = acc + (mine + squares(g, 1 - core))
        return acc

    def gain_copy(stage, k):
        if stage == 0:
            return pltpu.make_async_remote_copy(
                src_ref=gains.at[0, 0], dst_ref=gains.at[0, 1], send_sem=gs.at[0], recv_sem=gr.at[0],
                device_id=sibling, device_id_type=MESH)
        axis = stage - 1
        i = 1 + axis * 3 + k - 1
        return pltpu.make_async_remote_copy(
            src_ref=gains.at[stage, coord[axis]], dst_ref=gains.at[stage, coord[axis]],
            send_sem=gs.at[i], recv_sem=gr.at[i],
            device_id=peer(axis, (coord[axis] + k) % 4), device_id_type=MESH)

    def gain_step(stage):
        if stage == 0:
            gain_copy(0, 0).wait_recv()
            gains[1, coord[0]] = gains[0, 0] + gains[0, 1]
        else:
            for k in (1, 2, 3):
                gain_copy(stage, k).wait_recv()
            v = ((gains[stage, 0] + gains[stage, 1]) + gains[stage, 2]) + gains[stage, 3]
            if stage == 3:
                return v
            gains[stage + 1, coord[stage]] = v
        for k in (1, 2, 3):
            gain_copy(stage + 1, k).start()

    def second_half(s, f):
        if f == 0:
            gather(ah, s, grid2, 0)
            v = conv(ah, s, w2) * live[s] + feat[s].astype(F32) * live[s]
        else:
            gather(ap, s, grid2, 1)
            v = (conv_t(ap, s, r1) + cot[s].astype(F32)) * live[s]
        outv[f, s] = v.astype(BF16)

    def forward(s):
        patch(ag, s, grid1, 0)
        fix_first(s)
        pre = pre_ref[s].reshape(512, C)
        center = pre - jnp.mean(pre, axis=-1, keepdims=True)
        inv = lax.rsqrt(jnp.mean(center * center, axis=-1, keepdims=True) + 1e-05)
        unit = center * inv
        normed = unit * gain
        sig = jax.nn.sigmoid(normed)
        hidden = normed * sig * live[s]
        hid[s] = hidden.astype(BF16)
        units[s] = unit
        invs[s] = jnp.broadcast_to(inv, (512, C))
        return hidden.T.astype(BF16)

    def backward(s):
        if s == 0:
            fix_second()
            hgrad = hg_ref[...].reshape(512, C) * live[s]
        else:
            hgrad = conv_t(au, s, r2) * live[s]
        unit, inv = units[s], invs[s]
        normed = unit * gain
        sig = jax.nn.sigmoid(normed)
        dn = hgrad * (sig * (1.0 + normed * (1.0 - sig)))
        du = dn * gain
        dc = inv * (du - unit * jnp.mean(du * unit, axis=-1, keepdims=True))
        pg = (dc - jnp.mean(dc, axis=-1, keepdims=True)) * live[s]
        pgr[s] = pg.astype(BF16)
        return pg.T.astype(BF16), jnp.sum(dn * unit, axis=0, keepdims=True)

    for g in range(6):
        sb[g, pl.ds(18, 2)] = jnp.zeros((2, 8, C), F32)
    hid_t = [forward(0), forward(1)]
    patch(au, 0, grid1, 1)
    gather(au, 1, grid1, 1)
    early, late = (0, 1, 2), (3, 4, 5)
    for g in early:
        group(g, au, hid_t)
    pg0, gg0 = backward(0)
    for g in early:
        scatter(g)
    pg1, gg1 = backward(1)
    gains[0, 0] = jnp.broadcast_to(gg0 + gg1, (8, C))
    gain_copy(0, 0).start()
    for g in late:
        group(g, ag, [pg0, pg1])
    scatter(3)
    scatter(4)
    place(grid2, 0, hid)
    scatter(5)
    place(grid2, 1, pgr)
    start2()
    gain_step(0)
    for t in range(27):
        r1[t // 9, :, pl.ds(t % 9 * C, C)] = w1[26 - t]
    for g in early:
        reduce_a(g)
    arrive2()
    second_half(0, 0)
    for g in late:
        reduce_a(g)
    for g in early:
        reduce_b(g)
    gain_step(1)
    second_half(1, 0)
    for g in late:
        reduce_b(g)
    for g in early:
        reduce_c(g)
    gain_step(2)
    second_half(0, 1)
    for g in late:
        reduce_c(g)
    for g in early:
        spread(g)
    second_half(1, 1)
    gain_sum = gain_step(3)
    for g in late:
        spread(g)
    acc = close(early)

    acc = acc + close(late)
    total = jnp.sum(acc) + jnp.sum(gain_sum[0:1] * gain_sum[0:1])
    entries = 54.0 * C * C + C
    mean = jnp.full((8, C), total / entries + 1e-06, F32)
    shrink = jnp.minimum(1.0, CLIP / jnp.sqrt(mean))
    stats_ref[0] = shrink
    stats_ref[1] = shrink * gain_sum

    done1()
    done2()
    for g in range(6):
        core_copy(g).wait_send()
        sib_copy(g).wait_send()
        for sent in (all_a, all_b, all_c, all_eb, all_ea):
            sent(g).wait_send()
    gain_copy(0, 0).wait_send()
    for k in (1, 2, 3):
        for stage in (1, 2, 3):
            gain_copy(stage, k).wait_send()


def finish_kernel(outv, full_ref, stats_ref, out_hbm, fgrad_hbm, update_hbm, gain_ref, scaled, sem):
    copies = [pltpu.make_async_copy(outv.at[0], out_hbm, sem.at[18]),
              pltpu.make_async_copy(outv.at[1], fgrad_hbm, sem.at[19])]
    for c in copies:
        c.start()
    shrink = stats_ref[0, 0:1, :]
    for g in range(6):
        for k in range(9):
            for h in range(2):
                v = full_ref[g, h, :, pl.ds(k * 2, 2)].astype(F32).reshape(64, C)
                scaled[g, k, pl.ds(h * 64, 64)] = v * shrink
            if k % 3 == 2:
                c = pltpu.make_async_copy(
                    scaled.at[g, pl.ds(k - 2, 3)], update_hbm.at[1 - g // 3, pl.ds(g % 3 * 9 + k - 2, 3)],
                    sem.at[g * 3 + k // 3])
                c.start()
                copies.append(c)
    gain_ref[...] = stats_ref[1, 0:1, :]
    for c in copies:
        c.wait()


def per_device(features, brick_pos, cotangent, first_kernel, second_kernel, norm_gain):
    hbm = pl.BlockSpec(memory_space=pltpu.HBM)
    vmem = pl.BlockSpec(memory_space=pltpu.VMEM)
    dma = pltpu.SemaphoreType.DMA
    V = pltpu.VMEM
    tile = (2, 10, 64, 9 * C)
    outv, full, stats = pl.pallas_call(
        step_kernel,
        out_shape=(V((2, 2, 512, C), BF16), V((6, 2, 4, 20, 8, C), BF16), V((2, 8, C), F32)),
        in_specs=[pl.BlockSpec(memory_space=pltpu.SMEM), vmem, hbm, hbm, hbm, hbm],
        out_specs=(vmem, vmem, vmem),
        scratch_shapes=[
            V((2, 512, C), BF16), V((2, 512, C), BF16),
            V((27, C, C), BF16), V((27, C, C), BF16),
            V((3, C, 9 * C), BF16), V((3, C, 9 * C), BF16), V((3, 3, C, 3 * C), BF16),
            V((2, 18, 18, 8, C), BF16), V((2, 18, 18, 8, C), BF16), V((2, 18, 18, 8, C), BF16),
            V(tile, BF16), V(tile, BF16), V(tile, BF16), V(tile, BF16),
            V((2, 8, 8, 8, C), F32), V((8, 8, 8, C), F32),
            V((2, 512, C), BF16), V((2, 512, C), BF16),
            V((54, C, C), F32), V((54, 64, C), F32),
            V((6, 9, 4, 16, C), BF16), V((6, 3, 9, 16, C), BF16),
            V((6, 20, 8, C), F32), V((6, 3, 5, 8, C), F32), V((6, 4, 5, 8, C), F32),
            V((4, 4, 8, C), F32),
            V((2, 512, C), F32), V((2, 512, C), F32),
            dma((4,)), dma((2, 8)), dma((2, 8)), dma((6,)), dma((6,)),
            dma((6,)), dma((6,)), dma((6,)), dma((6,)), dma((6,)), dma((6,)),
            dma((6,)), dma((6,)), dma((6,)), dma((6,)),
            dma((6,)), dma((6,)), dma((10,)), dma((10,)),
        ],
        compiler_params=pltpu.CompilerParams(
            collective_id=0, has_side_effects=True, vmem_limit_bytes=56 * 2**20
        ),
        name="step",
    )(brick_pos, norm_gain.reshape(1, C), features, cotangent, first_kernel, second_kernel)
    out, fgrad, update, gain = pl.pallas_call(
        finish_kernel,
        out_shape=(
            jax.ShapeDtypeStruct((2, 512, C), BF16),
            jax.ShapeDtypeStruct((2, 512, C), BF16),
            jax.ShapeDtypeStruct((2, 27, C, C), F32),
            jax.ShapeDtypeStruct((1, C), F32),
        ),
        in_specs=[vmem, vmem, vmem],
        out_specs=(hbm, hbm, hbm, vmem),
        scratch_shapes=[V((6, 9, C, C), F32), dma((20,))],
        compiler_params=pltpu.CompilerParams(vmem_limit_bytes=10 * 2**20),
        name="finish",
    )(outv, full, stats)
    return out, fgrad, update, gain.reshape(C)


def solution(mesh):
    rows = P(("gx", "gy"), None, None)
    return jax.shard_map(
        per_device, mesh=mesh, in_specs=(rows, P(("gx", "gy")), rows, P(), P(), P()),
        out_specs=(rows, rows, P(), P()), check_vma=False,
    )
```

```python
import jax
import jax.numpy as jnp
from jax import lax
from jax.experimental import pallas as pl
from jax.experimental.pallas import tpu as pltpu
from jax.sharding import PartitionSpec as P

MESH = pl.DeviceIdType.MESH
F32 = jnp.float32
BF16 = jnp.bfloat16
CLIP = 0.5
C = 128
POS = 4
DIRS = [(dx, dy) for dx in (-1, 0, 1) for dy in (-1, 0, 1) if (dx, dy) != (0, 0)]
ORDERS = [(0, 1, 2), (1, 2, 0), (2, 0, 1)]
NT = (((1,), (1,)), ((), ()))


def span(d, size, halo):
    if d == 0:
        return pl.ds(1, 16)
    if d < 0:
        return pl.ds(0 if halo else 1, 1)
    return pl.ds(17 if halo else 16, 1)


def step_kernel(
    pos_ref, gain_ref, feat_hbm, cot_hbm, k1_hbm, k2_hbm,
    outv, full_ref, stats_ref,
    feat, cot, w1, w2, r1, r2, r2y, grid1, land, grid2, ag, au, ah, ap, pre_ref, hg_ref,
    hid, pgr, part, rcore, sa, ra, sb, rb, rc, gains, units, invs,
    in_sem, hs, hr, cs, cr, a_s, a_r, b_s, b_r, c_s, c_r, eb_s, eb_r, ea_s, ea_r, sib_s, sib_r, gs, gr,
):
    gx = lax.axis_index("gx")
    gy = lax.axis_index("gy")
    core = gy % 2
    coord = ((gy // 2) % 2 * 2 + gx // 4, gx % 4, gy // 4)

    def device(x, y, z):
        return (x % 2 * 4 + y, z * 4 + x // 2 * 2 + core)

    def peer(axis, value):
        return device(*(value if i == axis else coord[i] for i in range(3)))

    sibling = (gx, gy + 1 - 2 * core)

    def there(d):
        x, y = gx + d[0], gy + d[1]
        return (x >= 0) & (x < 8) & (y >= 0) & (y < 16)

    def load(i, src, dst):
        return pltpu.make_async_copy(src, dst, in_sem.at[i])

    loads = [load(0, feat_hbm, feat), load(1, cot_hbm, cot), load(2, k1_hbm, w1), load(3, k2_hbm, w2)]
    for c in loads:
        c.start()

    def clear(g):
        for f in range(2):
            for e in (0, 17):
                g[f, e] = jnp.zeros((18, 8, C), BF16)
                g[f, pl.ds(1, 16), e] = jnp.zeros((16, 8, C), BF16)

    clear(land)
    barrier = pltpu.get_barrier_semaphore()
    for d in DIRS:
        @pl.when(there(d))
        def _():
            pl.semaphore_signal(barrier, inc=1, device_id=(gx + d[0], gy + d[1]), device_id_type=MESH)
    for axis in range(3):
        for k in (1, 2, 3):
            pl.semaphore_signal(barrier, inc=1, device_id=peer(axis, (coord[axis] + k) % 4), device_id_type=MESH)
    pl.semaphore_signal(barrier, inc=1, device_id=sibling, device_id_type=MESH)

    clear(grid1)
    clear(grid2)
    p0, p1 = pos_ref[0], pos_ref[1]
    where = [jnp.minimum(p0, POS - 1), jnp.minimum(p1, POS - 1)]
    bx = [w // 2 for w in where]
    by = [w % 2 for w in where]
    live = [(p0 < POS).astype(F32), (p1 < POS).astype(F32)]

    def place(grid, f, source):
        masks = [((p0 == p).astype(F32), (p1 == p).astype(F32)) for p in range(POS)]
        for x in range(8):
            rows = pl.ds(x * 64, 64)
            v0, v1 = source[0, rows].astype(F32), source[1, rows].astype(F32)
            for p, (m0, m1) in enumerate(masks):
                v = (v0 * m0 + v1 * m1).reshape(8, 8, C).astype(BF16)
                grid[f, 1 + p // 2 * 8 + x, pl.ds(1 + p % 2 * 8, 8)] = v

    def halo(phase, grid, landing):
        def copies(d):
            i = DIRS.index(d)
            return pltpu.make_async_remote_copy(
                src_ref=grid.at[:, span(d[0], 16, False), span(d[1], 16, False)],
                dst_ref=landing.at[:, span(-d[0], 16, True), span(-d[1], 16, True)],
                send_sem=hs.at[phase, i], recv_sem=hr.at[phase, i],
                device_id=(gx + d[0], gy + d[1]), device_id_type=MESH,
            )

        def start():
            for d in DIRS:
                @pl.when(there(d))
                def _():
                    copies(d).start()

        def arrive():
            for d in DIRS:
                @pl.when(there((-d[0], -d[1])))
                def _():
                    copies(d).wait_recv()

        def done():
            for d in DIRS:
                @pl.when(there(d))
                def _():
                    copies(d).wait_send()

        return start, arrive, done

    start1, arrive1, done1 = halo(0, grid1, land)
    start2, arrive2, done2 = halo(1, grid2, grid2)

    loads[0].wait()
    loads[1].wait()
    place(grid1, 0, feat)
    place(grid1, 1, cot)

    expected = 10
    for d in DIRS:
        expected = expected + there(d).astype(jnp.int32)
    pl.semaphore_wait(barrier, expected)
    start1()

    loads[2].wait()
    loads[3].wait()
    for t in range(27):
        r2[t // 9, :, pl.ds(t % 9 * C, C)] = w2[26 - t]
        r2y[t // 9, t % 9 // 3, :, pl.ds(t % 3 * C, C)] = w2[26 - t]

    z = lax.broadcasted_iota(jnp.int32, (10, 8, C), 1)
    first, last = z == 0, z == 7

    def sides(t):
        n = t.shape[0]
        return (jnp.where(first[:n], 0.0, pltpu.roll(t, 1, 1)), t, jnp.where(last[:n], 0.0, pltpu.roll(t, 7, 1)))

    def gather(a, s, grid, f, layers=None):
        def layer(x, carry):
            t = grid[f, bx[s] * 8 + x, pl.ds(by[s] * 8, 10)].astype(F32)
            for oz, v in enumerate(sides(t)):
                for oy in range(3):
                    a[s, x, :, pl.ds((oy * 3 + oz) * C, C)] = v[oy : oy + 8].reshape(64, C).astype(BF16)
            return carry

        if layers is None:
            lax.fori_loop(0, 10, layer, 0)
        else:
            for x in layers:
                layer(x, 0)

    def patch(a, s, grid, f):
        gather(a, s, grid, f, (0, 9))

        def layer(x, carry):
            for oy in (0, 2):
                t = grid[f, bx[s] * 8 + x, pl.ds(by[s] * 8 + oy * 4, 2)].astype(F32)
                for oz, v in enumerate(sides(t)):
                    a[s, x, pl.ds(oy * 24, 16), pl.ds((oy * 3 + oz) * C, C)] = v.reshape(16, C).astype(BF16)
            return carry

        lax.fori_loop(1, 9, layer, 0)

    def conv(a, s, w):
        total = None
        for ox in range(3):
            v = jnp.dot(a[s, pl.ds(ox, 8)].reshape(512, 9 * C), w[pl.ds(ox * 9, 9)].reshape(9 * C, C), preferred_element_type=F32)
            total = v if total is None else total + v
        return total

    def conv_t(a, s, r):
        total = None
        for ox in range(3):
            v = lax.dot_general(a[s, pl.ds(ox, 8)].reshape(512, 9 * C), r[ox], NT, preferred_element_type=F32)
            total = v if total is None else total + v
        return total

    def fix(a, s, f, total, weights, block):
        cx = weights(a[s, bx[s] * 9], bx[s] * 2)
        for i in (0, 1):
            edge = (bx[s] == i).astype(F32)
            total[i * 7] = total[i * 7] + (cx * edge).reshape(8, 8, C)
        t = grid1[f, pl.ds(bx[s] * 8, 10), by[s] * 17].astype(F32)
        layer = lax.broadcasted_iota(jnp.int32, (10, 8, C), 0)
        low, high = (bx[s] == 1).astype(F32), (bx[s] == 0).astype(F32)
        t = t * jnp.where(layer == 0, low, jnp.where(layer == 9, high, 1.0))
        shifted = sides(t)
        cy = None
        for ox in range(3):
            rows = jnp.concatenate([v[ox : ox + 8].reshape(64, C) for v in shifted], axis=1).astype(BF16)
            v = block(rows, ox, by[s] * 2)
            cy = v if cy is None else cy + v
        for i in (0, 1):
            edge = (by[s] == i).astype(F32)
            total[:, i * 7] = total[:, i * 7] + (cy * edge).reshape(8, 8, C)

    def fix_first(s):
        fix(ag, s, 0, pre_ref.at[s],
            lambda rows, ox: jnp.dot(rows, w1[pl.ds(ox * 9, 9)].reshape(9 * C, C), preferred_element_type=F32),
            lambda rows, ox, oy: jnp.dot(
                rows, w1[pl.ds(ox * 9 + oy * 3, 3)].reshape(3 * C, C), preferred_element_type=F32))

    def fix_second():
        fix(au, 0, 1, hg_ref,
            lambda rows, ox: lax.dot_general(rows, r2[ox], NT, preferred_element_type=F32),
            lambda rows, ox, oy: lax.dot_general(
                rows, r2y[ox, oy], NT, preferred_element_type=F32))

    for s in range(2):
        gather(ag, s, grid1, 0)
        pre_ref[s] = conv(ag, s, w1).reshape(8, 8, 8, C)
    gather(au, 0, grid1, 1)
    hg_ref[...] = conv_t(au, 0, r2).reshape(8, 8, 8, C)

    arrive1()
    for f in range(2):
        for e in (0, 17):
            grid1[f, e] = land[f, e]
            grid1[f, pl.ds(1, 16), e] = land[f, pl.ds(1, 16), e]
    gain = gain_ref[0:1, :]

    half = pl.multiple_of(core * 64, 64)
    other = pl.multiple_of((1 - core) * 64, 64)

    def core_copy(g, first=0, count=9):
        taps = pl.ds(g * 9 + first, count)
        return pltpu.make_async_remote_copy(
            src_ref=part.at[taps, pl.ds(other, 64)], dst_ref=rcore.at[taps],
            send_sem=cs.at[g], recv_sem=cr.at[g], device_id=sibling, device_id_type=MESH)

    def group(g, a, lhs):
        ox = 2 - g if g < 3 else g - 3
        v = (jnp.dot(lhs[0], a[0, pl.ds(ox, 8)].reshape(512, 9 * C), preferred_element_type=F32)
             + jnp.dot(lhs[1], a[1, pl.ds(ox, 8)].reshape(512, 9 * C), preferred_element_type=F32))
        for k in range(9):
            if g < 3:
                part[g * 9 + 8 - k] = v[:, k * C : (k + 1) * C]
            else:
                part[g * 9 + k] = v[:, k * C : (k + 1) * C].T
            if k % 3 == 2:
                core_copy(g, 8 - k if g < 3 else k - 2, 3).start()

    def axes(g):
        return ORDERS[g % 3]

    def remote(src, dst, send_sem, recv_sem, to):
        return pltpu.make_async_remote_copy(
            src_ref=src, dst_ref=dst, send_sem=send_sem, recv_sem=recv_sem, device_id=to, device_id_type=MESH)

    def local(ref, send_sem, recv_sem):
        return remote(ref, ref, send_sem, recv_sem, sibling)

    def three(axis, copy):
        for k in (1, 2, 3):
            to = (coord[axis] + k) % 4
            copy(k - 1, to, peer(axis, to)).start()

    def all_a(g):
        return local(ra.at[g], a_s.at[g], a_r.at[g])

    def all_b(g):
        return local(rb.at[g], b_s.at[g], b_r.at[g])

    def all_c(g):
        return local(rc.at[g, pl.ds(0, 3)], c_s.at[g], c_r.at[g])

    def all_eb(g):
        return local(full_ref.at[g, 0, 0, pl.ds(0, 15)], eb_s.at[g], eb_r.at[g])

    def all_ea(g):
        return local(full_ref.at[g, 0, pl.ds(0, 3)], ea_s.at[g], ea_r.at[g])

    def scatter(g):
        core_copy(g).wait_recv()

        def tap(k, carry):
            v = part[g * 9 + k, pl.ds(half, 64)] + rcore[g * 9 + k]
            rcore[g * 9 + k] = v
            sa[g, k] = v.reshape(4, 16, C).astype(BF16)
            return carry

        lax.fori_loop(0, 9, tap, 0)
        three(axes(g)[0], lambda k, to, d: remote(
            sa.at[g, :, to], ra.at[g, k], a_s.at[g], a_r.at[g], d))

    def reduce_a(g):
        all_a(g).wait_recv()
        a, b, _ = axes(g)
        v = rcore[pl.ds(g * 9, 9), pl.ds(pl.multiple_of(coord[a] * 16, 16), 16)]
        for k in range(3):
            v = v + ra[g, k].astype(F32)
        sb[g, pl.ds(0, 18)] = v.reshape(18, 8, C)
        three(b, lambda k, to, d: remote(
            sb.at[g, pl.ds(to * 5, 5)], rb.at[g, k], b_s.at[g], b_r.at[g], d))

    def reduce_b(g):
        all_b(g).wait_recv()
        _, b, c = axes(g)
        v = sb[g, pl.ds(coord[b] * 5, 5)]
        for k in range(3):
            v = v + rb[g, k]
        rc[g, coord[c]] = v
        mine = rc.at[g, coord[c]]
        three(c, lambda k, to, d: remote(mine, mine, c_s.at[g], c_r.at[g], d))

    def reduce_c(g):
        all_c(g).wait_recv()
        a, b, _ = axes(g)
        v = ((rc[g, 0] + rc[g, 1]) + rc[g, 2]) + rc[g, 3]
        full_ref[g, core, coord[a], pl.ds(coord[b] * 5, 5)] = v.astype(BF16)
        mine = full_ref.at[g, core, coord[a], pl.ds(coord[b] * 5, 5)]
        three(b, lambda k, to, d: remote(mine, mine, eb_s.at[g], eb_r.at[g], d))

    def spread(g):
        all_eb(g).wait_recv()
        a = axes(g)[0]
        mine = full_ref.at[g, core, coord[a]]
        three(a, lambda k, to, d: remote(mine, mine, ea_s.at[g], ea_r.at[g], d))

    def sib_copy(g):
        ref = full_ref.at[g, core]
        return remote(ref, ref, sib_s.at[g], sib_r.at[g], sibling)

    def squares(g, h):
        acc = None
        for a in range(4):
            v = full_ref[g, h, a, pl.ds(0, 18)].astype(F32)
            v = jnp.sum(v * v, axis=0)
            acc = v if acc is None else acc + v
        return acc

    def pass_on(g):
        all_ea(g).wait_recv()
        sib_copy(g).start()

    def close(groups):
        for g in groups:
            pass_on(g)
        own = [squares(g, core) for g in groups]
        acc = jnp.zeros((8, C), F32)
        for g, mine in zip(groups, own):
            sib_copy(g).wait_recv()
            acc = acc + (mine + squares(g, 1 - core))
        return acc

    def gain_copy(stage, k):
        if stage == 0:
            return pltpu.make_async_remote_copy(
                src_ref=gains.at[0, 0], dst_ref=gains.at[0, 1], send_sem=gs.at[0], recv_sem=gr.at[0],
                device_id=sibling, device_id_type=MESH)
        axis = stage - 1
        i = 1 + axis * 3 + k - 1
        return pltpu.make_async_remote_copy(
            src_ref=gains.at[stage, coord[axis]], dst_ref=gains.at[stage, coord[axis]],
            send_sem=gs.at[i], recv_sem=gr.at[i],
            device_id=peer(axis, (coord[axis] + k) % 4), device_id_type=MESH)

    def gain_step(stage):
        if stage == 0:
            gain_copy(0, 0).wait_recv()
            gains[1, coord[0]] = gains[0, 0] + gains[0, 1]
        else:
            for k in (1, 2, 3):
                gain_copy(stage, k).wait_recv()
            v = ((gains[stage, 0] + gains[stage, 1]) + gains[stage, 2]) + gains[stage, 3]
            if stage == 3:
                return v
            gains[stage + 1, coord[stage]] = v
        for k in (1, 2, 3):
            gain_copy(stage + 1, k).start()

    def second_half(s, f):
        if f == 0:
            gather(ah, s, grid2, 0)
            v = conv(ah, s, w2) * live[s] + feat[s].astype(F32) * live[s]
        else:
            gather(ap, s, grid2, 1)
            v = (conv_t(ap, s, r1) + cot[s].astype(F32)) * live[s]
        outv[f, s] = v.astype(BF16)

    def forward(s):
        patch(ag, s, grid1, 0)
        fix_first(s)
        pre = pre_ref[s].reshape(512, C)
        center = pre - jnp.mean(pre, axis=-1, keepdims=True)
        inv = lax.rsqrt(jnp.mean(center * center, axis=-1, keepdims=True) + 1e-05)
        unit = center * inv
        normed = unit * gain
        sig = jax.nn.sigmoid(normed)
        hidden = normed * sig * live[s]
        hid[s] = hidden.astype(BF16)
        units[s] = unit
        invs[s] = jnp.broadcast_to(inv, (512, C))
        return hidden.T.astype(BF16)

    def backward(s):
        if s == 0:
            fix_second()
            hgrad = hg_ref[...].reshape(512, C) * live[s]
        else:
            hgrad = conv_t(au, s, r2) * live[s]
        unit, inv = units[s], invs[s]
        normed = unit * gain
        sig = jax.nn.sigmoid(normed)
        dn = hgrad * (sig * (1.0 + normed * (1.0 - sig)))
        du = dn * gain
        dc = inv * (du - unit * jnp.mean(du * unit, axis=-1, keepdims=True))
        pg = (dc - jnp.mean(dc, axis=-1, keepdims=True)) * live[s]
        pgr[s] = pg.astype(BF16)
        return pg.T.astype(BF16), jnp.sum(dn * unit, axis=0, keepdims=True)

    for g in range(6):
        sb[g, pl.ds(18, 2)] = jnp.zeros((2, 8, C), F32)
    hid_t = [forward(0), forward(1)]
    patch(au, 0, grid1, 1)
    gather(au, 1, grid1, 1)
    early, late = (0, 1, 2), (3, 4, 5)
    for g in early:
        group(g, au, hid_t)
    pg0, gg0 = backward(0)
    for g in early:
        scatter(g)
    pg1, gg1 = backward(1)
    gains[0, 0] = jnp.broadcast_to(gg0 + gg1, (8, C))
    gain_copy(0, 0).start()
    for g in late:
        group(g, ag, [pg0, pg1])
    place(grid2, 0, hid)
    for g in late:
        scatter(g)
    place(grid2, 1, pgr)
    start2()
    gain_step(0)
    for t in range(27):
        r1[t // 9, :, pl.ds(t % 9 * C, C)] = w1[26 - t]
    for g in early + late:
        reduce_a(g)
    gain_step(1)
    arrive2()
    second_half(0, 0)
    for g in early + late:
        reduce_b(g)
    gain_step(2)
    second_half(1, 0)
    for g in early + late:
        reduce_c(g)
    second_half(0, 1)
    for g in early + late:
        spread(g)
    gain_sum = gain_step(3)
    second_half(1, 1)
    acc = close(early)

    acc = acc + close(late)
    total = jnp.sum(acc) + jnp.sum(gain_sum[0:1] * gain_sum[0:1])
    entries = 54.0 * C * C + C
    mean = jnp.full((8, C), total / entries + 1e-06, F32)
    shrink = jnp.minimum(1.0, CLIP / jnp.sqrt(mean))
    stats_ref[0] = shrink
    stats_ref[1] = shrink * gain_sum

    done1()
    done2()
    for g in range(6):
        core_copy(g).wait_send()
        sib_copy(g).wait_send()
        for sent in (all_a, all_b, all_c, all_eb, all_ea):
            sent(g).wait_send()
    gain_copy(0, 0).wait_send()
    for k in (1, 2, 3):
        for stage in (1, 2, 3):
            gain_copy(stage, k).wait_send()


def finish_kernel(outv, full_ref, stats_ref, out_hbm, fgrad_hbm, update_hbm, gain_ref, scaled, sem):
    copies = [pltpu.make_async_copy(outv.at[0], out_hbm, sem.at[18]),
              pltpu.make_async_copy(outv.at[1], fgrad_hbm, sem.at[19])]
    for c in copies:
        c.start()
    shrink = stats_ref[0, 0:1, :]
    for g in range(6):
        for k in range(9):
            for h in range(2):
                v = full_ref[g, h, :, pl.ds(k * 2, 2)].astype(F32).reshape(64, C)
                scaled[g, k, pl.ds(h * 64, 64)] = v * shrink
            if k % 3 == 2:
                c = pltpu.make_async_copy(
                    scaled.at[g, pl.ds(k - 2, 3)], update_hbm.at[1 - g // 3, pl.ds(g % 3 * 9 + k - 2, 3)],
                    sem.at[g * 3 + k // 3])
                c.start()
                copies.append(c)
    gain_ref[...] = stats_ref[1, 0:1, :]
    for c in copies:
        c.wait()


def per_device(features, brick_pos, cotangent, first_kernel, second_kernel, norm_gain):
    hbm = pl.BlockSpec(memory_space=pltpu.HBM)
    vmem = pl.BlockSpec(memory_space=pltpu.VMEM)
    dma = pltpu.SemaphoreType.DMA
    V = pltpu.VMEM
    tile = (2, 10, 64, 9 * C)
    outv, full, stats = pl.pallas_call(
        step_kernel,
        out_shape=(V((2, 2, 512, C), BF16), V((6, 2, 4, 20, 8, C), BF16), V((2, 8, C), F32)),
        in_specs=[pl.BlockSpec(memory_space=pltpu.SMEM), vmem, hbm, hbm, hbm, hbm],
        out_specs=(vmem, vmem, vmem),
        scratch_shapes=[
            V((2, 512, C), BF16), V((2, 512, C), BF16),
            V((27, C, C), BF16), V((27, C, C), BF16),
            V((3, C, 9 * C), BF16), V((3, C, 9 * C), BF16), V((3, 3, C, 3 * C), BF16),
            V((2, 18, 18, 8, C), BF16), V((2, 18, 18, 8, C), BF16), V((2, 18, 18, 8, C), BF16),
            V(tile, BF16), V(tile, BF16), V(tile, BF16), V(tile, BF16),
            V((2, 8, 8, 8, C), F32), V((8, 8, 8, C), F32),
            V((2, 512, C), BF16), V((2, 512, C), BF16),
            V((54, C, C), F32), V((54, 64, C), F32),
            V((6, 9, 4, 16, C), BF16), V((6, 3, 9, 16, C), BF16),
            V((6, 20, 8, C), F32), V((6, 3, 5, 8, C), F32), V((6, 4, 5, 8, C), F32),
            V((4, 4, 8, C), F32),
            V((2, 512, C), F32), V((2, 512, C), F32),
            dma((4,)), dma((2, 8)), dma((2, 8)), dma((6,)), dma((6,)),
            dma((6,)), dma((6,)), dma((6,)), dma((6,)), dma((6,)), dma((6,)),
            dma((6,)), dma((6,)), dma((6,)), dma((6,)),
            dma((6,)), dma((6,)), dma((10,)), dma((10,)),
        ],
        compiler_params=pltpu.CompilerParams(
            collective_id=0, has_side_effects=True, vmem_limit_bytes=56 * 2**20
        ),
        name="step",
    )(brick_pos, norm_gain.reshape(1, C), features, cotangent, first_kernel, second_kernel)
    out, fgrad, update, gain = pl.pallas_call(
        finish_kernel,
        out_shape=(
            jax.ShapeDtypeStruct((2, 512, C), BF16),
            jax.ShapeDtypeStruct((2, 512, C), BF16),
            jax.ShapeDtypeStruct((2, 27, C, C), F32),
            jax.ShapeDtypeStruct((1, C), F32),
        ),
        in_specs=[vmem, vmem, vmem],
        out_specs=(hbm, hbm, hbm, vmem),
        scratch_shapes=[V((6, 9, C, C), F32), dma((20,))],
        compiler_params=pltpu.CompilerParams(vmem_limit_bytes=10 * 2**20),
        name="finish",
    )(outv, full, stats)
    return out, fgrad, update, gain.reshape(C)


def solution(mesh):
    rows = P(("gx", "gy"), None, None)
    return jax.shard_map(
        per_device, mesh=mesh, in_specs=(rows, P(("gx", "gy")), rows, P(), P(), P()),
        out_specs=(rows, rows, P(), P()), check_vma=False,
    )
```

```python
import jax
import jax.numpy as jnp
from jax import lax
from jax.experimental import pallas as pl
from jax.experimental.pallas import tpu as pltpu
from jax.sharding import PartitionSpec as P

MESH = pl.DeviceIdType.MESH
F32 = jnp.float32
BF16 = jnp.bfloat16
CLIP = 0.5
C = 128
POS = 4
DIRS = [(dx, dy) for dx in (-1, 0, 1) for dy in (-1, 0, 1) if (dx, dy) != (0, 0)]
ORDERS = [(0, 1, 2), (1, 2, 0), (2, 0, 1)]
NT = (((1,), (1,)), ((), ()))


def span(d, size, halo):
    if d == 0:
        return pl.ds(1, 16)
    if d < 0:
        return pl.ds(0 if halo else 1, 1)
    return pl.ds(17 if halo else 16, 1)


def step_kernel(
    pos_ref, gain_ref, feat_hbm, cot_hbm, k1_hbm, k2_hbm,
    outv, full_ref, stats_ref,
    feat, cot, w1, w2, r1, r2, grid1, land, grid2, ag, au, ah, ap, pre_ref, hid_t, pgr_t,
    hid, pgr, part, rcore, sa, ra, sb, rb, rc, gains, sums, units, invs,
    in_sem, hs, hr, cs, cr, a_s, a_r, b_s, b_r, c_s, c_r, eb_s, eb_r, ea_s, ea_r, sib_s, sib_r, sums_s, sums_r, gs, gr,
):
    gx = lax.axis_index("gx")
    gy = lax.axis_index("gy")
    core = gy % 2
    coord = ((gy // 2) % 2 * 2 + gx // 4, gx % 4, gy // 4)

    def device(x, y, z):
        return (x % 2 * 4 + y, z * 4 + x // 2 * 2 + core)

    def peer(axis, value):
        return device(*(value if i == axis else coord[i] for i in range(3)))

    sibling = (gx, gy + 1 - 2 * core)

    def there(d):
        x, y = gx + d[0], gy + d[1]
        return (x >= 0) & (x < 8) & (y >= 0) & (y < 16)

    def load(i, src, dst):
        return pltpu.make_async_copy(src, dst, in_sem.at[i])

    loads = [load(0, feat_hbm, feat), load(1, cot_hbm, cot), load(2, k1_hbm, w1), load(3, k2_hbm, w2)]
    for c in loads:
        c.start()

    def clear(g):
        for f in range(2):
            for e in (0, 17):
                g[f, e] = jnp.zeros((18, 8, C), BF16)
                g[f, pl.ds(1, 16), e] = jnp.zeros((16, 8, C), BF16)

    clear(land)
    barrier = pltpu.get_barrier_semaphore()
    for d in DIRS:
        @pl.when(there(d))
        def _():
            pl.semaphore_signal(barrier, inc=1, device_id=(gx + d[0], gy + d[1]), device_id_type=MESH)
    for axis in range(3):
        for k in (1, 2, 3):
            pl.semaphore_signal(barrier, inc=1, device_id=peer(axis, (coord[axis] + k) % 4), device_id_type=MESH)
    pl.semaphore_signal(barrier, inc=1, device_id=sibling, device_id_type=MESH)

    clear(grid1)
    clear(grid2)
    p0, p1 = pos_ref[0], pos_ref[1]
    where = [jnp.minimum(p0, POS - 1), jnp.minimum(p1, POS - 1)]

    def pick(pair, s):
        return pair[s] if isinstance(s, int) else jnp.where(s == 0, pair[0], pair[1])

    def bx(s):
        return pick(where, s) // 2

    def by(s):
        return pick(where, s) % 2

    live = [(p0 < POS).astype(F32), (p1 < POS).astype(F32)]

    def place(grid, f, source):
        masks = [((p0 == p).astype(F32), (p1 == p).astype(F32)) for p in range(POS)]
        for x in range(8):
            rows = pl.ds(x * 64, 64)
            v0, v1 = source[0, rows].astype(F32), source[1, rows].astype(F32)
            for p, (m0, m1) in enumerate(masks):
                v = (v0 * m0 + v1 * m1).reshape(8, 8, C).astype(BF16)
                grid[f, 1 + p // 2 * 8 + x, pl.ds(1 + p % 2 * 8, 8)] = v

    def halo(phase, grid, landing):
        def copies(d):
            i = DIRS.index(d)
            return pltpu.make_async_remote_copy(
                src_ref=grid.at[:, span(d[0], 16, False), span(d[1], 16, False)],
                dst_ref=landing.at[:, span(-d[0], 16, True), span(-d[1], 16, True)],
                send_sem=hs.at[phase, i], recv_sem=hr.at[phase, i],
                device_id=(gx + d[0], gy + d[1]), device_id_type=MESH,
            )

        def start():
            for d in DIRS:
                @pl.when(there(d))
                def _():
                    copies(d).start()

        def arrive():
            for d in DIRS:
                @pl.when(there((-d[0], -d[1])))
                def _():
                    copies(d).wait_recv()

        def done():
            for d in DIRS:
                @pl.when(there(d))
                def _():
                    copies(d).wait_send()

        return start, arrive, done

    start1, arrive1, done1 = halo(0, grid1, land)
    start2, arrive2, done2 = halo(1, grid2, grid2)

    loads[0].wait()
    loads[1].wait()
    place(grid1, 0, feat)
    place(grid1, 1, cot)

    expected = 10
    for d in DIRS:
        expected = expected + there(d).astype(jnp.int32)
    pl.semaphore_wait(barrier, expected)
    start1()

    loads[2].wait()
    loads[3].wait()
    for t in range(27):
        r2[t // 9, :, pl.ds(t % 9 * C, C)] = w2[26 - t]

    z = lax.broadcasted_iota(jnp.int32, (10, 8, C), 1)
    first, last = z == 0, z == 7

    def sides(t):
        n = t.shape[0]
        return (jnp.where(first[:n], 0.0, pltpu.roll(t, 1, 1)), t, jnp.where(last[:n], 0.0, pltpu.roll(t, 7, 1)))

    def gather(a, s, grid, f, layers=None):
        def layer(x, carry):
            t = grid[f, bx(s) * 8 + x, pl.ds(by(s) * 8, 10)].astype(F32)
            for oz, v in enumerate(sides(t)):
                for oy in range(3):
                    a[s, x, :, pl.ds((oy * 3 + oz) * C, C)] = v[oy : oy + 8].reshape(64, C).astype(BF16)
            return carry

        if layers is None:
            lax.fori_loop(0, 10, layer, 0)
        else:
            for x in layers:
                layer(x, 0)

    def patch(a, s, grid, f):
        gather(a, s, grid, f, (0, 9))

        def layer(x, carry):
            for oy in (0, 2):
                t = grid[f, bx(s) * 8 + x, pl.ds(by(s) * 8 + oy * 4, 2)].astype(F32)
                for oz, v in enumerate(sides(t)):
                    a[s, x, pl.ds(oy * 24, 16), pl.ds((oy * 3 + oz) * C, C)] = v.reshape(16, C).astype(BF16)
            return carry

        lax.fori_loop(1, 9, layer, 0)

    def conv(a, s, w):
        total = None
        for ox in range(3):
            v = jnp.dot(a[s, pl.ds(ox, 8)].reshape(512, 9 * C), w[pl.ds(ox * 9, 9)].reshape(9 * C, C), preferred_element_type=F32)
            total = v if total is None else total + v
        return total

    def conv_t(a, s, r):
        total = None
        for ox in range(3):
            v = lax.dot_general(a[s, pl.ds(ox, 8)].reshape(512, 9 * C), r[ox], NT, preferred_element_type=F32)
            total = v if total is None else total + v
        return total

    def fix(a, s, f, total, weights, block):
        cx = weights(a[s, bx(s) * 9], bx(s) * 2)
        for i in (0, 1):
            edge = (bx(s) == i).astype(F32)
            total[i * 7] = total[i * 7] + (cx * edge).reshape(8, 8, C)
        t = grid1[f, pl.ds(bx(s) * 8, 10), by(s) * 17].astype(F32)
        layer = lax.broadcasted_iota(jnp.int32, (10, 8, C), 0)
        low, high = (bx(s) == 1).astype(F32), (bx(s) == 0).astype(F32)
        t = t * jnp.where(layer == 0, low, jnp.where(layer == 9, high, 1.0))
        shifted = sides(t)
        cy = None
        for ox in range(3):
            rows = jnp.concatenate([v[ox : ox + 8].reshape(64, C) for v in shifted], axis=1).astype(BF16)
            v = block(rows, ox, by(s) * 2)
            cy = v if cy is None else cy + v
        for i in (0, 1):
            edge = (by(s) == i).astype(F32)
            total[:, i * 7] = total[:, i * 7] + (cy * edge).reshape(8, 8, C)

    def fix_first(s):
        fix(ag, s, 0, pre_ref.at[s],
            lambda rows, ox: jnp.dot(rows, w1[pl.ds(ox * 9, 9)].reshape(9 * C, C), preferred_element_type=F32),
            lambda rows, ox, oy: jnp.dot(
                rows, w1[pl.ds(ox * 9 + oy * 3, 3)].reshape(3 * C, C), preferred_element_type=F32))

    def first_local(s, carry):
        gather(ag, s, grid1, 0)
        pre_ref[s] = conv(ag, s, w1).reshape(8, 8, 8, C)
        gather(au, s, grid1, 1)
        return carry

    lax.fori_loop(0, 2, first_local, 0)
    arrive1()
    for f in range(2):
        for e in (0, 17):
            grid1[f, e] = land[f, e]
            grid1[f, pl.ds(1, 16), e] = land[f, pl.ds(1, 16), e]
    gain = gain_ref[0:1, :]

    half = pl.multiple_of(core * 64, 64)
    other = pl.multiple_of((1 - core) * 64, 64)

    def core_copy(g, first=0, count=9):
        taps = pl.ds(g * 9 + first, count)
        return pltpu.make_async_remote_copy(
            src_ref=part.at[taps, pl.ds(other, 64)], dst_ref=rcore.at[taps],
            send_sem=cs.at[g], recv_sem=cr.at[g], device_id=sibling, device_id_type=MESH)

    def group(g, flip, a, lhs):
        ox = 2 - g if flip else g - 3
        v = (jnp.dot(lhs[0], a[0, pl.ds(ox, 8)].reshape(512, 9 * C), preferred_element_type=F32)
             + jnp.dot(lhs[1], a[1, pl.ds(ox, 8)].reshape(512, 9 * C), preferred_element_type=F32))
        for k in range(9):
            if flip:
                part[g * 9 + 8 - k] = v[:, k * C : (k + 1) * C]
            else:
                part[g * 9 + k] = v[:, k * C : (k + 1) * C].T
            if k % 3 == 2:
                core_copy(g, 8 - k if flip else k - 2, 3).start()

    def axes(g):
        return ORDERS[g % 3]

    def remote(src, dst, send_sem, recv_sem, to):
        return pltpu.make_async_remote_copy(
            src_ref=src, dst_ref=dst, send_sem=send_sem, recv_sem=recv_sem, device_id=to, device_id_type=MESH)

    def local(ref, send_sem, recv_sem):
        return remote(ref, ref, send_sem, recv_sem, sibling)

    def three(axis, copy):
        for k in (2, 1, 3):
            to = (coord[axis] + k) % 4
            copy(k - 1, to, peer(axis, to)).start()

    def all_a(g):
        return local(ra.at[g], a_s.at[g], a_r.at[g])

    def all_b(g):
        return local(rb.at[g], b_s.at[g], b_r.at[g])

    def all_c(g):
        return local(rc.at[g, pl.ds(0, 3)], c_s.at[g], c_r.at[g])

    def all_eb(g):
        return local(full_ref.at[g, 0, 0, pl.ds(0, 15)], eb_s.at[g], eb_r.at[g])

    def all_ea(g):
        return local(full_ref.at[g, 0, pl.ds(0, 3)], ea_s.at[g], ea_r.at[g])

    def scatter(g):
        core_copy(g).wait_recv()

        def tap(k, carry):
            v = part[g * 9 + k, pl.ds(half, 64)] + rcore[g * 9 + k]
            rcore[g * 9 + k] = v
            sa[g, k] = v.reshape(4, 16, C).astype(BF16)
            return carry

        lax.fori_loop(0, 9, tap, 0)
        three(axes(g)[0], lambda k, to, d: remote(
            sa.at[g, :, to], ra.at[g, k], a_s.at[g], a_r.at[g], d))

    def reduce_a(g):
        all_a(g).wait_recv()
        a, b, _ = axes(g)
        v = rcore[pl.ds(g * 9, 9), pl.ds(pl.multiple_of(coord[a] * 16, 16), 16)]
        for k in range(3):
            v = v + ra[g, k].astype(F32)
        sb[g, pl.ds(0, 18)] = v.reshape(18, 8, C)
        three(b, lambda k, to, d: remote(
            sb.at[g, pl.ds(to * 5, 5)], rb.at[g, k], b_s.at[g], b_r.at[g], d))

    def reduce_b(g):
        all_b(g).wait_recv()
        _, b, c = axes(g)
        v = sb[g, pl.ds(coord[b] * 5, 5)]
        for k in range(3):
            v = v + rb[g, k]
        rc[g, coord[c]] = v
        mine = rc.at[g, coord[c]]
        three(c, lambda k, to, d: remote(mine, mine, c_s.at[g], c_r.at[g], d))

    def reduce_c(g):
        all_c(g).wait_recv()
        a, b, _ = axes(g)
        v = ((rc[g, 0] + rc[g, 1]) + rc[g, 2]) + rc[g, 3]
        full_ref[g, core, coord[a], pl.ds(coord[b] * 5, 5)] = v.astype(BF16)
        mine = full_ref.at[g, core, coord[a], pl.ds(coord[b] * 5, 5)]
        three(b, lambda k, to, d: remote(mine, mine, eb_s.at[g], eb_r.at[g], d))

    def spread(g):
        all_eb(g).wait_recv()
        a = axes(g)[0]
        mine = full_ref.at[g, core, coord[a]]
        three(a, lambda k, to, d: remote(mine, mine, ea_s.at[g], ea_r.at[g], d))

    def sib_copy(g):
        ref = full_ref.at[g, core]
        return remote(ref, ref, sib_s.at[g], sib_r.at[g], sibling)

    def squares(g, h):
        acc = None
        for a in range(4):
            v = full_ref[g, h, a, pl.ds(0, 18)].astype(F32)
            v = jnp.sum(v * v, axis=0)
            acc = v if acc is None else acc + v
        return acc

    def pass_on(g):
        all_ea(g).wait_recv()
        sib_copy(g).start()

    def close(groups, acc):
        for g in groups:
            pass_on(g)
        for g in groups:
            acc = acc + squares(g, core)
        return acc

    sums_copy = remote(sums.at[0], sums.at[1], sums_s.at[0], sums_r.at[0], sibling)

    def gain_copy(stage, k):
        if stage == 0:
            return pltpu.make_async_remote_copy(
                src_ref=gains.at[0, 0], dst_ref=gains.at[0, 1], send_sem=gs.at[0], recv_sem=gr.at[0],
                device_id=sibling, device_id_type=MESH)
        axis = stage - 1
        i = 1 + axis * 3 + k - 1
        return pltpu.make_async_remote_copy(
            src_ref=gains.at[stage, coord[axis]], dst_ref=gains.at[stage, coord[axis]],
            send_sem=gs.at[i], recv_sem=gr.at[i],
            device_id=peer(axis, (coord[axis] + k) % 4), device_id_type=MESH)

    def gain_step(stage):
        if stage == 0:
            gain_copy(0, 0).wait_recv()
            gains[1, coord[0]] = gains[0, 0] + gains[0, 1]
        else:
            for k in (1, 2, 3):
                gain_copy(stage, k).wait_recv()
            v = ((gains[stage, 0] + gains[stage, 1]) + gains[stage, 2]) + gains[stage, 3]
            if stage == 3:
                return v
            gains[stage + 1, coord[stage]] = v
        for k in (1, 2, 3):
            gain_copy(stage + 1, k).start()

    def outputs(s, carry):
        gather(ah, s, grid2, 0)
        v = conv(ah, s, w2) * pick(live, s) + feat[s].astype(F32) * pick(live, s)
        outv[0, s] = v.astype(BF16)
        return carry

    def feature_grads(s, carry):
        gather(ap, s, grid2, 1)
        v = (conv_t(ap, s, r1) + cot[s].astype(F32)) * pick(live, s)
        outv[1, s] = v.astype(BF16)
        return carry

    def forward(s, carry):
        patch(ag, s, grid1, 0)
        fix_first(s)
        pre = pre_ref[s].reshape(512, C)
        center = pre - jnp.mean(pre, axis=-1, keepdims=True)
        inv = lax.rsqrt(jnp.mean(center * center, axis=-1, keepdims=True) + 1e-05)
        unit = center * inv
        normed = unit * gain
        hidden = normed * jax.nn.sigmoid(normed) * pick(live, s)
        hid[s] = hidden.astype(BF16)
        units[s] = unit
        invs[s] = jnp.broadcast_to(inv, (512, C))
        hid_t[s] = hidden.T.astype(BF16)
        patch(au, s, grid1, 1)
        return carry

    def backward(s, total):
        hgrad = conv_t(au, s, r2) * pick(live, s)
        unit, inv = units[s], invs[s]
        normed = unit * gain
        sig = jax.nn.sigmoid(normed)
        dn = hgrad * (sig * (1.0 + normed * (1.0 - sig)))
        du = dn * gain
        dc = inv * (du - unit * jnp.mean(du * unit, axis=-1, keepdims=True))
        pg = (dc - jnp.mean(dc, axis=-1, keepdims=True)) * pick(live, s)
        pgr[s] = pg.astype(BF16)
        pgr_t[s] = pg.T.astype(BF16)
        return total + jnp.sum(dn * unit, axis=0, keepdims=True)

    for g in range(6):
        sb[g, pl.ds(18, 2)] = jnp.zeros((2, 8, C), F32)
    lax.fori_loop(0, 2, forward, 0)
    early, late = (0, 1, 2), (3, 4, 5)

    def early_group(g, carry):
        group(g, True, au, hid_t)
        return carry

    def late_group(g, carry):
        group(g, False, ag, pgr_t)
        return carry

    lax.fori_loop(0, 3, early_group, 0)
    gsum = lax.fori_loop(0, 2, backward, jnp.zeros((1, C), F32))
    for g in early:
        scatter(g)
    gains[0, 0] = jnp.broadcast_to(gsum, (8, C))
    gain_copy(0, 0).start()
    lax.fori_loop(3, 6, late_group, 0)
    place(grid2, 0, hid)
    place(grid2, 1, pgr)
    start2()
    for g in late:
        scatter(g)
    gain_step(0)
    for t in range(27):
        r1[t // 9, :, pl.ds(t % 9 * C, C)] = w1[26 - t]
    for g in early:
        reduce_a(g)
    arrive2()
    for g in late:
        reduce_a(g)
    gain_step(1)
    for g in early + late:
        reduce_b(g)
    lax.fori_loop(0, 2, outputs, 0)
    gain_step(2)
    for g in early + late:
        reduce_c(g)
    lax.fori_loop(0, 2, feature_grads, 0)
    for g in early:
        spread(g)
    for g in late:
        spread(g)
    gain_sum = gain_step(3)
    acc = close(early, jnp.zeros((8, C), F32))
    acc = close(late, acc)
    sums[0] = acc
    sums_copy.start()
    for g in early + late:
        sib_copy(g).wait_recv()
    sums_copy.wait_recv()
    acc = acc + sums[1]
    total = jnp.sum(acc) + jnp.sum(gain_sum[0:1] * gain_sum[0:1])
    entries = 54.0 * C * C + C
    mean = jnp.full((8, C), total / entries + 1e-06, F32)
    shrink = jnp.minimum(1.0, CLIP / jnp.sqrt(mean))
    stats_ref[0] = shrink
    stats_ref[1] = shrink * gain_sum

    done1()
    done2()
    for g in range(6):
        core_copy(g).wait_send()
        sib_copy(g).wait_send()
        for sent in (all_a, all_b, all_c, all_eb, all_ea):
            sent(g).wait_send()
    gain_copy(0, 0).wait_send()
    sums_copy.wait_send()
    for k in (1, 2, 3):
        for stage in (1, 2, 3):
            gain_copy(stage, k).wait_send()


def finish_kernel(outv, full_ref, stats_ref, out_hbm, fgrad_hbm, update_hbm, gain_ref, scaled, sem):
    copies = [pltpu.make_async_copy(outv.at[0], out_hbm, sem.at[18]),
              pltpu.make_async_copy(outv.at[1], fgrad_hbm, sem.at[19])]
    for c in copies:
        c.start()
    shrink = stats_ref[0, 0:1, :]
    for g in range(6):
        for k in range(9):
            for h in range(2):
                v = full_ref[g, h, :, pl.ds(k * 2, 2)].astype(F32).reshape(64, C)
                scaled[g, k, pl.ds(h * 64, 64)] = v * shrink
            if k % 3 == 2:
                c = pltpu.make_async_copy(
                    scaled.at[g, pl.ds(k - 2, 3)], update_hbm.at[1 - g // 3, pl.ds(g % 3 * 9 + k - 2, 3)],
                    sem.at[g * 3 + k // 3])
                c.start()
                copies.append(c)
    gain_ref[...] = stats_ref[1, 0:1, :]
    for c in copies:
        c.wait()


def per_device(features, brick_pos, cotangent, first_kernel, second_kernel, norm_gain):
    hbm = pl.BlockSpec(memory_space=pltpu.HBM)
    vmem = pl.BlockSpec(memory_space=pltpu.VMEM)
    dma = pltpu.SemaphoreType.DMA
    V = pltpu.VMEM
    tile = (2, 10, 64, 9 * C)
    outv, full, stats = pl.pallas_call(
        step_kernel,
        out_shape=(V((2, 2, 512, C), BF16), V((6, 2, 4, 20, 8, C), BF16), V((2, 8, C), F32)),
        in_specs=[pl.BlockSpec(memory_space=pltpu.SMEM), vmem, hbm, hbm, hbm, hbm],
        out_specs=(vmem, vmem, vmem),
        scratch_shapes=[
            V((2, 512, C), BF16), V((2, 512, C), BF16),
            V((27, C, C), BF16), V((27, C, C), BF16),
            V((3, C, 9 * C), BF16), V((3, C, 9 * C), BF16),
            V((2, 18, 18, 8, C), BF16), V((2, 18, 18, 8, C), BF16), V((2, 18, 18, 8, C), BF16),
            V(tile, BF16), V(tile, BF16), V(tile, BF16), V(tile, BF16),
            V((2, 8, 8, 8, C), F32), V((2, C, 512), BF16), V((2, C, 512), BF16),
            V((2, 512, C), BF16), V((2, 512, C), BF16),
            V((54, C, C), F32), V((54, 64, C), F32),
            V((6, 9, 4, 16, C), BF16), V((6, 3, 9, 16, C), BF16),
            V((6, 20, 8, C), F32), V((6, 3, 5, 8, C), F32), V((6, 4, 5, 8, C), F32),
            V((4, 4, 8, C), F32), V((2, 8, C), F32),
            V((2, 512, C), F32), V((2, 512, C), F32),
            dma((4,)), dma((2, 8)), dma((2, 8)), dma((6,)), dma((6,)),
            dma((6,)), dma((6,)), dma((6,)), dma((6,)), dma((6,)), dma((6,)),
            dma((6,)), dma((6,)), dma((6,)), dma((6,)),
            dma((6,)), dma((6,)), dma((1,)), dma((1,)), dma((10,)), dma((10,)),
        ],
        compiler_params=pltpu.CompilerParams(
            collective_id=0, has_side_effects=True, vmem_limit_bytes=56 * 2**20
        ),
        name="step",
    )(brick_pos, norm_gain.reshape(1, C), features, cotangent, first_kernel, second_kernel)
    out, fgrad, update, gain = pl.pallas_call(
        finish_kernel,
        out_shape=(
            jax.ShapeDtypeStruct((2, 512, C), BF16),
            jax.ShapeDtypeStruct((2, 512, C), BF16),
            jax.ShapeDtypeStruct((2, 27, C, C), F32),
            jax.ShapeDtypeStruct((1, C), F32),
        ),
        in_specs=[vmem, vmem, vmem],
        out_specs=(hbm, hbm, hbm, vmem),
        scratch_shapes=[V((6, 9, C, C), F32), dma((20,))],
        compiler_params=pltpu.CompilerParams(vmem_limit_bytes=10 * 2**20),
        name="finish",
    )(outv, full, stats)
    return out, fgrad, update, gain.reshape(C)


def solution(mesh):
    rows = P(("gx", "gy"), None, None)
    return jax.shard_map(
        per_device, mesh=mesh, in_specs=(rows, P(("gx", "gy")), rows, P(), P(), P()),
        out_specs=(rows, rows, P(), P()), check_vma=False,
    )
```

```python
import jax
import jax.numpy as jnp
from jax import lax
from jax.experimental import pallas as pl
from jax.experimental.pallas import tpu as pltpu
from jax.sharding import PartitionSpec as P

MESH = pl.DeviceIdType.MESH
F32 = jnp.float32
BF16 = jnp.bfloat16
CLIP = 0.5
C = 128
POS = 4
DIRS = [(dx, dy) for dx in (-1, 0, 1) for dy in (-1, 0, 1) if (dx, dy) != (0, 0)]
ORDERS = [(0, 1, 2), (1, 2, 0), (2, 0, 1)]
NT = (((1,), (1,)), ((), ()))


def span(d, size, halo):
    if d == 0:
        return pl.ds(1, 16)
    if d < 0:
        return pl.ds(0 if halo else 1, 1)
    return pl.ds(17 if halo else 16, 1)


def step_kernel(
    pos_ref, gain_ref, feat_hbm, cot_hbm, k1_hbm, k2_hbm,
    outv, full_ref, stats_ref,
    feat, cot, w1, w2, r1, r2, r2y, grid1, land, grid2, ag, au, ah, ap, pre_ref, hg_ref, hid_t, pgr_t,
    hid, pgr, part, rcore, sa, ra, sb, rb, rc, gains, sums, units, invs,
    in_sem, hs, hr, cs, cr, a_s, a_r, b_s, b_r, c_s, c_r, eb_s, eb_r, ea_s, ea_r, sib_s, sib_r, sums_s, sums_r, gs, gr,
):
    gx = lax.axis_index("gx")
    gy = lax.axis_index("gy")
    core = gy % 2
    coord = ((gy // 2) % 2 * 2 + gx // 4, gx % 4, gy // 4)

    def device(x, y, z):
        return (x % 2 * 4 + y, z * 4 + x // 2 * 2 + core)

    def peer(axis, value):
        return device(*(value if i == axis else coord[i] for i in range(3)))

    sibling = (gx, gy + 1 - 2 * core)

    def there(d):
        x, y = gx + d[0], gy + d[1]
        return (x >= 0) & (x < 8) & (y >= 0) & (y < 16)

    def load(i, src, dst):
        return pltpu.make_async_copy(src, dst, in_sem.at[i])

    loads = [load(0, feat_hbm, feat), load(1, cot_hbm, cot), load(2, k1_hbm, w1), load(3, k2_hbm, w2)]
    for c in loads:
        c.start()

    def clear(g):
        for f in range(2):
            for e in (0, 17):
                g[f, e] = jnp.zeros((18, 8, C), BF16)
                g[f, pl.ds(1, 16), e] = jnp.zeros((16, 8, C), BF16)

    clear(land)
    barrier = pltpu.get_barrier_semaphore()
    for d in DIRS:
        @pl.when(there(d))
        def _():
            pl.semaphore_signal(barrier, inc=1, device_id=(gx + d[0], gy + d[1]), device_id_type=MESH)
    for axis in range(3):
        for k in (1, 2, 3):
            pl.semaphore_signal(barrier, inc=1, device_id=peer(axis, (coord[axis] + k) % 4), device_id_type=MESH)
    pl.semaphore_signal(barrier, inc=1, device_id=sibling, device_id_type=MESH)

    clear(grid1)
    clear(grid2)
    p0, p1 = pos_ref[0], pos_ref[1]
    where = [jnp.minimum(p0, POS - 1), jnp.minimum(p1, POS - 1)]

    def pick(pair, s):
        return pair[s] if isinstance(s, int) else jnp.where(s == 0, pair[0], pair[1])

    def bx(s):
        return pick(where, s) // 2

    def by(s):
        return pick(where, s) % 2

    live = [(p0 < POS).astype(F32), (p1 < POS).astype(F32)]

    def place(grid, f, source):
        masks = [((p0 == p).astype(F32), (p1 == p).astype(F32)) for p in range(POS)]
        for x in range(8):
            rows = pl.ds(x * 64, 64)
            v0, v1 = source[0, rows].astype(F32), source[1, rows].astype(F32)
            for p, (m0, m1) in enumerate(masks):
                v = (v0 * m0 + v1 * m1).reshape(8, 8, C).astype(BF16)
                grid[f, 1 + p // 2 * 8 + x, pl.ds(1 + p % 2 * 8, 8)] = v

    def halo(phase, grid, landing):
        def copies(d):
            i = DIRS.index(d)
            return pltpu.make_async_remote_copy(
                src_ref=grid.at[:, span(d[0], 16, False), span(d[1], 16, False)],
                dst_ref=landing.at[:, span(-d[0], 16, True), span(-d[1], 16, True)],
                send_sem=hs.at[phase, i], recv_sem=hr.at[phase, i],
                device_id=(gx + d[0], gy + d[1]), device_id_type=MESH,
            )

        def start():
            for d in DIRS:
                @pl.when(there(d))
                def _():
                    copies(d).start()

        def arrive():
            for d in DIRS:
                @pl.when(there((-d[0], -d[1])))
                def _():
                    copies(d).wait_recv()

        def done():
            for d in DIRS:
                @pl.when(there(d))
                def _():
                    copies(d).wait_send()

        return start, arrive, done

    start1, arrive1, done1 = halo(0, grid1, land)
    start2, arrive2, done2 = halo(1, grid2, grid2)

    loads[0].wait()
    loads[1].wait()
    place(grid1, 0, feat)
    place(grid1, 1, cot)

    expected = 10
    for d in DIRS:
        expected = expected + there(d).astype(jnp.int32)
    pl.semaphore_wait(barrier, expected)
    start1()

    loads[2].wait()
    loads[3].wait()
    for t in range(27):
        r2[t // 9, :, pl.ds(t % 9 * C, C)] = w2[26 - t]
        r2y[t // 9, t % 9 // 3, :, pl.ds(t % 3 * C, C)] = w2[26 - t]

    z = lax.broadcasted_iota(jnp.int32, (10, 8, C), 1)
    first, last = z == 0, z == 7

    def sides(t):
        n = t.shape[0]
        return (jnp.where(first[:n], 0.0, pltpu.roll(t, 1, 1)), t, jnp.where(last[:n], 0.0, pltpu.roll(t, 7, 1)))

    def gather(a, s, grid, f, layers=None):
        def layer(x, carry):
            t = grid[f, bx(s) * 8 + x, pl.ds(by(s) * 8, 10)].astype(F32)
            for oz, v in enumerate(sides(t)):
                for oy in range(3):
                    a[s, x, :, pl.ds((oy * 3 + oz) * C, C)] = v[oy : oy + 8].reshape(64, C).astype(BF16)
            return carry

        if layers is None:
            lax.fori_loop(0, 10, layer, 0)
        else:
            for x in layers:
                layer(x, 0)

    def patch(a, s, grid, f):
        gather(a, s, grid, f, (0, 9))

        def layer(x, carry):
            for oy in (0, 2):
                t = grid[f, bx(s) * 8 + x, pl.ds(by(s) * 8 + oy * 4, 2)].astype(F32)
                for oz, v in enumerate(sides(t)):
                    a[s, x, pl.ds(oy * 24, 16), pl.ds((oy * 3 + oz) * C, C)] = v.reshape(16, C).astype(BF16)
            return carry

        lax.fori_loop(1, 9, layer, 0)

    def conv(a, s, w):
        total = None
        for ox in range(3):
            v = jnp.dot(a[s, pl.ds(ox, 8)].reshape(512, 9 * C), w[pl.ds(ox * 9, 9)].reshape(9 * C, C), preferred_element_type=F32)
            total = v if total is None else total + v
        return total

    def conv_t(a, s, r):
        total = None
        for ox in range(3):
            v = lax.dot_general(a[s, pl.ds(ox, 8)].reshape(512, 9 * C), r[ox], NT, preferred_element_type=F32)
            total = v if total is None else total + v
        return total

    def fix(a, s, f, total, weights, block):
        cx = weights(a[s, bx(s) * 9], bx(s) * 2)
        for i in (0, 1):
            edge = (bx(s) == i).astype(F32)
            total[i * 7] = total[i * 7] + (cx * edge).reshape(8, 8, C)
        t = grid1[f, pl.ds(bx(s) * 8, 10), by(s) * 17].astype(F32)
        layer = lax.broadcasted_iota(jnp.int32, (10, 8, C), 0)
        low, high = (bx(s) == 1).astype(F32), (bx(s) == 0).astype(F32)
        t = t * jnp.where(layer == 0, low, jnp.where(layer == 9, high, 1.0))
        shifted = sides(t)
        cy = None
        for ox in range(3):
            rows = jnp.concatenate([v[ox : ox + 8].reshape(64, C) for v in shifted], axis=1).astype(BF16)
            v = block(rows, ox, by(s) * 2)
            cy = v if cy is None else cy + v
        for i in (0, 1):
            edge = (by(s) == i).astype(F32)
            total[:, i * 7] = total[:, i * 7] + (cy * edge).reshape(8, 8, C)

    def fix_first(s):
        fix(ag, s, 0, pre_ref.at[s],
            lambda rows, ox: jnp.dot(rows, w1[pl.ds(ox * 9, 9)].reshape(9 * C, C), preferred_element_type=F32),
            lambda rows, ox, oy: jnp.dot(
                rows, w1[pl.ds(ox * 9 + oy * 3, 3)].reshape(3 * C, C), preferred_element_type=F32))

    def fix_second(s):
        fix(au, s, 1, hg_ref.at[s],
            lambda rows, ox: lax.dot_general(rows, r2[ox], NT, preferred_element_type=F32),
            lambda rows, ox, oy: lax.dot_general(rows, r2y[ox, oy], NT, preferred_element_type=F32))

    def first_local(s, carry):
        gather(ag, s, grid1, 0)
        pre_ref[s] = conv(ag, s, w1).reshape(8, 8, 8, C)
        gather(au, s, grid1, 1)
        hg_ref[s] = conv_t(au, s, r2).reshape(8, 8, 8, C)
        return carry

    lax.fori_loop(0, 2, first_local, 0)
    arrive1()
    for f in range(2):
        for e in (0, 17):
            grid1[f, e] = land[f, e]
            grid1[f, pl.ds(1, 16), e] = land[f, pl.ds(1, 16), e]
    gain = gain_ref[0:1, :]

    half = pl.multiple_of(core * 64, 64)
    other = pl.multiple_of((1 - core) * 64, 64)

    def core_copy(g, first=0, count=9):
        taps = pl.ds(g * 9 + first, count)
        return pltpu.make_async_remote_copy(
            src_ref=part.at[taps, pl.ds(other, 64)], dst_ref=rcore.at[taps],
            send_sem=cs.at[g], recv_sem=cr.at[g], device_id=sibling, device_id_type=MESH)

    def group(g, flip, a, lhs):
        ox = 2 - g if flip else g - 3
        v = (jnp.dot(lhs[0], a[0, pl.ds(ox, 8)].reshape(512, 9 * C), preferred_element_type=F32)
             + jnp.dot(lhs[1], a[1, pl.ds(ox, 8)].reshape(512, 9 * C), preferred_element_type=F32))
        for k in range(9):
            if flip:
                part[g * 9 + 8 - k] = v[:, k * C : (k + 1) * C]
            else:
                part[g * 9 + k] = v[:, k * C : (k + 1) * C].T
            if k % 3 == 2:
                core_copy(g, 8 - k if flip else k - 2, 3).start()

    def axes(g):
        return ORDERS[g % 3]

    def remote(src, dst, send_sem, recv_sem, to):
        return pltpu.make_async_remote_copy(
            src_ref=src, dst_ref=dst, send_sem=send_sem, recv_sem=recv_sem, device_id=to, device_id_type=MESH)

    def local(ref, send_sem, recv_sem):
        return remote(ref, ref, send_sem, recv_sem, sibling)

    def three(axis, copy):
        for k in (2, 1, 3):
            to = (coord[axis] + k) % 4
            copy(k - 1, to, peer(axis, to)).start()

    def all_a(g):
        return local(ra.at[g], a_s.at[g], a_r.at[g])

    def all_b(g):
        return local(rb.at[g], b_s.at[g], b_r.at[g])

    def all_c(g):
        return local(rc.at[g, pl.ds(0, 3)], c_s.at[g], c_r.at[g])

    def all_eb(g):
        return local(full_ref.at[g, 0, 0, pl.ds(0, 15)], eb_s.at[g], eb_r.at[g])

    def all_ea(g):
        return local(full_ref.at[g, 0, pl.ds(0, 3)], ea_s.at[g], ea_r.at[g])

    def scatter(g):
        core_copy(g).wait_recv()

        def tap(k, carry):
            v = part[g * 9 + k, pl.ds(half, 64)] + rcore[g * 9 + k]
            rcore[g * 9 + k] = v
            sa[g, k] = v.reshape(4, 16, C).astype(BF16)
            return carry

        lax.fori_loop(0, 9, tap, 0)
        three(axes(g)[0], lambda k, to, d: remote(
            sa.at[g, :, to], ra.at[g, k], a_s.at[g], a_r.at[g], d))

    def reduce_a(g):
        all_a(g).wait_recv()
        a, b, _ = axes(g)
        v = rcore[pl.ds(g * 9, 9), pl.ds(pl.multiple_of(coord[a] * 16, 16), 16)]
        for k in range(3):
            v = v + ra[g, k].astype(F32)
        sb[g, pl.ds(0, 18)] = v.reshape(18, 8, C)
        three(b, lambda k, to, d: remote(
            sb.at[g, pl.ds(to * 5, 5)], rb.at[g, k], b_s.at[g], b_r.at[g], d))

    def reduce_b(g):
        all_b(g).wait_recv()
        _, b, c = axes(g)
        v = sb[g, pl.ds(coord[b] * 5, 5)]
        for k in range(3):
            v = v + rb[g, k]
        rc[g, coord[c]] = v
        mine = rc.at[g, coord[c]]
        three(c, lambda k, to, d: remote(mine, mine, c_s.at[g], c_r.at[g], d))

    def reduce_c(g):
        all_c(g).wait_recv()
        a, b, _ = axes(g)
        v = ((rc[g, 0] + rc[g, 1]) + rc[g, 2]) + rc[g, 3]
        full_ref[g, core, coord[a], pl.ds(coord[b] * 5, 5)] = v.astype(BF16)
        mine = full_ref.at[g, core, coord[a], pl.ds(coord[b] * 5, 5)]
        three(b, lambda k, to, d: remote(mine, mine, eb_s.at[g], eb_r.at[g], d))

    def spread(g):
        all_eb(g).wait_recv()
        a = axes(g)[0]
        mine = full_ref.at[g, core, coord[a]]
        three(a, lambda k, to, d: remote(mine, mine, ea_s.at[g], ea_r.at[g], d))

    def sib_copy(g):
        ref = full_ref.at[g, core]
        return remote(ref, ref, sib_s.at[g], sib_r.at[g], sibling)

    def squares(g, h):
        acc = None
        for a in range(4):
            v = full_ref[g, h, a, pl.ds(0, 18)].astype(F32)
            v = jnp.sum(v * v, axis=0)
            acc = v if acc is None else acc + v
        return acc

    def pass_on(g):
        all_ea(g).wait_recv()
        sib_copy(g).start()

    def close(groups, acc):
        for g in groups:
            pass_on(g)
        for g in groups:
            acc = acc + squares(g, core)
        return acc

    sums_copy = remote(sums.at[0], sums.at[1], sums_s.at[0], sums_r.at[0], sibling)

    def gain_copy(stage, k):
        if stage == 0:
            return pltpu.make_async_remote_copy(
                src_ref=gains.at[0, 0], dst_ref=gains.at[0, 1], send_sem=gs.at[0], recv_sem=gr.at[0],
                device_id=sibling, device_id_type=MESH)
        axis = stage - 1
        i = 1 + axis * 3 + k - 1
        return pltpu.make_async_remote_copy(
            src_ref=gains.at[stage, coord[axis]], dst_ref=gains.at[stage, coord[axis]],
            send_sem=gs.at[i], recv_sem=gr.at[i],
            device_id=peer(axis, (coord[axis] + k) % 4), device_id_type=MESH)

    def gain_step(stage):
        if stage == 0:
            gain_copy(0, 0).wait_recv()
            gains[1, coord[0]] = gains[0, 0] + gains[0, 1]
        else:
            for k in (1, 2, 3):
                gain_copy(stage, k).wait_recv()
            v = ((gains[stage, 0] + gains[stage, 1]) + gains[stage, 2]) + gains[stage, 3]
            if stage == 3:
                return v
            gains[stage + 1, coord[stage]] = v
        for k in (1, 2, 3):
            gain_copy(stage + 1, k).start()

    def outputs(s, carry):
        gather(ah, s, grid2, 0)
        v = conv(ah, s, w2) * pick(live, s) + feat[s].astype(F32) * pick(live, s)
        outv[0, s] = v.astype(BF16)
        return carry

    def feature_grads(s, carry):
        gather(ap, s, grid2, 1)
        v = (conv_t(ap, s, r1) + cot[s].astype(F32)) * pick(live, s)
        outv[1, s] = v.astype(BF16)
        return carry

    def forward(s, carry):
        patch(ag, s, grid1, 0)
        fix_first(s)
        pre = pre_ref[s].reshape(512, C)
        center = pre - jnp.mean(pre, axis=-1, keepdims=True)
        inv = lax.rsqrt(jnp.mean(center * center, axis=-1, keepdims=True) + 1e-05)
        unit = center * inv
        normed = unit * gain
        hidden = normed * jax.nn.sigmoid(normed) * pick(live, s)
        hid[s] = hidden.astype(BF16)
        units[s] = unit
        invs[s] = jnp.broadcast_to(inv, (512, C))
        hid_t[s] = hidden.T.astype(BF16)
        patch(au, s, grid1, 1)
        return carry

    def backward(s, total):
        fix_second(s)
        hgrad = hg_ref[s].reshape(512, C) * pick(live, s)
        unit, inv = units[s], invs[s]
        normed = unit * gain
        sig = jax.nn.sigmoid(normed)
        dn = hgrad * (sig * (1.0 + normed * (1.0 - sig)))
        du = dn * gain
        dc = inv * (du - unit * jnp.mean(du * unit, axis=-1, keepdims=True))
        pg = (dc - jnp.mean(dc, axis=-1, keepdims=True)) * pick(live, s)
        pgr[s] = pg.astype(BF16)
        pgr_t[s] = pg.T.astype(BF16)
        return total + jnp.sum(dn * unit, axis=0, keepdims=True)

    for g in range(6):
        sb[g, pl.ds(18, 2)] = jnp.zeros((2, 8, C), F32)
    lax.fori_loop(0, 2, forward, 0)
    early, late = (0, 1, 2), (3, 4, 5)

    def early_group(g, carry):
        group(g, True, au, hid_t)
        return carry

    def late_group(g, carry):
        group(g, False, ag, pgr_t)
        return carry

    lax.fori_loop(0, 3, early_group, 0)
    gsum = lax.fori_loop(0, 2, backward, jnp.zeros((1, C), F32))
    for g in early:
        scatter(g)
    gains[0, 0] = jnp.broadcast_to(gsum, (8, C))
    gain_copy(0, 0).start()
    lax.fori_loop(3, 6, late_group, 0)
    place(grid2, 0, hid)
    place(grid2, 1, pgr)
    start2()
    for g in late:
        scatter(g)
    gain_step(0)
    for t in range(27):
        r1[t // 9, :, pl.ds(t % 9 * C, C)] = w1[26 - t]
    for g in early:
        reduce_a(g)
    arrive2()
    for g in late:
        reduce_a(g)
    gain_step(1)
    for g in early + late:
        reduce_b(g)
    lax.fori_loop(0, 2, outputs, 0)
    gain_step(2)
    for g in early + late:
        reduce_c(g)
    lax.fori_loop(0, 2, feature_grads, 0)
    for g in early:
        spread(g)
    for g in late:
        spread(g)
    gain_sum = gain_step(3)
    acc = close(early, jnp.zeros((8, C), F32))
    acc = close(late, acc)
    sums[0] = acc
    sums_copy.start()
    for g in early + late:
        sib_copy(g).wait_recv()
    sums_copy.wait_recv()
    acc = acc + sums[1]
    total = jnp.sum(acc) + jnp.sum(gain_sum[0:1] * gain_sum[0:1])
    entries = 54.0 * C * C + C
    mean = jnp.full((8, C), total / entries + 1e-06, F32)
    shrink = jnp.minimum(1.0, CLIP / jnp.sqrt(mean))
    stats_ref[0] = shrink
    stats_ref[1] = shrink * gain_sum

    done1()
    done2()
    for g in range(6):
        core_copy(g).wait_send()
        sib_copy(g).wait_send()
        for sent in (all_a, all_b, all_c, all_eb, all_ea):
            sent(g).wait_send()
    gain_copy(0, 0).wait_send()
    sums_copy.wait_send()
    for k in (1, 2, 3):
        for stage in (1, 2, 3):
            gain_copy(stage, k).wait_send()


def finish_kernel(outv, full_ref, stats_ref, out_hbm, fgrad_hbm, update_hbm, gain_ref, scaled, sem):
    copies = [pltpu.make_async_copy(outv.at[0], out_hbm, sem.at[18]),
              pltpu.make_async_copy(outv.at[1], fgrad_hbm, sem.at[19])]
    for c in copies:
        c.start()
    shrink = stats_ref[0, 0:1, :]
    for g in range(6):
        for k in range(9):
            for h in range(2):
                v = full_ref[g, h, :, pl.ds(k * 2, 2)].astype(F32).reshape(64, C)
                scaled[g, k, pl.ds(h * 64, 64)] = v * shrink
            if k % 3 == 2:
                c = pltpu.make_async_copy(
                    scaled.at[g, pl.ds(k - 2, 3)], update_hbm.at[1 - g // 3, pl.ds(g % 3 * 9 + k - 2, 3)],
                    sem.at[g * 3 + k // 3])
                c.start()
                copies.append(c)
    gain_ref[...] = stats_ref[1, 0:1, :]
    for c in copies:
        c.wait()


def per_device(features, brick_pos, cotangent, first_kernel, second_kernel, norm_gain):
    hbm = pl.BlockSpec(memory_space=pltpu.HBM)
    vmem = pl.BlockSpec(memory_space=pltpu.VMEM)
    dma = pltpu.SemaphoreType.DMA
    V = pltpu.VMEM
    tile = (2, 10, 64, 9 * C)
    outv, full, stats = pl.pallas_call(
        step_kernel,
        out_shape=(V((2, 2, 512, C), BF16), V((6, 2, 4, 20, 8, C), BF16), V((2, 8, C), F32)),
        in_specs=[pl.BlockSpec(memory_space=pltpu.SMEM), vmem, hbm, hbm, hbm, hbm],
        out_specs=(vmem, vmem, vmem),
        scratch_shapes=[
            V((2, 512, C), BF16), V((2, 512, C), BF16),
            V((27, C, C), BF16), V((27, C, C), BF16),
            V((3, C, 9 * C), BF16), V((3, C, 9 * C), BF16), V((3, 3, C, 3 * C), BF16),
            V((2, 18, 18, 8, C), BF16), V((2, 18, 18, 8, C), BF16), V((2, 18, 18, 8, C), BF16),
            V(tile, BF16), V(tile, BF16), V(tile, BF16), V(tile, BF16),
            V((2, 8, 8, 8, C), F32), V((2, 8, 8, 8, C), F32), V((2, C, 512), BF16), V((2, C, 512), BF16),
            V((2, 512, C), BF16), V((2, 512, C), BF16),
            V((54, C, C), F32), V((54, 64, C), F32),
            V((6, 9, 4, 16, C), BF16), V((6, 3, 9, 16, C), BF16),
            V((6, 20, 8, C), F32), V((6, 3, 5, 8, C), F32), V((6, 4, 5, 8, C), F32),
            V((4, 4, 8, C), F32), V((2, 8, C), F32),
            V((2, 512, C), F32), V((2, 512, C), F32),
            dma((4,)), dma((2, 8)), dma((2, 8)), dma((6,)), dma((6,)),
            dma((6,)), dma((6,)), dma((6,)), dma((6,)), dma((6,)), dma((6,)),
            dma((6,)), dma((6,)), dma((6,)), dma((6,)),
            dma((6,)), dma((6,)), dma((1,)), dma((1,)), dma((10,)), dma((10,)),
        ],
        compiler_params=pltpu.CompilerParams(
            collective_id=0, has_side_effects=True, vmem_limit_bytes=56 * 2**20
        ),
        name="step",
    )(brick_pos, norm_gain.reshape(1, C), features, cotangent, first_kernel, second_kernel)
    out, fgrad, update, gain = pl.pallas_call(
        finish_kernel,
        out_shape=(
            jax.ShapeDtypeStruct((2, 512, C), BF16),
            jax.ShapeDtypeStruct((2, 512, C), BF16),
            jax.ShapeDtypeStruct((2, 27, C, C), F32),
            jax.ShapeDtypeStruct((1, C), F32),
        ),
        in_specs=[vmem, vmem, vmem],
        out_specs=(hbm, hbm, hbm, vmem),
        scratch_shapes=[V((6, 9, C, C), F32), dma((20,))],
        compiler_params=pltpu.CompilerParams(vmem_limit_bytes=10 * 2**20),
        name="finish",
    )(outv, full, stats)
    return out, fgrad, update, gain.reshape(C)


def solution(mesh):
    rows = P(("gx", "gy"), None, None)
    return jax.shard_map(
        per_device, mesh=mesh, in_specs=(rows, P(("gx", "gy")), rows, P(), P(), P()),
        out_specs=(rows, rows, P(), P()), check_vma=False,
    )
```

```python
import jax
import jax.numpy as jnp
from jax import lax
from jax.experimental import pallas as pl
from jax.experimental.pallas import tpu as pltpu
from jax.sharding import PartitionSpec as P

MESH = pl.DeviceIdType.MESH
F32 = jnp.float32
BF16 = jnp.bfloat16
CLIP = 0.5
C = 128
POS = 4
DIRS = [(dx, dy) for dx in (-1, 0, 1) for dy in (-1, 0, 1) if (dx, dy) != (0, 0)]
ORDERS = [(0, 1, 2), (1, 2, 0), (2, 0, 1)]
NT = (((1,), (1,)), ((), ()))


def span(d, size, halo):
    if d == 0:
        return pl.ds(1, 16)
    if d < 0:
        return pl.ds(0 if halo else 1, 1)
    return pl.ds(17 if halo else 16, 1)


def step_kernel(
    pos_ref, gain_ref, feat_hbm, cot_hbm, k1_hbm, k2_hbm,
    outv, full_ref, stats_ref,
    feat, cot, w1, w2, r1, r2, r2y, grid1, land, grid2, ag, au, ah, ap, pre_ref, hg_ref, hid_t, pgr_t,
    hid, pgr, part, rcore, sa, ra, sb, rb, rc, gains, sums, units, invs,
    in_sem, hs, hr, cs, cr, a_s, a_r, b_s, b_r, c_s, c_r, eb_s, eb_r, ea_s, ea_r, sib_s, sib_r, sums_s, sums_r, gs, gr,
):
    gx = lax.axis_index("gx")
    gy = lax.axis_index("gy")
    core = gy % 2
    coord = ((gy // 2) % 2 * 2 + gx // 4, gx % 4, gy // 4)

    def device(x, y, z):
        return (x % 2 * 4 + y, z * 4 + x // 2 * 2 + core)

    def peer(axis, value):
        return device(*(value if i == axis else coord[i] for i in range(3)))

    sibling = (gx, gy + 1 - 2 * core)

    def there(d):
        x, y = gx + d[0], gy + d[1]
        return (x >= 0) & (x < 8) & (y >= 0) & (y < 16)

    def load(i, src, dst):
        return pltpu.make_async_copy(src, dst, in_sem.at[i])

    loads = [load(0, feat_hbm, feat), load(1, cot_hbm, cot), load(2, k1_hbm, w1), load(3, k2_hbm, w2)]
    for c in loads:
        c.start()

    def clear(g):
        for f in range(2):
            for e in (0, 17):
                g[f, e] = jnp.zeros((18, 8, C), BF16)
                g[f, pl.ds(1, 16), e] = jnp.zeros((16, 8, C), BF16)

    clear(land)
    barrier = pltpu.get_barrier_semaphore()
    for d in DIRS:
        @pl.when(there(d))
        def _():
            pl.semaphore_signal(barrier, inc=1, device_id=(gx + d[0], gy + d[1]), device_id_type=MESH)
    for axis in range(3):
        for k in (1, 2, 3):
            pl.semaphore_signal(barrier, inc=1, device_id=peer(axis, (coord[axis] + k) % 4), device_id_type=MESH)
    pl.semaphore_signal(barrier, inc=1, device_id=sibling, device_id_type=MESH)

    clear(grid1)
    clear(grid2)
    p0, p1 = pos_ref[0], pos_ref[1]
    where = [jnp.minimum(p0, POS - 1), jnp.minimum(p1, POS - 1)]

    def pick(pair, s):
        return pair[s] if isinstance(s, int) else jnp.where(s == 0, pair[0], pair[1])

    def bx(s):
        return pick(where, s) // 2

    def by(s):
        return pick(where, s) % 2

    live = [(p0 < POS).astype(F32), (p1 < POS).astype(F32)]

    def place(grid, f, source):
        masks = [((p0 == p).astype(F32), (p1 == p).astype(F32)) for p in range(POS)]
        for x in range(8):
            rows = pl.ds(x * 64, 64)
            v0, v1 = source[0, rows].astype(F32), source[1, rows].astype(F32)
            for p, (m0, m1) in enumerate(masks):
                v = (v0 * m0 + v1 * m1).reshape(8, 8, C).astype(BF16)
                grid[f, 1 + p // 2 * 8 + x, pl.ds(1 + p % 2 * 8, 8)] = v

    def halo(phase, grid, landing):
        def copies(d):
            i = DIRS.index(d)
            return pltpu.make_async_remote_copy(
                src_ref=grid.at[:, span(d[0], 16, False), span(d[1], 16, False)],
                dst_ref=landing.at[:, span(-d[0], 16, True), span(-d[1], 16, True)],
                send_sem=hs.at[phase, i], recv_sem=hr.at[phase, i],
                device_id=(gx + d[0], gy + d[1]), device_id_type=MESH,
            )

        def start():
            for d in DIRS:
                @pl.when(there(d))
                def _():
                    copies(d).start()

        def arrive():
            for d in DIRS:
                @pl.when(there((-d[0], -d[1])))
                def _():
                    copies(d).wait_recv()

        def done():
            for d in DIRS:
                @pl.when(there(d))
                def _():
                    copies(d).wait_send()

        return start, arrive, done

    start1, arrive1, done1 = halo(0, grid1, land)
    start2, arrive2, done2 = halo(1, grid2, grid2)

    loads[0].wait()
    loads[1].wait()
    place(grid1, 0, feat)
    place(grid1, 1, cot)

    expected = 10
    for d in DIRS:
        expected = expected + there(d).astype(jnp.int32)
    pl.semaphore_wait(barrier, expected)
    start1()

    loads[2].wait()
    loads[3].wait()
    for t in range(27):
        r2[t // 9, :, pl.ds(t % 9 * C, C)] = w2[26 - t]
        r2y[t // 9, t % 9 // 3, :, pl.ds(t % 3 * C, C)] = w2[26 - t]

    z = lax.broadcasted_iota(jnp.int32, (10, 8, C), 1)
    first, last = z == 0, z == 7

    def sides(t):
        n = t.shape[0]
        return (jnp.where(first[:n], 0.0, pltpu.roll(t, 1, 1)), t, jnp.where(last[:n], 0.0, pltpu.roll(t, 7, 1)))

    def gather(a, s, grid, f, layers=None):
        def layer(x, carry):
            t = grid[f, bx(s) * 8 + x, pl.ds(by(s) * 8, 10)].astype(F32)
            for oz, v in enumerate(sides(t)):
                for oy in range(3):
                    a[s, x, :, pl.ds((oy * 3 + oz) * C, C)] = v[oy : oy + 8].reshape(64, C).astype(BF16)
            return carry

        if layers is None:
            lax.fori_loop(0, 10, layer, 0, unroll=2)
        else:
            for x in layers:
                layer(x, 0)

    def patch(a, s, grid, f):
        gather(a, s, grid, f, (0, 9))

        def layer(x, carry):
            for oy in (0, 2):
                t = grid[f, bx(s) * 8 + x, pl.ds(by(s) * 8 + oy * 4, 2)].astype(F32)
                for oz, v in enumerate(sides(t)):
                    a[s, x, pl.ds(oy * 24, 16), pl.ds((oy * 3 + oz) * C, C)] = v.reshape(16, C).astype(BF16)
            return carry

        lax.fori_loop(1, 9, layer, 0, unroll=4)

    def conv(a, s, w):
        total = None
        for ox in range(3):
            v = jnp.dot(a[s, pl.ds(ox, 8)].reshape(512, 9 * C), w[pl.ds(ox * 9, 9)].reshape(9 * C, C), preferred_element_type=F32)
            total = v if total is None else total + v
        return total

    def conv_t(a, s, r):
        total = None
        for ox in range(3):
            v = lax.dot_general(a[s, pl.ds(ox, 8)].reshape(512, 9 * C), r[ox], NT, preferred_element_type=F32)
            total = v if total is None else total + v
        return total

    def fix(a, s, f, total, weights, block):
        cx = weights(a[s, bx(s) * 9], bx(s) * 2)
        for i in (0, 1):
            edge = (bx(s) == i).astype(F32)
            total[i * 7] = total[i * 7] + (cx * edge).reshape(8, 8, C)
        t = grid1[f, pl.ds(bx(s) * 8, 10), by(s) * 17].astype(F32)
        layer = lax.broadcasted_iota(jnp.int32, (10, 8, C), 0)
        low, high = (bx(s) == 1).astype(F32), (bx(s) == 0).astype(F32)
        t = t * jnp.where(layer == 0, low, jnp.where(layer == 9, high, 1.0))
        shifted = sides(t)
        cy = None
        for ox in range(3):
            rows = jnp.concatenate([v[ox : ox + 8].reshape(64, C) for v in shifted], axis=1).astype(BF16)
            v = block(rows, ox, by(s) * 2)
            cy = v if cy is None else cy + v
        for i in (0, 1):
            edge = (by(s) == i).astype(F32)
            total[:, i * 7] = total[:, i * 7] + (cy * edge).reshape(8, 8, C)

    def fix_first(s):
        fix(ag, s, 0, pre_ref.at[s],
            lambda rows, ox: jnp.dot(rows, w1[pl.ds(ox * 9, 9)].reshape(9 * C, C), preferred_element_type=F32),
            lambda rows, ox, oy: jnp.dot(
                rows, w1[pl.ds(ox * 9 + oy * 3, 3)].reshape(3 * C, C), preferred_element_type=F32))

    def fix_second(s):
        fix(au, s, 1, hg_ref.at[s],
            lambda rows, ox: lax.dot_general(rows, r2[ox], NT, preferred_element_type=F32),
            lambda rows, ox, oy: lax.dot_general(rows, r2y[ox, oy], NT, preferred_element_type=F32))

    def first_local(s, carry):
        gather(ag, s, grid1, 0)
        pre_ref[s] = conv(ag, s, w1).reshape(8, 8, 8, C)
        gather(au, s, grid1, 1)
        hg_ref[s] = conv_t(au, s, r2).reshape(8, 8, 8, C)
        return carry

    lax.fori_loop(0, 2, first_local, 0)
    arrive1()
    for f in range(2):
        for e in (0, 17):
            grid1[f, e] = land[f, e]
            grid1[f, pl.ds(1, 16), e] = land[f, pl.ds(1, 16), e]
    gain = gain_ref[0:1, :]

    half = pl.multiple_of(core * 64, 64)
    other = pl.multiple_of((1 - core) * 64, 64)

    def core_copy(g, first=0, count=9):
        taps = pl.ds(g * 9 + first, count)
        return pltpu.make_async_remote_copy(
            src_ref=part.at[taps, pl.ds(other, 64)], dst_ref=rcore.at[taps],
            send_sem=cs.at[g], recv_sem=cr.at[g], device_id=sibling, device_id_type=MESH)

    def group(g, flip, a, lhs):
        ox = 2 - g if flip else g - 3
        v = (jnp.dot(lhs[0], a[0, pl.ds(ox, 8)].reshape(512, 9 * C), preferred_element_type=F32)
             + jnp.dot(lhs[1], a[1, pl.ds(ox, 8)].reshape(512, 9 * C), preferred_element_type=F32))
        for k in range(9):
            if flip:
                part[g * 9 + 8 - k] = v[:, k * C : (k + 1) * C]
            else:
                part[g * 9 + k] = v[:, k * C : (k + 1) * C].T
            if k % 3 == 2:
                core_copy(g, 8 - k if flip else k - 2, 3).start()

    def axes(g):
        return ORDERS[g % 3]

    def remote(src, dst, send_sem, recv_sem, to):
        return pltpu.make_async_remote_copy(
            src_ref=src, dst_ref=dst, send_sem=send_sem, recv_sem=recv_sem, device_id=to, device_id_type=MESH)

    def local(ref, send_sem, recv_sem):
        return remote(ref, ref, send_sem, recv_sem, sibling)

    def three(axis, copy):
        for k in (2, 1, 3):
            to = (coord[axis] + k) % 4
            copy(k - 1, to, peer(axis, to)).start()

    def all_a(g):
        return local(ra.at[g], a_s.at[g], a_r.at[g])

    def all_b(g):
        return local(rb.at[g], b_s.at[g], b_r.at[g])

    def all_c(g):
        return local(rc.at[g, pl.ds(0, 3)], c_s.at[g], c_r.at[g])

    def all_eb(g):
        return local(full_ref.at[g, 0, 0, pl.ds(0, 15)], eb_s.at[g], eb_r.at[g])

    def all_ea(g):
        return local(full_ref.at[g, 0, pl.ds(0, 3)], ea_s.at[g], ea_r.at[g])

    def scatter(g):
        core_copy(g).wait_recv()

        def tap(k, carry):
            v = part[g * 9 + k, pl.ds(half, 64)] + rcore[g * 9 + k]
            rcore[g * 9 + k] = v
            sa[g, k] = v.reshape(4, 16, C).astype(BF16)
            return carry

        lax.fori_loop(0, 9, tap, 0)
        three(axes(g)[0], lambda k, to, d: remote(
            sa.at[g, :, to], ra.at[g, k], a_s.at[g], a_r.at[g], d))

    def reduce_a(g):
        all_a(g).wait_recv()
        a, b, _ = axes(g)
        v = rcore[pl.ds(g * 9, 9), pl.ds(pl.multiple_of(coord[a] * 16, 16), 16)]
        for k in range(3):
            v = v + ra[g, k].astype(F32)
        sb[g, pl.ds(0, 18)] = v.reshape(18, 8, C)
        three(b, lambda k, to, d: remote(
            sb.at[g, pl.ds(to * 5, 5)], rb.at[g, k], b_s.at[g], b_r.at[g], d))

    def reduce_b(g):
        all_b(g).wait_recv()
        _, b, c = axes(g)
        v = sb[g, pl.ds(coord[b] * 5, 5)]
        for k in range(3):
            v = v + rb[g, k]
        rc[g, coord[c]] = v
        mine = rc.at[g, coord[c]]
        three(c, lambda k, to, d: remote(mine, mine, c_s.at[g], c_r.at[g], d))

    def reduce_c(g):
        all_c(g).wait_recv()
        a, b, _ = axes(g)
        v = ((rc[g, 0] + rc[g, 1]) + rc[g, 2]) + rc[g, 3]
        full_ref[g, core, coord[a], pl.ds(coord[b] * 5, 5)] = v.astype(BF16)
        mine = full_ref.at[g, core, coord[a], pl.ds(coord[b] * 5, 5)]
        three(b, lambda k, to, d: remote(mine, mine, eb_s.at[g], eb_r.at[g], d))

    def spread(g):
        all_eb(g).wait_recv()
        a = axes(g)[0]
        mine = full_ref.at[g, core, coord[a]]
        three(a, lambda k, to, d: remote(mine, mine, ea_s.at[g], ea_r.at[g], d))

    def sib_copy(g):
        ref = full_ref.at[g, core]
        return remote(ref, ref, sib_s.at[g], sib_r.at[g], sibling)

    def squares(g, h):
        acc = None
        for a in range(4):
            v = full_ref[g, h, a, pl.ds(0, 18)].astype(F32)
            v = jnp.sum(v * v, axis=0)
            acc = v if acc is None else acc + v
        return acc

    def pass_on(g):
        all_ea(g).wait_recv()
        sib_copy(g).start()

    def close(groups, acc):
        for g in groups:
            pass_on(g)
        for g in groups:
            acc = acc + squares(g, core)
        return acc

    sums_copy = remote(sums.at[0], sums.at[1], sums_s.at[0], sums_r.at[0], sibling)

    def gain_copy(stage, k):
        if stage == 0:
            return pltpu.make_async_remote_copy(
                src_ref=gains.at[0, 0], dst_ref=gains.at[0, 1], send_sem=gs.at[0], recv_sem=gr.at[0],
                device_id=sibling, device_id_type=MESH)
        axis = stage - 1
        i = 1 + axis * 3 + k - 1
        return pltpu.make_async_remote_copy(
            src_ref=gains.at[stage, coord[axis]], dst_ref=gains.at[stage, coord[axis]],
            send_sem=gs.at[i], recv_sem=gr.at[i],
            device_id=peer(axis, (coord[axis] + k) % 4), device_id_type=MESH)

    def gain_step(stage):
        if stage == 0:
            gain_copy(0, 0).wait_recv()
            gains[1, coord[0]] = gains[0, 0] + gains[0, 1]
        else:
            for k in (1, 2, 3):
                gain_copy(stage, k).wait_recv()
            v = ((gains[stage, 0] + gains[stage, 1]) + gains[stage, 2]) + gains[stage, 3]
            if stage == 3:
                return v
            gains[stage + 1, coord[stage]] = v
        for k in (1, 2, 3):
            gain_copy(stage + 1, k).start()

    def outputs(s, carry):
        gather(ah, s, grid2, 0)
        v = conv(ah, s, w2) * pick(live, s) + feat[s].astype(F32) * pick(live, s)
        outv[0, s] = v.astype(BF16)
        return carry

    def feature_grads(s, carry):
        gather(ap, s, grid2, 1)
        v = (conv_t(ap, s, r1) + cot[s].astype(F32)) * pick(live, s)
        outv[1, s] = v.astype(BF16)
        return carry

    def forward(s, carry):
        patch(ag, s, grid1, 0)
        fix_first(s)
        pre = pre_ref[s].reshape(512, C)
        center = pre - jnp.mean(pre, axis=-1, keepdims=True)
        inv = lax.rsqrt(jnp.mean(center * center, axis=-1, keepdims=True) + 1e-05)
        unit = center * inv
        normed = unit * gain
        hidden = normed * jax.nn.sigmoid(normed) * pick(live, s)
        hid[s] = hidden.astype(BF16)
        units[s] = unit
        invs[s] = jnp.broadcast_to(inv, (512, C))
        hid_t[s] = hidden.T.astype(BF16)
        patch(au, s, grid1, 1)
        return carry

    def backward(s, total):
        fix_second(s)
        hgrad = hg_ref[s].reshape(512, C) * pick(live, s)
        unit, inv = units[s], invs[s]
        normed = unit * gain
        sig = jax.nn.sigmoid(normed)
        dn = hgrad * (sig * (1.0 + normed * (1.0 - sig)))
        du = dn * gain
        dc = inv * (du - unit * jnp.mean(du * unit, axis=-1, keepdims=True))
        pg = (dc - jnp.mean(dc, axis=-1, keepdims=True)) * pick(live, s)
        pgr[s] = pg.astype(BF16)
        pgr_t[s] = pg.T.astype(BF16)
        return total + jnp.sum(dn * unit, axis=0, keepdims=True)

    for g in range(6):
        sb[g, pl.ds(18, 2)] = jnp.zeros((2, 8, C), F32)
    lax.fori_loop(0, 2, forward, 0)
    early, late = (0, 1, 2), (3, 4, 5)

    def early_group(g, carry):
        group(g, True, au, hid_t)
        return carry

    def late_group(g, carry):
        group(g, False, ag, pgr_t)
        return carry

    lax.fori_loop(0, 3, early_group, 0)
    gsum = lax.fori_loop(0, 2, backward, jnp.zeros((1, C), F32))
    for g in early:
        scatter(g)
    gains[0, 0] = jnp.broadcast_to(gsum, (8, C))
    gain_copy(0, 0).start()
    lax.fori_loop(3, 6, late_group, 0)
    place(grid2, 0, hid)
    place(grid2, 1, pgr)
    start2()
    for g in late:
        scatter(g)
    gain_step(0)
    for t in range(27):
        r1[t // 9, :, pl.ds(t % 9 * C, C)] = w1[26 - t]
    for g in early:
        reduce_a(g)
    arrive2()
    for g in late:
        reduce_a(g)
    gain_step(1)
    for g in early + late:
        reduce_b(g)
    lax.fori_loop(0, 2, outputs, 0)
    gain_step(2)
    for g in early + late:
        reduce_c(g)
    lax.fori_loop(0, 2, feature_grads, 0)
    for g in early:
        spread(g)
    for g in late:
        spread(g)
    gain_sum = gain_step(3)
    acc = close(early, jnp.zeros((8, C), F32))
    acc = close(late, acc)
    sums[0] = acc
    sums_copy.start()
    for g in early + late:
        sib_copy(g).wait_recv()
    sums_copy.wait_recv()
    acc = acc + sums[1]
    total = jnp.sum(acc) + jnp.sum(gain_sum[0:1] * gain_sum[0:1])
    entries = 54.0 * C * C + C
    mean = jnp.full((8, C), total / entries + 1e-06, F32)
    shrink = jnp.minimum(1.0, CLIP / jnp.sqrt(mean))
    stats_ref[0] = shrink
    stats_ref[1] = shrink * gain_sum

    done1()
    done2()
    for g in range(6):
        core_copy(g).wait_send()
        sib_copy(g).wait_send()
        for sent in (all_a, all_b, all_c, all_eb, all_ea):
            sent(g).wait_send()
    gain_copy(0, 0).wait_send()
    sums_copy.wait_send()
    for k in (1, 2, 3):
        for stage in (1, 2, 3):
            gain_copy(stage, k).wait_send()


def finish_kernel(outv, full_ref, stats_ref, out_hbm, fgrad_hbm, update_hbm, gain_ref, scaled, sem):
    copies = [pltpu.make_async_copy(outv.at[0], out_hbm, sem.at[18]),
              pltpu.make_async_copy(outv.at[1], fgrad_hbm, sem.at[19])]
    for c in copies:
        c.start()
    shrink = stats_ref[0, 0:1, :]
    for g in range(6):
        for k in range(9):
            for h in range(2):
                v = full_ref[g, h, :, pl.ds(k * 2, 2)].astype(F32).reshape(64, C)
                scaled[g, k, pl.ds(h * 64, 64)] = v * shrink
            if k % 3 == 2:
                c = pltpu.make_async_copy(
                    scaled.at[g, pl.ds(k - 2, 3)], update_hbm.at[1 - g // 3, pl.ds(g % 3 * 9 + k - 2, 3)],
                    sem.at[g * 3 + k // 3])
                c.start()
                copies.append(c)
    gain_ref[...] = stats_ref[1, 0:1, :]
    for c in copies:
        c.wait()


def per_device(features, brick_pos, cotangent, first_kernel, second_kernel, norm_gain):
    hbm = pl.BlockSpec(memory_space=pltpu.HBM)
    vmem = pl.BlockSpec(memory_space=pltpu.VMEM)
    dma = pltpu.SemaphoreType.DMA
    V = pltpu.VMEM
    tile = (2, 10, 64, 9 * C)
    outv, full, stats = pl.pallas_call(
        step_kernel,
        out_shape=(V((2, 2, 512, C), BF16), V((6, 2, 4, 20, 8, C), BF16), V((2, 8, C), F32)),
        in_specs=[pl.BlockSpec(memory_space=pltpu.SMEM), vmem, hbm, hbm, hbm, hbm],
        out_specs=(vmem, vmem, vmem),
        scratch_shapes=[
            V((2, 512, C), BF16), V((2, 512, C), BF16),
            V((27, C, C), BF16), V((27, C, C), BF16),
            V((3, C, 9 * C), BF16), V((3, C, 9 * C), BF16), V((3, 3, C, 3 * C), BF16),
            V((2, 18, 18, 8, C), BF16), V((2, 18, 18, 8, C), BF16), V((2, 18, 18, 8, C), BF16),
            V(tile, BF16), V(tile, BF16), V(tile, BF16), V(tile, BF16),
            V((2, 8, 8, 8, C), F32), V((2, 8, 8, 8, C), F32), V((2, C, 512), BF16), V((2, C, 512), BF16),
            V((2, 512, C), BF16), V((2, 512, C), BF16),
            V((54, C, C), F32), V((54, 64, C), F32),
            V((6, 9, 4, 16, C), BF16), V((6, 3, 9, 16, C), BF16),
            V((6, 20, 8, C), F32), V((6, 3, 5, 8, C), F32), V((6, 4, 5, 8, C), F32),
            V((4, 4, 8, C), F32), V((2, 8, C), F32),
            V((2, 512, C), F32), V((2, 512, C), F32),
            dma((4,)), dma((2, 8)), dma((2, 8)), dma((6,)), dma((6,)),
            dma((6,)), dma((6,)), dma((6,)), dma((6,)), dma((6,)), dma((6,)),
            dma((6,)), dma((6,)), dma((6,)), dma((6,)),
            dma((6,)), dma((6,)), dma((1,)), dma((1,)), dma((10,)), dma((10,)),
        ],
        compiler_params=pltpu.CompilerParams(
            collective_id=0, has_side_effects=True, vmem_limit_bytes=56 * 2**20
        ),
        name="step",
    )(brick_pos, norm_gain.reshape(1, C), features, cotangent, first_kernel, second_kernel)
    out, fgrad, update, gain = pl.pallas_call(
        finish_kernel,
        out_shape=(
            jax.ShapeDtypeStruct((2, 512, C), BF16),
            jax.ShapeDtypeStruct((2, 512, C), BF16),
            jax.ShapeDtypeStruct((2, 27, C, C), F32),
            jax.ShapeDtypeStruct((1, C), F32),
        ),
        in_specs=[vmem, vmem, vmem],
        out_specs=(hbm, hbm, hbm, vmem),
        scratch_shapes=[V((6, 9, C, C), F32), dma((20,))],
        compiler_params=pltpu.CompilerParams(vmem_limit_bytes=10 * 2**20),
        name="finish",
    )(outv, full, stats)
    return out, fgrad, update, gain.reshape(C)


def solution(mesh):
    rows = P(("gx", "gy"), None, None)
    return jax.shard_map(
        per_device, mesh=mesh, in_specs=(rows, P(("gx", "gy")), rows, P(), P(), P()),
        out_specs=(rows, rows, P(), P()), check_vma=False,
    )
```

```python
import jax
import jax.numpy as jnp
from jax import lax
from jax.experimental import pallas as pl
from jax.experimental.pallas import tpu as pltpu
from jax.sharding import PartitionSpec as P

MESH = pl.DeviceIdType.MESH
F32 = jnp.float32
BF16 = jnp.bfloat16
CLIP = 0.5
C = 128
POS = 4
DIRS = [(dx, dy) for dx in (-1, 0, 1) for dy in (-1, 0, 1) if (dx, dy) != (0, 0)]
ORDERS = [(0, 1, 2), (1, 2, 0), (2, 0, 1)]
NT = (((1,), (1,)), ((), ()))


def span(d, size, halo):
    if d == 0:
        return pl.ds(1, 16)
    if d < 0:
        return pl.ds(0 if halo else 1, 1)
    return pl.ds(17 if halo else 16, 1)


def step_kernel(
    pos_ref, gain_ref, feat_hbm, cot_hbm, k1_hbm, k2_hbm,
    outv, full_ref, stats_ref,
    feat, cot, w1, w2, r1, r2, r2y, grid1, land, grid2, ag, au, ah, ap, pre_ref, hg_ref, hid_t, pgr_t,
    hid, pgr, part, rcore, sa, ra, sb, rb, rc, gains, sums, units, invs,
    in_sem, hs, hr, cs, cr, a_s, a_r, b_s, b_r, c_s, c_r, eb_s, eb_r, ea_s, ea_r, sib_s, sib_r, sums_s, sums_r, gs, gr,
):
    gx = lax.axis_index("gx")
    gy = lax.axis_index("gy")
    core = gy % 2
    coord = ((gy // 2) % 2 * 2 + gx // 4, gx % 4, gy // 4)

    def device(x, y, z):
        return (x % 2 * 4 + y, z * 4 + x // 2 * 2 + core)

    def peer(axis, value):
        return device(*(value if i == axis else coord[i] for i in range(3)))

    sibling = (gx, gy + 1 - 2 * core)

    def there(d):
        x, y = gx + d[0], gy + d[1]
        return (x >= 0) & (x < 8) & (y >= 0) & (y < 16)

    def load(i, src, dst):
        return pltpu.make_async_copy(src, dst, in_sem.at[i])

    loads = [load(0, feat_hbm, feat), load(1, cot_hbm, cot), load(2, k1_hbm, w1), load(3, k2_hbm, w2)]
    for c in loads:
        c.start()

    def clear(g):
        for f in range(2):
            for e in (0, 17):
                g[f, e] = jnp.zeros((18, 8, C), BF16)
                g[f, pl.ds(1, 16), e] = jnp.zeros((16, 8, C), BF16)

    clear(land)
    barrier = pltpu.get_barrier_semaphore()
    for d in DIRS:
        @pl.when(there(d))
        def _():
            pl.semaphore_signal(barrier, inc=1, device_id=(gx + d[0], gy + d[1]), device_id_type=MESH)
    for axis in range(3):
        for k in (1, 2, 3):
            pl.semaphore_signal(barrier, inc=1, device_id=peer(axis, (coord[axis] + k) % 4), device_id_type=MESH)
    pl.semaphore_signal(barrier, inc=1, device_id=sibling, device_id_type=MESH)

    clear(grid1)
    clear(grid2)
    p0, p1 = pos_ref[0], pos_ref[1]
    where = [jnp.minimum(p0, POS - 1), jnp.minimum(p1, POS - 1)]

    def pick(pair, s):
        return pair[s] if isinstance(s, int) else jnp.where(s == 0, pair[0], pair[1])

    def bx(s):
        return pick(where, s) // 2

    def by(s):
        return pick(where, s) % 2

    live = [(p0 < POS).astype(F32), (p1 < POS).astype(F32)]

    def place(grid, f, source):
        masks = [((p0 == p).astype(F32), (p1 == p).astype(F32)) for p in range(POS)]
        for x in range(8):
            rows = pl.ds(x * 64, 64)
            v0, v1 = source[0, rows].astype(F32), source[1, rows].astype(F32)
            for p, (m0, m1) in enumerate(masks):
                v = (v0 * m0 + v1 * m1).reshape(8, 8, C).astype(BF16)
                grid[f, 1 + p // 2 * 8 + x, pl.ds(1 + p % 2 * 8, 8)] = v

    def halo(phase, grid, landing):
        def copies(d):
            i = DIRS.index(d)
            return pltpu.make_async_remote_copy(
                src_ref=grid.at[:, span(d[0], 16, False), span(d[1], 16, False)],
                dst_ref=landing.at[:, span(-d[0], 16, True), span(-d[1], 16, True)],
                send_sem=hs.at[phase, i], recv_sem=hr.at[phase, i],
                device_id=(gx + d[0], gy + d[1]), device_id_type=MESH,
            )

        def start():
            for d in DIRS:
                @pl.when(there(d))
                def _():
                    copies(d).start()

        def arrive():
            for d in DIRS:
                @pl.when(there((-d[0], -d[1])))
                def _():
                    copies(d).wait_recv()

        def done():
            for d in DIRS:
                @pl.when(there(d))
                def _():
                    copies(d).wait_send()

        return start, arrive, done

    start1, arrive1, done1 = halo(0, grid1, land)
    start2, arrive2, done2 = halo(1, grid2, grid2)

    loads[0].wait()
    loads[1].wait()
    place(grid1, 0, feat)
    place(grid1, 1, cot)

    expected = 10
    for d in DIRS:
        expected = expected + there(d).astype(jnp.int32)
    pl.semaphore_wait(barrier, expected)
    start1()

    loads[2].wait()
    loads[3].wait()
    for t in range(27):
        r2[t // 9, :, pl.ds(t % 9 * C, C)] = w2[26 - t]
        r2y[t // 9, t % 9 // 3, :, pl.ds(t % 3 * C, C)] = w2[26 - t]

    z = lax.broadcasted_iota(jnp.int32, (10, 8, C), 1)
    first, last = z == 0, z == 7

    def sides(t):
        n = t.shape[0]
        return (jnp.where(first[:n], 0.0, pltpu.roll(t, 1, 1)), t, jnp.where(last[:n], 0.0, pltpu.roll(t, 7, 1)))

    def gather(a, s, grid, f, layers=None):
        def layer(x, carry):
            t = grid[f, bx(s) * 8 + x, pl.ds(by(s) * 8, 10)].astype(F32)
            for oz, v in enumerate(sides(t)):
                for oy in range(3):
                    a[s, x, :, pl.ds((oy * 3 + oz) * C, C)] = v[oy : oy + 8].reshape(64, C).astype(BF16)
            return carry

        if layers is None:
            lax.fori_loop(0, 10, layer, 0, unroll=2)
        else:
            for x in layers:
                layer(x, 0)

    def patch(a, s, grid, f):
        gather(a, s, grid, f, (0, 9))

        def layer(x, carry):
            for oy in (0, 2):
                t = grid[f, bx(s) * 8 + x, pl.ds(by(s) * 8 + oy * 4, 2)].astype(F32)
                for oz, v in enumerate(sides(t)):
                    a[s, x, pl.ds(oy * 24, 16), pl.ds((oy * 3 + oz) * C, C)] = v.reshape(16, C).astype(BF16)
            return carry

        lax.fori_loop(1, 9, layer, 0, unroll=4)

    def conv(a, s, w):
        total = None
        for ox in range(3):
            v = jnp.dot(a[s, pl.ds(ox, 8)].reshape(512, 9 * C), w[pl.ds(ox * 9, 9)].reshape(9 * C, C), preferred_element_type=F32)
            total = v if total is None else total + v
        return total

    def conv_t(a, s, r):
        total = None
        for ox in range(3):
            v = lax.dot_general(a[s, pl.ds(ox, 8)].reshape(512, 9 * C), r[ox], NT, preferred_element_type=F32)
            total = v if total is None else total + v
        return total

    def fix(a, s, f, total, weights, block):
        cx = weights(a[s, bx(s) * 9], bx(s) * 2)
        for i in (0, 1):
            edge = (bx(s) == i).astype(F32)
            total[i * 7] = total[i * 7] + (cx * edge).reshape(8, 8, C)
        t = grid1[f, pl.ds(bx(s) * 8, 10), by(s) * 17].astype(F32)
        layer = lax.broadcasted_iota(jnp.int32, (10, 8, C), 0)
        low, high = (bx(s) == 1).astype(F32), (bx(s) == 0).astype(F32)
        t = t * jnp.where(layer == 0, low, jnp.where(layer == 9, high, 1.0))
        shifted = sides(t)
        cy = None
        for ox in range(3):
            rows = jnp.concatenate([v[ox : ox + 8].reshape(64, C) for v in shifted], axis=1).astype(BF16)
            v = block(rows, ox, by(s) * 2)
            cy = v if cy is None else cy + v
        for i in (0, 1):
            edge = (by(s) == i).astype(F32)
            total[:, i * 7] = total[:, i * 7] + (cy * edge).reshape(8, 8, C)

    def fix_first(s):
        fix(ag, s, 0, pre_ref.at[s],
            lambda rows, ox: jnp.dot(rows, w1[pl.ds(ox * 9, 9)].reshape(9 * C, C), preferred_element_type=F32),
            lambda rows, ox, oy: jnp.dot(
                rows, w1[pl.ds(ox * 9 + oy * 3, 3)].reshape(3 * C, C), preferred_element_type=F32))

    def fix_second(s):
        fix(au, s, 1, hg_ref.at[s],
            lambda rows, ox: lax.dot_general(rows, r2[ox], NT, preferred_element_type=F32),
            lambda rows, ox, oy: lax.dot_general(rows, r2y[ox, oy], NT, preferred_element_type=F32))

    def first_local(s, carry):
        gather(ag, s, grid1, 0)
        pre_ref[s] = conv(ag, s, w1).reshape(8, 8, 8, C)
        gather(au, s, grid1, 1)
        hg_ref[s] = conv_t(au, s, r2).reshape(8, 8, 8, C)
        return carry

    lax.fori_loop(0, 2, first_local, 0)
    arrive1()
    for f in range(2):
        for e in (0, 17):
            grid1[f, e] = land[f, e]
            grid1[f, pl.ds(1, 16), e] = land[f, pl.ds(1, 16), e]
    gain = gain_ref[0:1, :]

    half = pl.multiple_of(core * 64, 64)
    other = pl.multiple_of((1 - core) * 64, 64)

    def core_copy(g, first=0, count=9):
        taps = pl.ds(g * 9 + first, count)
        return pltpu.make_async_remote_copy(
            src_ref=part.at[taps, pl.ds(other, 64)], dst_ref=rcore.at[taps],
            send_sem=cs.at[g], recv_sem=cr.at[g], device_id=sibling, device_id_type=MESH)

    def group(g, flip, a, lhs):
        ox = 2 - g if flip else g - 3
        v = (jnp.dot(lhs[0], a[0, pl.ds(ox, 8)].reshape(512, 9 * C), preferred_element_type=F32)
             + jnp.dot(lhs[1], a[1, pl.ds(ox, 8)].reshape(512, 9 * C), preferred_element_type=F32))
        for k in range(9):
            if flip:
                part[g * 9 + 8 - k] = v[:, k * C : (k + 1) * C]
            else:
                part[g * 9 + k] = v[:, k * C : (k + 1) * C].T
            if k % 3 == 2:
                core_copy(g, 8 - k if flip else k - 2, 3).start()

    def axes(g):
        return ORDERS[g % 3]

    def remote(src, dst, send_sem, recv_sem, to):
        return pltpu.make_async_remote_copy(
            src_ref=src, dst_ref=dst, send_sem=send_sem, recv_sem=recv_sem, device_id=to, device_id_type=MESH)

    def local(ref, send_sem, recv_sem):
        return remote(ref, ref, send_sem, recv_sem, sibling)

    def three(axis, copy):
        for k in (2, 1, 3):
            to = (coord[axis] + k) % 4
            copy(k - 1, to, peer(axis, to)).start()

    def all_a(g):
        return local(ra.at[g], a_s.at[g], a_r.at[g])

    def all_b(g):
        return local(rb.at[g], b_s.at[g], b_r.at[g])

    def all_c(g):
        return local(rc.at[g, pl.ds(0, 3)], c_s.at[g], c_r.at[g])

    def all_eb(g):
        return local(full_ref.at[g, 0, 0, pl.ds(0, 15)], eb_s.at[g], eb_r.at[g])

    def all_ea(g):
        return local(full_ref.at[g, 0, pl.ds(0, 3)], ea_s.at[g], ea_r.at[g])

    def scatter(g):
        core_copy(g).wait_recv()

        def tap(k, carry):
            v = part[g * 9 + k, pl.ds(half, 64)] + rcore[g * 9 + k]
            rcore[g * 9 + k] = v
            sa[g, k] = v.reshape(4, 16, C).astype(BF16)
            return carry

        lax.fori_loop(0, 9, tap, 0, unroll=3)
        three(axes(g)[0], lambda k, to, d: remote(
            sa.at[g, :, to], ra.at[g, k], a_s.at[g], a_r.at[g], d))

    def reduce_a(g):
        all_a(g).wait_recv()
        a, b, _ = axes(g)
        v = rcore[pl.ds(g * 9, 9), pl.ds(pl.multiple_of(coord[a] * 16, 16), 16)]
        for k in range(3):
            v = v + ra[g, k].astype(F32)
        sb[g, pl.ds(0, 18)] = v.reshape(18, 8, C)
        three(b, lambda k, to, d: remote(
            sb.at[g, pl.ds(to * 5, 5)], rb.at[g, k], b_s.at[g], b_r.at[g], d))

    def reduce_b(g):
        all_b(g).wait_recv()
        _, b, c = axes(g)
        v = sb[g, pl.ds(coord[b] * 5, 5)]
        for k in range(3):
            v = v + rb[g, k]
        rc[g, coord[c]] = v
        mine = rc.at[g, coord[c]]
        three(c, lambda k, to, d: remote(mine, mine, c_s.at[g], c_r.at[g], d))

    def reduce_c(g):
        all_c(g).wait_recv()
        a, b, _ = axes(g)
        v = ((rc[g, 0] + rc[g, 1]) + rc[g, 2]) + rc[g, 3]
        full_ref[g, core, coord[a], pl.ds(coord[b] * 5, 5)] = v.astype(BF16)
        mine = full_ref.at[g, core, coord[a], pl.ds(coord[b] * 5, 5)]
        three(b, lambda k, to, d: remote(mine, mine, eb_s.at[g], eb_r.at[g], d))

    def spread(g):
        all_eb(g).wait_recv()
        a = axes(g)[0]
        mine = full_ref.at[g, core, coord[a]]
        three(a, lambda k, to, d: remote(mine, mine, ea_s.at[g], ea_r.at[g], d))

    def sib_copy(g):
        ref = full_ref.at[g, core]
        return remote(ref, ref, sib_s.at[g], sib_r.at[g], sibling)

    def squares(g, h):
        acc = None
        for a in range(4):
            v = full_ref[g, h, a, pl.ds(0, 18)].astype(F32)
            v = jnp.sum(v * v, axis=0)
            acc = v if acc is None else acc + v
        return acc

    def pass_on(g):
        all_ea(g).wait_recv()
        sib_copy(g).start()

    def close(groups, acc):
        for g in groups:
            pass_on(g)
        for g in groups:
            acc = acc + squares(g, core)
        return acc

    sums_copy = remote(sums.at[0], sums.at[1], sums_s.at[0], sums_r.at[0], sibling)

    def gain_copy(stage, k):
        if stage == 0:
            return pltpu.make_async_remote_copy(
                src_ref=gains.at[0, 0], dst_ref=gains.at[0, 1], send_sem=gs.at[0], recv_sem=gr.at[0],
                device_id=sibling, device_id_type=MESH)
        axis = stage - 1
        i = 1 + axis * 3 + k - 1
        return pltpu.make_async_remote_copy(
            src_ref=gains.at[stage, coord[axis]], dst_ref=gains.at[stage, coord[axis]],
            send_sem=gs.at[i], recv_sem=gr.at[i],
            device_id=peer(axis, (coord[axis] + k) % 4), device_id_type=MESH)

    def gain_step(stage):
        if stage == 0:
            gain_copy(0, 0).wait_recv()
            gains[1, coord[0]] = gains[0, 0] + gains[0, 1]
        else:
            for k in (1, 2, 3):
                gain_copy(stage, k).wait_recv()
            v = ((gains[stage, 0] + gains[stage, 1]) + gains[stage, 2]) + gains[stage, 3]
            if stage == 3:
                return v
            gains[stage + 1, coord[stage]] = v
        for k in (1, 2, 3):
            gain_copy(stage + 1, k).start()

    def outputs(s, carry):
        gather(ah, s, grid2, 0)
        v = conv(ah, s, w2) * pick(live, s) + feat[s].astype(F32) * pick(live, s)
        outv[0, s] = v.astype(BF16)
        return carry

    def feature_grads(s, carry):
        gather(ap, s, grid2, 1)
        v = (conv_t(ap, s, r1) + cot[s].astype(F32)) * pick(live, s)
        outv[1, s] = v.astype(BF16)
        return carry

    def forward(s, carry):
        patch(ag, s, grid1, 0)
        fix_first(s)
        pre = pre_ref[s].reshape(512, C)
        center = pre - jnp.mean(pre, axis=-1, keepdims=True)
        inv = lax.rsqrt(jnp.mean(center * center, axis=-1, keepdims=True) + 1e-05)
        unit = center * inv
        normed = unit * gain
        hidden = normed * jax.nn.sigmoid(normed) * pick(live, s)
        hid[s] = hidden.astype(BF16)
        units[s] = unit
        invs[s] = jnp.broadcast_to(inv, (512, C))
        hid_t[s] = hidden.T.astype(BF16)
        patch(au, s, grid1, 1)
        return carry

    def backward(s, total):
        fix_second(s)
        hgrad = hg_ref[s].reshape(512, C) * pick(live, s)
        unit, inv = units[s], invs[s]
        normed = unit * gain
        sig = jax.nn.sigmoid(normed)
        dn = hgrad * (sig * (1.0 + normed * (1.0 - sig)))
        du = dn * gain
        dc = inv * (du - unit * jnp.mean(du * unit, axis=-1, keepdims=True))
        pg = (dc - jnp.mean(dc, axis=-1, keepdims=True)) * pick(live, s)
        pgr[s] = pg.astype(BF16)
        pgr_t[s] = pg.T.astype(BF16)
        return total + jnp.sum(dn * unit, axis=0, keepdims=True)

    for g in range(6):
        sb[g, pl.ds(18, 2)] = jnp.zeros((2, 8, C), F32)
    lax.fori_loop(0, 2, forward, 0)
    early, late = (0, 1, 2), (3, 4, 5)

    def early_group(g, carry):
        group(g, True, au, hid_t)
        return carry

    def late_group(g, carry):
        group(g, False, ag, pgr_t)
        return carry

    lax.fori_loop(0, 3, early_group, 0)
    gsum = lax.fori_loop(0, 2, backward, jnp.zeros((1, C), F32))
    for g in early:
        scatter(g)
    gains[0, 0] = jnp.broadcast_to(gsum, (8, C))
    gain_copy(0, 0).start()
    lax.fori_loop(3, 6, late_group, 0)
    place(grid2, 0, hid)
    place(grid2, 1, pgr)
    start2()
    for g in late:
        scatter(g)
    gain_step(0)
    for t in range(27):
        r1[t // 9, :, pl.ds(t % 9 * C, C)] = w1[26 - t]
    for g in early:
        reduce_a(g)
    arrive2()
    for g in late:
        reduce_a(g)
    gain_step(1)
    for g in early + late:
        reduce_b(g)
    lax.fori_loop(0, 2, outputs, 0)
    gain_step(2)
    for g in early + late:
        reduce_c(g)
    lax.fori_loop(0, 2, feature_grads, 0)
    for g in early:
        spread(g)
    for g in late:
        spread(g)
    gain_sum = gain_step(3)
    acc = close(early, jnp.zeros((8, C), F32))
    acc = close(late, acc)
    sums[0] = acc
    sums_copy.start()
    for g in early + late:
        sib_copy(g).wait_recv()
    sums_copy.wait_recv()
    acc = acc + sums[1]
    total = jnp.sum(acc) + jnp.sum(gain_sum[0:1] * gain_sum[0:1])
    entries = 54.0 * C * C + C
    mean = jnp.full((8, C), total / entries + 1e-06, F32)
    shrink = jnp.minimum(1.0, CLIP / jnp.sqrt(mean))
    stats_ref[0] = shrink
    stats_ref[1] = shrink * gain_sum

    done1()
    done2()
    for g in range(6):
        core_copy(g).wait_send()
        sib_copy(g).wait_send()
        for sent in (all_a, all_b, all_c, all_eb, all_ea):
            sent(g).wait_send()
    gain_copy(0, 0).wait_send()
    sums_copy.wait_send()
    for k in (1, 2, 3):
        for stage in (1, 2, 3):
            gain_copy(stage, k).wait_send()


def finish_kernel(outv, full_ref, stats_ref, out_hbm, fgrad_hbm, update_hbm, gain_ref, scaled, sem):
    copies = [pltpu.make_async_copy(outv.at[0], out_hbm, sem.at[18]),
              pltpu.make_async_copy(outv.at[1], fgrad_hbm, sem.at[19])]
    for c in copies:
        c.start()
    shrink = stats_ref[0, 0:1, :]
    for g in range(6):
        for k in range(9):
            for h in range(2):
                v = full_ref[g, h, :, pl.ds(k * 2, 2)].astype(F32).reshape(64, C)
                scaled[g, k, pl.ds(h * 64, 64)] = v * shrink
            if k % 3 == 2:
                c = pltpu.make_async_copy(
                    scaled.at[g, pl.ds(k - 2, 3)], update_hbm.at[1 - g // 3, pl.ds(g % 3 * 9 + k - 2, 3)],
                    sem.at[g * 3 + k // 3])
                c.start()
                copies.append(c)
    gain_ref[...] = stats_ref[1, 0:1, :]
    for c in copies:
        c.wait()


def per_device(features, brick_pos, cotangent, first_kernel, second_kernel, norm_gain):
    hbm = pl.BlockSpec(memory_space=pltpu.HBM)
    vmem = pl.BlockSpec(memory_space=pltpu.VMEM)
    dma = pltpu.SemaphoreType.DMA
    V = pltpu.VMEM
    tile = (2, 10, 64, 9 * C)
    outv, full, stats = pl.pallas_call(
        step_kernel,
        out_shape=(V((2, 2, 512, C), BF16), V((6, 2, 4, 20, 8, C), BF16), V((2, 8, C), F32)),
        in_specs=[pl.BlockSpec(memory_space=pltpu.SMEM), vmem, hbm, hbm, hbm, hbm],
        out_specs=(vmem, vmem, vmem),
        scratch_shapes=[
            V((2, 512, C), BF16), V((2, 512, C), BF16),
            V((27, C, C), BF16), V((27, C, C), BF16),
            V((3, C, 9 * C), BF16), V((3, C, 9 * C), BF16), V((3, 3, C, 3 * C), BF16),
            V((2, 18, 18, 8, C), BF16), V((2, 18, 18, 8, C), BF16), V((2, 18, 18, 8, C), BF16),
            V(tile, BF16), V(tile, BF16), V(tile, BF16), V(tile, BF16),
            V((2, 8, 8, 8, C), F32), V((2, 8, 8, 8, C), F32), V((2, C, 512), BF16), V((2, C, 512), BF16),
            V((2, 512, C), BF16), V((2, 512, C), BF16),
            V((54, C, C), F32), V((54, 64, C), F32),
            V((6, 9, 4, 16, C), BF16), V((6, 3, 9, 16, C), BF16),
            V((6, 20, 8, C), F32), V((6, 3, 5, 8, C), F32), V((6, 4, 5, 8, C), F32),
            V((4, 4, 8, C), F32), V((2, 8, C), F32),
            V((2, 512, C), F32), V((2, 512, C), F32),
            dma((4,)), dma((2, 8)), dma((2, 8)), dma((6,)), dma((6,)),
            dma((6,)), dma((6,)), dma((6,)), dma((6,)), dma((6,)), dma((6,)),
            dma((6,)), dma((6,)), dma((6,)), dma((6,)),
            dma((6,)), dma((6,)), dma((1,)), dma((1,)), dma((10,)), dma((10,)),
        ],
        compiler_params=pltpu.CompilerParams(
            collective_id=0, has_side_effects=True, vmem_limit_bytes=56 * 2**20
        ),
        name="step",
    )(brick_pos, norm_gain.reshape(1, C), features, cotangent, first_kernel, second_kernel)
    out, fgrad, update, gain = pl.pallas_call(
        finish_kernel,
        out_shape=(
            jax.ShapeDtypeStruct((2, 512, C), BF16),
            jax.ShapeDtypeStruct((2, 512, C), BF16),
            jax.ShapeDtypeStruct((2, 27, C, C), F32),
            jax.ShapeDtypeStruct((1, C), F32),
        ),
        in_specs=[vmem, vmem, vmem],
        out_specs=(hbm, hbm, hbm, vmem),
        scratch_shapes=[V((6, 9, C, C), F32), dma((20,))],
        compiler_params=pltpu.CompilerParams(vmem_limit_bytes=10 * 2**20),
        name="finish",
    )(outv, full, stats)
    return out, fgrad, update, gain.reshape(C)


def solution(mesh):
    rows = P(("gx", "gy"), None, None)
    return jax.shard_map(
        per_device, mesh=mesh, in_specs=(rows, P(("gx", "gy")), rows, P(), P(), P()),
        out_specs=(rows, rows, P(), P()), check_vma=False,
    )
```
